32 devices in a mesh: seq: 4 (over y, x), vocab: 8 (over z, core).
Axes of the slice: x: 2, y: 2, z: 4, core: 2. Of those that a mesh axis runs over, the one named last changes fastest.
Arguments:
- tokens: int32 [2, 8, 1024], P(None, 'vocab', 'seq'), may hold values from 0 to 4095
- source: int32 [2, 8, 1024], P(None, 'vocab', 'seq'), may hold values from 0 to 4095
- segments: int32 [2, 8, 1024], P(None, 'vocab', 'seq'), may hold values from 0 to 7, never falling along the last dimension, each value on 1 to 512 neighbouring positions
- loss_rows: int32 [2, 8, 128], P(None, 'vocab', 'seq'), may hold values from 0 to 255
- targets: int32 [2, 8, 128], P(None, 'vocab', 'seq'), may hold values from 0 to 4095
- exit_depth: int32 [2, 8, 128], P(None, 'vocab', 'seq'), may hold values from 0 to 1
- qkv_weight: float32 [5, 512, 1536], P(None, 'vocab'), may hold values from -0.25 to 0.25
- out_weight: float32 [5, 512, 512], P(None, 'vocab'), may hold values from -1 to 1
- up_weight: float32 [3, 512, 2048], P(None, 'vocab'), may hold values from -0.25 to 0.25
- down_weight: float32 [3, 2048, 512], P(None, 'vocab'), may hold values from -0.125 to 0.125
- norm_gains: float32 [11, 512], P(None, 'vocab'), may hold values from 0.5 to 1.5
- embed_table: float32 [4096, 512], P('vocab'), may hold values from -0.25 to 0.25
- qkv_first: float32 [5, 512, 1536], P(None, 'vocab'), may hold values from -1.9073486e-06 to 1.9073486e-06
- out_first: float32 [5, 512, 512], P(None, 'vocab'), may hold values from -1.9073486e-06 to 1.9073486e-06
- up_first: float32 [3, 512, 2048], P(None, 'vocab'), may hold values from -1.9073486e-06 to 1.9073486e-06
- down_first: float32 [3, 2048, 512], P(None, 'vocab'), may hold values from -1.9073486e-06 to 1.9073486e-06
- gains_first: float32 [11, 512], P(None, 'vocab'), may hold values from -1.9073486e-06 to 1.9073486e-06
- table_first: float32 [4096, 512], P('vocab'), may hold values from -1.9073486e-06 to 1.9073486e-06
- qkv_second: float32 [5, 512, 1536], P(None, 'vocab'), may hold values from 3.6664634e-15 to 5.8663415e-14
- out_second: float32 [5, 512, 512], P(None, 'vocab'), may hold values from 3.6664634e-15 to 5.8663415e-14
- up_second: float32 [3, 512, 2048], P(None, 'vocab'), may hold values from 3.6664634e-15 to 5.8663415e-14
- down_second: float32 [3, 2048, 512], P(None, 'vocab'), may hold values from 3.6664634e-15 to 5.8663415e-14
- gains_second: float32 [11, 512], P(None, 'vocab'), may hold values from 3.6664634e-15 to 5.8663415e-14
- table_second: float32 [4096, 512], P('vocab'), may hold values from 3.6664634e-15 to 5.8663415e-14
Outputs:
- loss_total: float32 [], replicated
- grad_norm: float32 [], replicated
- new_qkv: float32 [5, 512, 1536], P(None, 'vocab')
- new_out: float32 [5, 512, 512], P(None, 'vocab')
- new_up: float32 [3, 512, 2048], P(None, 'vocab')
- new_down: float32 [3, 2048, 512], P(None, 'vocab')
- gains_grad: float32 [11, 512], P(None, 'vocab')
- new_table: float32 [4096, 512], P('vocab')
- new_qkv_first: float32 [5, 512, 1536], P(None, 'vocab')
- new_out_first: float32 [5, 512, 512], P(None, 'vocab')
- new_up_first: float32 [3, 512, 2048], P(None, 'vocab')
- new_down_first: float32 [3, 2048, 512], P(None, 'vocab')
- new_gains_first: float32 [11, 512], P(None, 'vocab')
- new_table_first: float32 [4096, 512], P('vocab')
- new_qkv_second: float32 [5, 512, 1536], P(None, 'vocab')
- new_out_second: float32 [5, 512, 512], P(None, 'vocab')
- new_up_second: float32 [3, 512, 2048], P(None, 'vocab')
- new_down_second: float32 [3, 2048, 512], P(None, 'vocab')
- new_gains_second: float32 [11, 512], P(None, 'vocab')
- new_table_second: float32 [4096, 512], P('vocab')
The draws below stay inside these ranges and needn't reach their ends.
All inputs are finite; a program needn't handle non-finite values.
Results may differ from the reference program's by a relative error of at most 0.0078.
The reference program's roundings to bfloat16 on the way count: a program that leaves them out, or rounds other values in their place, can miss the bound.
Values may be sent and summed in bfloat16 or wider, within the bound.
No kernel may reach another device: no remote copies, remote signals or barrier semaphores. Data moves between devices by JAX's collectives and lax.ppermute only.
A program may use at most 768 MiB of HBM per device.

```python
import math
import jax
import jax.numpy as jnp
import numpy as np
from jax import lax

D = 512
HEADS = 8
HEAD = 64
FF = 2048
VOCAB = 4096
ENC = 1
LAYERS = 2
MICRO = 2
TOK_DEV = 256
LOSS_DEV = 32
SENTS = 8
LEN = 1024
LONGEST = 512
ROWS = 8
LOSS_LEN = 128
NG = 11
PARAMS = 13637120


def plant(array, rng, smallest, top_value):
    index_at = [jax.random.randint(jax.random.fold_in(rng, axis), (), 0, length) for axis, length in enumerate(array.shape)]
    main_axis = array.shape.index(max(array.shape))
    next_to = index_at[:main_axis] + [(index_at[main_axis] + 1) % array.shape[main_axis]] + index_at[main_axis + 1:]
    return array.at[tuple(index_at)].set(smallest).at[tuple(next_to)].set(top_value)


def level_of(rng, dims, pieces, low, high):
    def one(dim, parts):
        steps = jax.random.uniform(jax.random.fold_in(jax.random.fold_in(rng, 6), dim), (parts,), jnp.float32, low / len(pieces), high / len(pieces))
        return jnp.repeat(jnp.exp(steps), dims[dim] // parts).reshape((-1,) + (1,) * (len(dims) - dim - 1))

    level = one(*pieces[0])
    for cut in pieces[1:]:
        level = level * one(*cut)
    return level


def rank_table(count, lean):
    loads = [(1 << 20) // math.isqrt(rank ** lean) + 1 for rank in range(1, count + 1)]
    spread = 1 + sum(loads) // (1 << 30)
    return np.cumsum(np.array([max(1, weight // spread) for weight in loads]))


def ranked_ids(key, extent, number_of, lean):
    grid = rank_table(number_of, lean)
    lot = jax.random.randint(jax.random.fold_in(key, 1), extent, 0, int(grid[number_of - 1]))
    rank = jnp.searchsorted(jnp.asarray(grid, jnp.int32), lot, side="right")
    return jax.random.permutation(jax.random.fold_in(key, 2), number_of)[rank].astype(jnp.int32)


def profile(amount, total, limit, lean):
    portions = [(1 << 20) // math.isqrt(rank ** lean) + 1 for rank in range(2, amount + 1)]
    rest, given = total - limit - (amount - 1), [1] * (amount - 1)
    while rest > 0:
        candidates = [i for i in range(amount - 1) if given[i] < limit]
        pool, remaining = sum([portions[i] for i in candidates]), rest
        for i in candidates:
            addition = min(limit - given[i], max(1, remaining * portions[i] // pool), rest)
            given[i] = given[i] + addition
            rest = rest - addition
    return np.array([limit] + given)


def ragged_sizes(rng, count, total, most, skew):
    if count == 2:
        one = jax.random.randint(rng, (), max(1, total - most), min(most, total - 1) + 1)
        return jnp.stack([one, total - one])
    sizes = jnp.asarray(profile(count, total, most, skew), jnp.int32)
    couples = (count - 1) // 2
    giver, taker = sizes[1:1 + 2 * couples:2], sizes[2:2 + 2 * couples:2]
    room = jnp.minimum(giver - 1, most - taker)
    shifted = jax.random.randint(jax.random.fold_in(rng, 1), (couples,), 0, 1 << 20) % (room + 1)
    sizes = sizes.at[1:1 + 2 * couples:2].set(giver - shifted).at[2:2 + 2 * couples:2].set(taker + shifted)
    return sizes[jax.random.permutation(jax.random.fold_in(rng, 2), count)]


def centred(key, dims, deviation, most, split=(), held_as=jnp.bfloat16):
    loudness = level_of(key, dims, split, -0.22, 0.18) if split else 1.0
    values = jax.random.normal(key, dims, jnp.float32) * deviation * loudness
    return jnp.minimum(jnp.maximum(values, -most), most).astype(held_as)


def setup_inputs(seed: int = 0) -> dict:
    key_list = jax.random.split(jax.random.key(seed), 25)
    return {
        "tokens": plant(ranked_ids(key_list[0], (MICRO, ROWS, LEN), VOCAB, 2), jax.random.fold_in(key_list[0], 3), 0, VOCAB - 1).astype(jnp.int32),
        "source": plant(ranked_ids(key_list[1], (MICRO, ROWS, LEN), VOCAB, 2), jax.random.fold_in(key_list[1], 3), 0, VOCAB - 1).astype(jnp.int32),
        "segments": jax.vmap(lambda own: jnp.searchsorted(jnp.cumsum(ragged_sizes(own, SENTS, LEN, LONGEST, 2)), jnp.arange(LEN), side="right"))(jax.random.split(key_list[2], MICRO * ROWS)).reshape((MICRO, ROWS, LEN)).astype(jnp.int32),
        "loss_rows": plant(jax.random.randint(key_list[3], (MICRO, ROWS, LOSS_LEN), 0, TOK_DEV), jax.random.fold_in(key_list[3], 1), 0, TOK_DEV - 1).astype(jnp.int32),
        "targets": plant(ranked_ids(key_list[4], (MICRO, ROWS, LOSS_LEN), VOCAB, 2), jax.random.fold_in(key_list[4], 3), 0, VOCAB - 1).astype(jnp.int32),
        "exit_depth": plant(jax.random.randint(key_list[5], (MICRO, ROWS, LOSS_LEN), 0, LAYERS), jax.random.fold_in(key_list[5], 1), 0, LAYERS - 1).astype(jnp.int32),
        "qkv_weight": centred(key_list[6], (ENC + 2 * LAYERS, D, 3 * D), D ** -0.5, 0.25, ((1, 8),), jnp.float32),
        "out_weight": centred(key_list[7], (ENC + 2 * LAYERS, D, D), (D // 16) ** -0.5, 1.0, ((1, 8),), jnp.float32),
        "up_weight": centred(key_list[8], (ENC + LAYERS, D, FF), D ** -0.5, 0.25, ((1, 8),), jnp.float32),
        "down_weight": centred(key_list[9], (ENC + LAYERS, FF, D), FF ** -0.5, 0.125, ((1, 8),), jnp.float32),
        "norm_gains": jnp.clip(1.0 + 0.1 * jax.random.normal(key_list[10], (NG, D), jnp.float32), 0.5, 1.5),
        "embed_table": centred(key_list[11], (VOCAB, D), D ** -0.5, 0.25, ((0, 8),), jnp.float32),
        "qkv_first": centred(key_list[12], (ENC + 2 * LAYERS, D, 3 * D), (0.0011 / PARAMS ** 0.5), 1.9073486328125e-06, ((1, 8),), jnp.float32),
        "out_first": centred(key_list[13], (ENC + 2 * LAYERS, D, D), (0.0011 / PARAMS ** 0.5), 1.9073486328125e-06, ((1, 8),), jnp.float32),
        "up_first": centred(key_list[14], (ENC + LAYERS, D, FF), (0.0011 / PARAMS ** 0.5), 1.9073486328125e-06, ((1, 8),), jnp.float32),
        "down_first": centred(key_list[15], (ENC + LAYERS, FF, D), (0.0011 / PARAMS ** 0.5), 1.9073486328125e-06, ((1, 8),), jnp.float32),
        "gains_first": centred(key_list[16], (NG, D), (0.0011 / PARAMS ** 0.5), 1.9073486328125e-06, ((1, 8),), jnp.float32),
        "table_first": centred(key_list[17], (VOCAB, D), (0.0011 / PARAMS ** 0.5), 1.9073486328125e-06, ((0, 8),), jnp.float32),
        "qkv_second": jnp.clip(jnp.exp(math.log(5.866341483765081e-14) - 2.7725887 * jax.random.uniform(key_list[18], (ENC + 2 * LAYERS, D, 3 * D), jnp.float32) ** level_of(key_list[18], (ENC + 2 * LAYERS, D, 3 * D), ((1, 8),), -0.2, 0.2)), 3.6664634273531754e-15, 5.866341483765081e-14),
        "out_second": jnp.clip(jnp.exp(math.log(5.866341483765081e-14) - 2.7725887 * jax.random.uniform(key_list[19], (ENC + 2 * LAYERS, D, D), jnp.float32) ** level_of(key_list[19], (ENC + 2 * LAYERS, D, D), ((1, 8),), -0.2, 0.2)), 3.6664634273531754e-15, 5.866341483765081e-14),
        "up_second": jnp.clip(jnp.exp(math.log(5.866341483765081e-14) - 2.7725887 * jax.random.uniform(key_list[20], (ENC + LAYERS, D, FF), jnp.float32) ** level_of(key_list[20], (ENC + LAYERS, D, FF), ((1, 8),), -0.2, 0.2)), 3.6664634273531754e-15, 5.866341483765081e-14),
        "down_second": jnp.clip(jnp.exp(math.log(5.866341483765081e-14) - 2.7725887 * jax.random.uniform(key_list[21], (ENC + LAYERS, FF, D), jnp.float32) ** level_of(key_list[21], (ENC + LAYERS, FF, D), ((1, 8),), -0.2, 0.2)), 3.6664634273531754e-15, 5.866341483765081e-14),
        "gains_second": jnp.clip(jnp.exp(math.log(5.866341483765081e-14) - 2.7725887 * jax.random.uniform(key_list[22], (NG, D), jnp.float32) ** level_of(key_list[22], (NG, D), ((1, 8),), -0.2, 0.2)), 3.6664634273531754e-15, 5.866341483765081e-14),
        "table_second": jnp.clip(jnp.exp(math.log(5.866341483765081e-14) - 2.7725887 * jax.random.uniform(key_list[23], (VOCAB, D), jnp.float32) ** level_of(key_list[23], (VOCAB, D), ((0, 8),), -0.2, 0.2)), 3.6664634273531754e-15, 5.866341483765081e-14),
    }


@jax.custom_vjp
def low(v):
    return lax.optimization_barrier(v.astype(jnp.bfloat16)).astype(jnp.float32)

@jax.custom_vjp
def low_back(v):
    return v

def low_keep(v):
    return (low(v), None)

def low_pass(kept, grad):
    return (grad,)

def back_keep(v):
    return (v, None)

def back_low(kept, grad):
    return (low(grad),)
low.defvjp(low_keep, low_pass)
low_back.defvjp(back_keep, back_low)
NORM_EPS = 1e-06
CLIP_NORM = 0.01
LEARN_RATE = 0.05
BETA_ONE = 0.9
BETA_TWO = 0.999
ADAM_EPS = 1e-08
WEIGHT_DECAY = 0.01
ADAM_STEP = 10
LOGIT_SCALE = 4.0
NEGATIVE = -1e+30
PRECISE = lax.Precision.HIGHEST

def matmul(a, b):
    return jnp.dot(a, b, precision=PRECISE, preferred_element_type=jnp.float32)

def normalize(v, g):
    return v * lax.rsqrt(lax.optimization_barrier(jnp.mean(v * v, axis=-1, keepdims=True)) + NORM_EPS) * g

def split_heads(v):
    return v.reshape(v.shape[0], HEADS, HEAD)

def attend(q, k, v, mask):
    s = low_back(jnp.einsum('qhd,khd->hqk', q, k, precision=PRECISE) * HEAD ** (-0.5))
    s = jnp.where(mask[None], s, NEGATIVE)
    p = low(jax.nn.softmax(s, axis=-1))
    return low_back(low(jnp.einsum('hqk,khd->qhd', p, v, precision=PRECISE).reshape(q.shape[0], D)))

def self_block(x, wqkv, wout, gain, mask):
    a = low(normalize(x, gain))
    packed = low_back(low(matmul(a, wqkv)))
    o = attend(split_heads(packed[:, :D]), split_heads(packed[:, D:2 * D]), split_heads(packed[:, 2 * D:]), mask)
    return x + low_back(matmul(o, wout))

def cross_block(x, memory, wqkv, wout, gain, mask):
    c = low(normalize(x, gain))
    queries = low_back(low(matmul(c, wqkv[:, :D])))
    pair = low_back(low(matmul(memory, wqkv[:, D:])))
    o = attend(split_heads(queries), split_heads(pair[:, :D]), split_heads(pair[:, D:]), mask)
    return x + low_back(matmul(o, wout))

def ffn_block(x, wup, wdown, gain):
    f = low(normalize(x, gain))
    h = low_back(matmul(f, wup))
    r = low(jnp.maximum(h, 0.0))
    return x + low_back(matmul(r, wdown))

def row_loss(lowered, src, ids, sentence, places, wanted, reach, counts):
    wqkv, wout, wup, wdown, g, table_low = lowered
    n = ids.shape[0]
    spots = jnp.arange(n)
    same = sentence[:, None] == sentence[None, :]
    allowed = same & (spots[:, None] >= spots[None, :])
    xe = low_back(table_low[src]) * D ** 0.5
    for enc_id in range(ENC):
        xe = self_block(xe, wqkv[enc_id], wout[enc_id], g[2 * enc_id], same)
        xe = ffn_block(xe, wup[enc_id], wdown[enc_id], g[2 * enc_id + 1])
    memory = low(normalize(xe, g[2 * ENC]))
    x = low_back(table_low[ids]) * D ** 0.5
    running = jnp.zeros((), jnp.float32)
    for layer_id in range(LAYERS):
        base = 2 * ENC + 1 + 4 * layer_id
        slot = ENC + 2 * layer_id
        x = self_block(x, wqkv[slot], wout[slot], g[base], allowed)
        x = cross_block(x, memory, wqkv[slot + 1], wout[slot + 1], g[base + 1], same)
        x = ffn_block(x, wup[ENC + layer_id], wdown[ENC + layer_id], g[base + 2])
        e = low(normalize(x[places], g[base + 3]))
        logits = low_back(matmul(e, table_low.T)) * LOGIT_SCALE
        lse = jax.nn.logsumexp(logits, axis=-1)
        picked = jnp.take_along_axis(logits, wanted[:, None], axis=1)[:, 0]
        shares = (reach >= layer_id).astype(jnp.float32) / counts[layer_id]
        running = running + jnp.sum((lse - picked) * shares)
    return running

def adam_update(master, first, second, grad):
    first = BETA_ONE * first + (1.0 - BETA_ONE) * grad
    second = BETA_TWO * second + (1.0 - BETA_TWO) * grad * grad
    fixed_first = first / (1.0 - BETA_ONE ** ADAM_STEP)
    fixed_second = second / (1.0 - BETA_TWO ** ADAM_STEP)
    master = master - LEARN_RATE * (fixed_first / (jnp.sqrt(fixed_second) + ADAM_EPS) + WEIGHT_DECAY * master)
    return (master, first, second)

def reference(tokens, source, segments, loss_rows, targets, exit_depth, qkv_weight, out_weight, up_weight, down_weight, norm_gains, embed_table, qkv_first, out_first, up_first, down_first, gains_first, table_first, qkv_second, out_second, up_second, down_second, gains_second, table_second):
    offsets = (jnp.arange(LOSS_LEN) // LOSS_DEV * TOK_DEV).astype(jnp.int32)
    counts = jnp.stack([jnp.stack([jnp.maximum(jnp.sum((exit_depth[micro] >= layer_id).astype(jnp.float32)), 1.0) for layer_id in range(LAYERS)]) for micro in range(MICRO)])

    def objective(params):
        lowered = tuple((low(p) for p in params))
        running = jnp.zeros((), jnp.float32)
        checked = jax.checkpoint(row_loss)
        for micro in range(MICRO):

            def advance(carry, inputs):
                src, ids, sentence, places, wanted, reach = inputs
                return (carry + checked(lowered, src, ids, sentence, places.astype(jnp.int32) + offsets, wanted, reach, counts[micro]), None)
            running, _ = lax.scan(advance, running, (source[micro], tokens[micro], segments[micro], loss_rows[micro], targets[micro], exit_depth[micro]))
        return running / MICRO
    params = (qkv_weight, out_weight, up_weight, down_weight, norm_gains, embed_table)
    loss_value, pullback = jax.vjp(objective, params)
    gradients, = pullback(jnp.ones_like(loss_value))
    squares = sum((jnp.sum(grad * grad) for grad in gradients))
    grad_norm = jnp.sqrt(squares)
    clip_factor = CLIP_NORM / jnp.maximum(grad_norm, CLIP_NORM)
    firsts = (qkv_first, out_first, up_first, down_first, gains_first, table_first)
    seconds = (qkv_second, out_second, up_second, down_second, gains_second, table_second)
    results = [adam_update(params[i], firsts[i], seconds[i], gradients[i] * clip_factor) for i in range(6)]
    gains_grad = gradients[4] * clip_factor
    return (loss_value, grad_norm, results[0][0], results[1][0], results[2][0], results[3][0], gains_grad, results[5][0], results[0][1], results[1][1], results[2][1], results[3][1], results[4][1], results[5][1], results[0][2], results[1][2], results[2][2], results[3][2], results[4][2], results[5][2])
```

```python
import functools
import math

import jax
import jax.numpy as jnp
from jax import lax
from jax.experimental import pallas as pl
from jax.experimental.pallas import tpu as pltpu
from jax.sharding import Mesh
from jax.sharding import PartitionSpec as P

HEADS = 8
HEAD = 64
ENC = 1
LAYERS = 2
MICRO = 2
COL = 512

NORM_EPS = 1e-06
CLIP_NORM = 0.01
LEARN_RATE = 0.05
BETA_ONE = 0.9
BETA_TWO = 0.999
ADAM_EPS = 1e-08
WEIGHT_DECAY = 0.01
ADAM_STEP = 10
LOGIT_SCALE = 4.0
NEGATIVE = -1e30

PLANE = ("sy", "sx")
LINE = ("z", "c")

BUCKETS = (
    (("table", 0, "blk"), ("qkv", 0, "row"), ("out", 0, "row")),
    (("up", 0, "row"), ("down", 0, "blk"), ("qkv", 1, "row"), ("out", 1, "row")),
    (("qkv", 2, "row"), ("out", 2, "row"), ("up", 1, "row"), ("down", 1, "blk")),
    (
        ("qkv", 3, "row"),
        ("out", 3, "row"),
        ("qkv", 4, "row"),
        ("out", 4, "row"),
        ("up", 2, "row"),
        ("down", 2, "blk"),
    ),
)


def flip(x, axis, bit=1):
    if isinstance(axis, tuple):
        n = math.prod(lax.axis_size(a) for a in axis)
    else:
        n = lax.axis_size(axis)
    return lax.ppermute(x, axis, [(i, i ^ bit) for i in range(n)])


def bits(axis):
    n = lax.axis_size(axis)
    return [1 << k for k in range(n.bit_length() - 1)]


def all_sum(x):
    for axis in ("c", "sx", "sy", "z"):
        for bit in bits(axis):
            x = x + flip(x, axis, bit)
    return x


def doubling(x, axes):
    x = x[None]
    for axis in axes:
        for bit in bits(axis):
            x = jnp.concatenate([x, flip(x, axis, bit)], axis=0)
    return x


def normalize(v, g):
    return v * lax.rsqrt(jnp.mean(v * v, axis=-1, keepdims=True) + NORM_EPS) * g


def norm_back(v, g, cotangent):
    _, pullback = jax.vjp(normalize, v, g)
    return pullback(cotangent)


def product(a, b):
    return jnp.dot(a, b, preferred_element_type=jnp.float32)


def outer_sum(a, b):
    return lax.dot_general(a, b, (((0,), (0,)), ((), ())), preferred_element_type=jnp.float32)


def against_rows(a, b):
    return lax.dot_general(a, b, (((1,), (1,)), ((), ())), preferred_element_type=jnp.float32)


def split_heads(v):
    return v.reshape(v.shape[0], HEADS, HEAD)


def low(v):
    return v.astype(jnp.bfloat16)


def wide(v):
    return v.astype(jnp.float32)


def adam_update(master, first, second, grad):
    first = BETA_ONE * first + (1.0 - BETA_ONE) * grad
    second = BETA_TWO * second + (1.0 - BETA_TWO) * grad * grad
    fixed_first = first / (1.0 - BETA_ONE**ADAM_STEP)
    fixed_second = second / (1.0 - BETA_TWO**ADAM_STEP)
    master = master - LEARN_RATE * (
        fixed_first / (jnp.sqrt(fixed_second) + ADAM_EPS) + WEIGHT_DECAY * master
    )
    return (master, first, second)


def owned_blocks(array, kind, unit):
    if kind == "row":
        rows, columns = array.shape
        return array.reshape(rows, columns // COL, COL).transpose(1, 0, 2)
    rows = array.shape[0]
    per = rows // (4 * unit)
    return array.reshape(4, per, unit, COL).transpose(1, 0, 2, 3).reshape(per, 4 * unit, COL)


def block_counts(entries, shard_shapes, unit):
    counts = []
    for name, _, kind in entries:
        rows, columns = shard_shapes[name]
        counts.append(columns // COL if kind == "row" else rows // (4 * unit))
    return counts


def natural_shape(kind, count, unit, owners):
    if kind == "row":
        return (count, owners * 4 * unit, COL)
    return (owners, 4, count, unit, COL)


def scatter_kernel(plan, unit, half, me_ref, *refs):
    pieces, outs, sem = refs[:12], refs[12:-1], refs[-1]
    c, z, s = me_ref[0], me_ref[1], me_ref[2]

    def put(out, kind, owner, part, rows, source):
        if kind == "row":
            start = pl.multiple_of(owner * (4 * unit) + part * unit, unit)
            target = outs[out].at[:, pl.ds(start, rows), :]
        else:
            target = outs[out].at[owner, part]
        pltpu.make_async_copy(source, target, sem.at[out]).start()

    for c_rel in range(2):
        shard, mine, from_x, from_y, diag_x, diag_y = pieces[6 * c_rel : 6 * c_rel + 6]
        for z_rel in range(4):
            owner = (z ^ z_rel) * 2 + (c ^ c_rel)
            for out, (kind, first, count) in enumerate(plan):
                last = first + count
                if z_rel == 0:
                    if kind == "row":
                        put(out, kind, owner, 0, 4 * unit, shard.at[first:last])
                    else:
                        for part in range(4):
                            rows = pl.ds(part * unit, unit)
                            put(out, kind, owner, part, unit, shard.at[first:last, rows, :])
                    continue
                i = z_rel - 1
                put(out, kind, owner, s, unit, mine.at[i, first:last])
                put(out, kind, owner, s ^ 1, unit, from_x.at[i, first:last])
                put(out, kind, owner, s ^ 2, unit, from_y.at[i, first:last])
                for piece, low_k, high_k in ((diag_x, 0, half), (diag_y, half, 2 * half)):
                    a, b = max(first, low_k), min(last, high_k)
                    if a >= b:
                        continue
                    source = piece.at[i, a - low_k : b - low_k]
                    part = s ^ 3
                    if kind == "row":
                        start = pl.multiple_of(owner * (4 * unit) + part * unit, unit)
                        target = outs[out].at[a - first : b - first, pl.ds(start, unit), :]
                    else:
                        target = outs[out].at[owner, part, a - first : b - first]
                    pltpu.make_async_copy(source, target, sem.at[out]).start()
    for out in range(len(plan)):
        pltpu.make_async_copy(outs[out], outs[out], sem.at[out]).wait()


def collect_kernel(plan, unit, me_ref, *refs):
    grads, keep, send, sem = refs[: len(plan)], refs[len(plan)], refs[len(plan) + 1], refs[-1]
    c, z, s = me_ref[0], me_ref[1], me_ref[2]
    for c_rel, out in ((0, keep), (1, send)):
        for z_rel in range(4):
            owner = (z ^ z_rel) * 2 + (c ^ c_rel)
            for s_rel in range(4):
                part = s ^ s_rel
                for grad, (kind, first, count) in zip(grads, plan):
                    if kind == "row":
                        start = pl.multiple_of(owner * (4 * unit) + part * unit, unit)
                        source = grad.at[:, pl.ds(start, unit), :]
                    else:
                        source = grad.at[owner, part]
                    target = out.at[z_rel, s_rel // 2, s_rel % 2, first : first + count]
                    pltpu.make_async_copy(source, target, sem.at[c_rel]).start()
    for c_rel, out in ((0, keep), (1, send)):
        pltpu.make_async_copy(out, out, sem.at[c_rel]).wait()


ANY = pl.BlockSpec(memory_space=pl.ANY)
SCALAR = pl.BlockSpec(memory_space=pltpu.SMEM)


def gather_bucket(me, shard, kinds, counts, unit, owners):
    total = sum(counts)
    starts = [sum(counts[:i]) for i in range(len(counts))]
    half = total // 2
    s = me[2]
    part = lax.dynamic_slice_in_dim(shard, s * unit, unit, axis=1)
    mine = jnp.stack([flip(part, "z", bit) for bit in (1, 2, 3)])
    from_x = flip(mine, "sx")
    from_y = flip(mine, "sy")
    diag_x = flip(from_x[:, :half], "sy")
    diag_y = flip(from_y[:, half:], "sx")
    held = (shard, mine, from_x, from_y, diag_x, diag_y)
    other = tuple(flip(piece, "c") for piece in held)
    plan = tuple(zip(kinds, starts, counts))
    return pl.pallas_call(
        functools.partial(scatter_kernel, plan, unit, half),
        out_shape=[
            jax.ShapeDtypeStruct(natural_shape(kind, count, unit, owners), jnp.bfloat16)
            for kind, count in zip(kinds, counts)
        ],
        in_specs=[SCALAR] + [ANY] * 12,
        out_specs=[ANY] * len(plan),
        scratch_shapes=[pltpu.SemaphoreType.DMA((len(plan),))],
        name="place_weights",
    )(me, *held, *other)


def reduce_bucket(me, grads, kinds, counts, unit):
    total = sum(counts)
    starts = [sum(counts[:i]) for i in range(len(counts))]
    half = total // 2
    plan = tuple(zip(kinds, starts, counts))
    shape = jax.ShapeDtypeStruct((4, 2, 2, total, unit, COL), jnp.bfloat16)
    keep, send = pl.pallas_call(
        functools.partial(collect_kernel, plan, unit),
        out_shape=[shape, shape],
        in_specs=[SCALAR] + [ANY] * len(plan),
        out_specs=[ANY, ANY],
        scratch_shapes=[pltpu.SemaphoreType.DMA((2,))],
        name="collect_gradients",
    )(me, *grads)
    chip = wide(keep) + wide(flip(send, "c"))
    got_a = flip(low(chip[:, :, 1, :half]), "sx")
    got_b = flip(low(chip[:, 1, :, half:]), "sy")
    pair_a = chip[:, :, 0, :half] + wide(got_a)
    pair_b = chip[:, 0, :, half:] + wide(got_b)
    got_a = flip(low(pair_a[:, 1]), "sy")
    got_b = flip(low(pair_b[:, 1]), "sx")
    plane_a = pair_a[:, 0] + wide(got_a)
    plane_b = pair_b[:, 0] + wide(got_b)
    plane = jnp.concatenate([plane_a, plane_b], axis=1)
    whole = plane[0]
    for bit in (1, 2, 3):
        whole = whole + wide(flip(low(plane[bit]), "z", bit))
    return whole


def share_rows(me, whole):
    own = low(whole)
    parts = jnp.stack([own, flip(own, "sx"), flip(own, "sy"), flip(own, PLANE, 3)])
    order = jnp.arange(4) ^ me[2]
    return jnp.concatenate(
        [lax.dynamic_index_in_dim(parts, order[i], 0, keepdims=True) for i in range(4)], axis=0
    )


def owned_natural(parts, kind):
    if kind == "row":
        four, count, unit, _ = parts.shape
        return parts.transpose(0, 2, 1, 3).reshape(four * unit, count * COL)
    return parts.reshape(-1, COL)


def exchange(pair):
    return flip(pair, "c")


def score_block(queries, keys, allowed):
    scores = jnp.einsum(
        "qhd,khd->hqk", queries, keys, preferred_element_type=jnp.float32
    ) * HEAD ** (-0.5)
    return jnp.where(allowed[None], scores, NEGATIVE)


def attend_forward(queries, keys_local, values_local, mask):
    n = queries.shape[0]
    other = exchange(jnp.stack([keys_local, values_local]))
    keys_all = jnp.concatenate([keys_local, other[0]])
    values_all = jnp.concatenate([values_local, other[1]])
    scores = score_block(split_heads(queries), split_heads(keys_all), mask)
    top = jnp.max(scores, axis=-1, keepdims=True)
    expo = jnp.exp(scores - top)
    denom = jnp.sum(expo, axis=-1, keepdims=True)
    probs = (expo / denom).astype(jnp.bfloat16)
    lse = top + jnp.log(denom)
    attended = (
        jnp.einsum(
            "hqk,khd->qhd", probs, split_heads(values_all), preferred_element_type=jnp.float32
        )
        .reshape(n, -1)
        .astype(jnp.bfloat16)
    )
    return (attended, (queries, keys_all, values_all, lse, attended))


def attend_backward(saved, mask, grad_att):
    queries, keys_all, values_all, lse, _ = saved
    n, width = queries.shape
    queries = split_heads(queries)
    keys = split_heads(keys_all)
    values = split_heads(values_all)
    probs = jnp.exp(score_block(queries, keys, mask) - lse)
    probs_low = probs.astype(jnp.bfloat16)
    grad_att = split_heads(grad_att)
    grad_values = jnp.einsum(
        "hqk,qhd->khd", probs_low, grad_att, preferred_element_type=jnp.float32
    )
    grad_probs = jnp.einsum("qhd,khd->hqk", grad_att, values, preferred_element_type=jnp.float32)
    grad_scores = (
        probs * (grad_probs - jnp.sum(probs * grad_probs, axis=-1, keepdims=True))
    ).astype(jnp.bfloat16)
    grad_queries = jnp.einsum(
        "hqk,khd->qhd", grad_scores, keys, preferred_element_type=jnp.float32
    ) * HEAD ** (-0.5)
    grad_keys = jnp.einsum(
        "hqk,qhd->khd", grad_scores, queries, preferred_element_type=jnp.float32
    ) * HEAD ** (-0.5)
    both = jnp.stack([grad_keys.reshape(-1, width), grad_values.reshape(-1, width)])
    both = both[:, :n] + exchange(both[:, n:])
    return (low(grad_queries.reshape(n, width)), low(both[0]), low(both[1]))


def self_forward(x, wqkv, wout, gain, mask):
    normed = low(normalize(x, gain))
    q, k, v = (low(product(normed, wqkv[i])) for i in range(3))
    attended, saved = attend_forward(q, k, v, mask)
    return (x + product(attended, wout[0]), (x, normed, saved))


def self_backward(kept, wqkv, wout, gain, mask, grad_out):
    x, normed, saved = kept
    grad_low = low(grad_out)
    grad_wout = low(outer_sum(saved[4], grad_low))[None]
    parts = attend_backward(saved, mask, low(against_rows(grad_low, wout[0])))
    grad_wqkv = jnp.stack([low(outer_sum(normed, part)) for part in parts])
    back = sum(against_rows(part, wqkv[i]) for i, part in enumerate(parts))
    grad_in, grad_gain = norm_back(x, gain, back)
    return (grad_out + grad_in, grad_wqkv, grad_wout, grad_gain)


def cross_forward(x, memory, wqkv, wout, gain, mask):
    normed = low(normalize(x, gain))
    q = low(product(normed, wqkv[0]))
    k, v = (low(product(memory, wqkv[i])) for i in (1, 2))
    attended, saved = attend_forward(q, k, v, mask)
    return (x + product(attended, wout[0]), (x, normed, saved))


def cross_backward(kept, memory, wqkv, wout, gain, mask, grad_out):
    x, normed, saved = kept
    grad_low = low(grad_out)
    grad_wout = low(outer_sum(saved[4], grad_low))[None]
    grad_q, grad_k, grad_v = attend_backward(saved, mask, low(against_rows(grad_low, wout[0])))
    grad_wqkv = jnp.stack(
        [
            low(outer_sum(normed, grad_q)),
            low(outer_sum(memory, grad_k)),
            low(outer_sum(memory, grad_v)),
        ]
    )
    grad_memory = against_rows(grad_k, wqkv[1]) + against_rows(grad_v, wqkv[2])
    grad_in, grad_gain = norm_back(x, gain, against_rows(grad_q, wqkv[0]))
    return (grad_out + grad_in, grad_memory, grad_wqkv, grad_wout, grad_gain)


def ffn_forward(x, wup, wdown, gain):
    normed = low(normalize(x, gain))
    hidden = [low(jnp.maximum(product(normed, wup[i]), 0.0)) for i in range(wup.shape[0])]
    y = x + sum(product(r, wdown[i]) for i, r in enumerate(hidden))
    return (y, (x, normed, hidden))


def ffn_backward(kept, wup, wdown, gain, grad_out):
    x, normed, hidden = kept
    grad_low = low(grad_out)
    grad_down = jnp.stack([low(outer_sum(r, grad_low)) for r in hidden])
    grad_hidden = [
        low(jnp.where(r > 0.0, against_rows(grad_low, wdown[i]), 0.0))
        for i, r in enumerate(hidden)
    ]
    grad_up = jnp.stack([low(outer_sum(normed, g)) for g in grad_hidden])
    back = sum(against_rows(g, wup[i]) for i, g in enumerate(grad_hidden))
    grad_in, grad_gain = norm_back(x, gain, back)
    return (grad_out + grad_in, grad_up, grad_down, grad_gain)


def shards(
    tokens,
    source,
    segments,
    loss_rows,
    targets,
    exit_depth,
    qkv_weight,
    out_weight,
    up_weight,
    down_weight,
    norm_gains,
    embed_table,
    qkv_first,
    out_first,
    up_first,
    down_first,
    gains_first,
    table_first,
    qkv_second,
    out_second,
    up_second,
    down_second,
    gains_second,
    table_second,
):
    sy, sx = lax.axis_index("sy"), lax.axis_index("sx")
    z, c = lax.axis_index("z"), lax.axis_index("c")
    s = sy * 2 + sx
    me = jnp.stack([c, z, s]).astype(jnp.int32)
    owners = lax.axis_size("z") * 2
    tok_dev = tokens.shape[2]
    loss_dev = targets.shape[2]
    voc_dev, width = embed_table.shape
    gain_count, gain_dev = norm_gains.shape
    vocabulary = voc_dev * owners
    root_width = math.sqrt(width)
    half_row = 2 * tok_dev
    unit = qkv_weight.shape[1] // 4
    fast = lax.axis_size("z") == 4 and unit % 16 == 0

    shard_of = {
        "table": embed_table[None],
        "qkv": qkv_weight,
        "out": out_weight,
        "up": up_weight,
        "down": down_weight,
    }
    shard_shapes = {name: array.shape[1:] for name, array in shard_of.items()}
    weights = {}
    for entries in BUCKETS:
        kinds = [kind for _, _, kind in entries]
        counts = block_counts(entries, shard_shapes, unit)
        shard = jnp.concatenate(
            [owned_blocks(low(shard_of[name][i]), kind, unit) for name, i, kind in entries]
        )
        if fast:
            outs = gather_bucket(me, shard, kinds, counts, unit, owners)
        else:
            everything = lax.all_gather(shard, LINE)
            outs = []
            first = 0
            for kind, count in zip(kinds, counts):
                piece = everything[:, first : first + count]
                first += count
                if kind == "row":
                    outs.append(piece.transpose(1, 0, 2, 3).reshape(count, -1, COL))
                else:
                    outs.append(
                        piece.reshape(owners, count, 4, unit, COL).transpose(0, 2, 1, 3, 4)
                    )
        for (name, i, kind), out in zip(entries, outs):
            weights[name, i] = out.reshape(-1, COL, COL) if kind == "blk" else out
    table = weights["table", 0].reshape(vocabulary, width)

    numbers = jnp.concatenate(
        [array[:, 0] for array in (tokens, source, segments, loss_rows, targets, exit_depth)],
        axis=1,
    )
    plane = doubling(numbers, ("c", "sx", "sy")).reshape(2, 2, 2, MICRO, -1)
    depths_seen = plane[..., 3 * tok_dev + 2 * loss_dev :]
    reached = jnp.stack(
        [
            jnp.sum((depths_seen >= layer_id).astype(jnp.float32), axis=(0, 1, 2, 4))
            for layer_id in range(LAYERS)
        ],
        axis=1,
    )
    small = jnp.concatenate([norm_gains.reshape(-1), reached.reshape(-1)])
    small = doubling(small, ("c", "z"))
    reach = jnp.maximum(
        jnp.sum(small[::2, gain_count * gain_dev :], axis=0).reshape(MICRO, LAYERS), 1.0
    )
    reach = lax.dynamic_index_in_dim(reach, sy, 0, False)
    gains_seen = small[:, : gain_count * gain_dev].reshape(owners, gain_count, gain_dev)
    order = jnp.arange(owners)
    rel = ((order // 2) ^ z) * 2 + ((order % 2) ^ c)
    gains_full = gains_seen[rel].transpose(1, 0, 2).reshape(gain_count, width)
    gains_full = wide(low(gains_full))

    row = lax.dynamic_index_in_dim(plane, sx ^ c, 2, False)
    row = lax.dynamic_index_in_dim(row, sy, 2, False).reshape(4, -1)
    row = row[jnp.arange(4) ^ s]
    mine = lax.dynamic_slice_in_dim(row, 2 * c, 2, 0)
    theirs = lax.dynamic_slice_in_dim(row, 2 * (1 - c), 2, 0)
    target_ids = mine[:, :tok_dev].reshape(-1)
    source_ids = mine[:, tok_dev : 2 * tok_dev].reshape(-1)
    sentence = mine[:, 2 * tok_dev : 3 * tok_dev].reshape(-1)
    other_sentence = theirs[:, 2 * tok_dev : 3 * tok_dev].reshape(-1)
    rest = 3 * tok_dev
    places = (
        mine[:, rest : rest + loss_dev] + (jnp.arange(2, dtype=jnp.int32) * tok_dev)[:, None]
    ).reshape(-1)
    wanted = mine[:, rest + loss_dev : rest + 2 * loss_dev].reshape(-1)
    depth = mine[:, rest + 2 * loss_dev :].reshape(-1)
    key_sentence = jnp.concatenate([sentence, other_sentence])
    spots = c * half_row + jnp.arange(half_row)
    key_spots = jnp.concatenate([spots, (1 - c) * half_row + jnp.arange(half_row)])
    same = sentence[:, None] == key_sentence[None, :]
    allowed = same & (spots[:, None] >= key_spots[None, :])

    looked_up = table[jnp.concatenate([source_ids, target_ids])].astype(jnp.float32) * root_width
    xe = looked_up[:half_row]
    x = looked_up[half_row:]
    xe, kept_enc_self = self_forward(
        xe, weights["qkv", 0], weights["out", 0], gains_full[0], same
    )
    xe, kept_enc_ffn = ffn_forward(xe, weights["up", 0], weights["down", 0], gains_full[1])
    final_gain = gains_full[2 * ENC]
    memory = low(normalize(xe, final_gain))
    kept = []
    states = []
    for layer_id in range(LAYERS):
        base = 2 * ENC + 1 + 4 * layer_id
        slot = ENC + 2 * layer_id
        x, kept_self = self_forward(
            x, weights["qkv", slot], weights["out", slot], gains_full[base], allowed
        )
        x, kept_cross = cross_forward(
            x,
            memory,
            weights["qkv", slot + 1],
            weights["out", slot + 1],
            gains_full[base + 1],
            same,
        )
        x, kept_ffn = ffn_forward(
            x, weights["up", ENC + layer_id], weights["down", ENC + layer_id], gains_full[base + 2]
        )
        kept.append((kept_self, kept_cross, kept_ffn))
        states.append(x)

    pick = (places[:, None] == jnp.arange(half_row)[None, :]).astype(jnp.bfloat16)
    exit_gains = [gains_full[2 * ENC + 4 + 4 * layer_id] for layer_id in range(LAYERS)]
    exits = jnp.concatenate(
        [low(product(pick, low(normalize(states[i], exit_gains[i])))) for i in range(LAYERS)]
    )
    logits = against_rows(exits, table) * LOGIT_SCALE
    wanted_all = jnp.concatenate([wanted] * LAYERS)
    hit = jnp.arange(vocabulary)[None, :] == wanted_all[:, None]
    picked = jnp.sum(jnp.where(hit, logits, 0.0), axis=-1)
    top = jnp.max(logits, axis=-1)
    lse = top + jnp.log(jnp.sum(jnp.exp(logits - top[:, None]), axis=-1))
    shares = jnp.concatenate(
        [(depth >= i).astype(jnp.float32) / reach[i] / MICRO for i in range(LAYERS)]
    )
    loss_part = jnp.sum((lse - picked) * shares)
    grad_logits = low(
        (jnp.exp(logits - lse[:, None]) - hit.astype(jnp.float32))
        * shares[:, None]
        * LOGIT_SCALE
    )
    grad_exits = product(grad_logits, table)
    table_grad = outer_sum(grad_logits, exits)

    grads = {}
    gain_parts = [None] * gain_count
    grad_x = None
    grad_memory = None
    for layer_id in reversed(range(LAYERS)):
        slot = ENC + 2 * layer_id
        base = 2 * ENC + 1 + 4 * layer_id
        count = places.shape[0]
        grad_rows = lax.dot_general(
            wide(pick),
            grad_exits[layer_id * count : (layer_id + 1) * count],
            (((0,), (0,)), ((), ())),
            precision=lax.Precision.HIGHEST,
            preferred_element_type=jnp.float32,
        )
        grad_here, gain_parts[base + 3] = norm_back(
            states[layer_id], exit_gains[layer_id], grad_rows
        )
        grad_x = grad_here if grad_x is None else grad_x + grad_here
        kept_self, kept_cross, kept_ffn = kept[layer_id]
        up, down = ("up", ENC + layer_id), ("down", ENC + layer_id)
        grad_x, grads[up], grads[down], gain_parts[base + 2] = ffn_backward(
            kept_ffn, weights[up], weights[down], gains_full[base + 2], grad_x
        )
        qkv, out = ("qkv", slot + 1), ("out", slot + 1)
        grad_x, more, grads[qkv], grads[out], gain_parts[base + 1] = cross_backward(
            kept_cross, memory, weights[qkv], weights[out], gains_full[base + 1], same, grad_x
        )
        grad_memory = more if grad_memory is None else grad_memory + more
        qkv, out = ("qkv", slot), ("out", slot)
        grad_x, grads[qkv], grads[out], gain_parts[base] = self_backward(
            kept_self, weights[qkv], weights[out], gains_full[base], allowed, grad_x
        )
    grad_enc, gain_parts[2 * ENC] = norm_back(xe, final_gain, grad_memory)
    up, down, qkv, out = ("up", 0), ("down", 0), ("qkv", 0), ("out", 0)
    grad_enc, grads[up], grads[down], gain_parts[1] = ffn_backward(
        kept_enc_ffn, weights[up], weights[down], gains_full[1], grad_enc
    )
    grad_enc, grads[qkv], grads[out], gain_parts[0] = self_backward(
        kept_enc_self, weights[qkv], weights[out], gains_full[0], same, grad_enc
    )
    token_ids = jnp.concatenate([source_ids, target_ids])
    token_grads = low(jnp.concatenate([grad_enc, grad_x]) * root_width)
    looked = (token_ids[:, None] == jnp.arange(vocabulary)[None, :]).astype(jnp.bfloat16)
    table_grad = low(table_grad + outer_sum(looked, token_grads))
    grads["table", 0] = table_grad

    shape_of = {}
    reduced = {}
    squares = jnp.zeros((), jnp.float32)
    for entries in reversed(BUCKETS):
        kinds = [kind for _, _, kind in entries]
        counts = block_counts(entries, shard_shapes, unit)
        own = [
            grads[name, i].reshape(natural_shape(kind, count, unit, owners))
            for (name, i, kind), count in zip(entries, counts)
        ]
        if fast:
            whole = reduce_bucket(me, own, kinds, counts, unit)
            squares = squares + jnp.sum(whole * whole)
            parts = share_rows(me, whole)
        else:
            parts = []
            for array, kind in zip(own, kinds):
                if kind == "row":
                    array = array.reshape(array.shape[0], owners, 4, unit, COL)
                    array = array.transpose(1, 2, 0, 3, 4)
                parts.append(array)
            total = jnp.concatenate([wide(part) for part in parts], axis=2)
            total = lax.psum_scatter(total, LINE, scatter_dimension=0, tiled=True)
            parts = lax.psum(total, PLANE)[0]
            squares = squares + jnp.sum(parts * parts) / 4.0
        first = 0
        for (name, i, kind), count in zip(entries, counts):
            reduced[name, i] = owned_natural(parts[:, first : first + count], kind)
            first += count
    gain_grad = jnp.stack(gain_parts)
    small = all_sum(jnp.concatenate([gain_grad.reshape(-1), loss_part[None]]))
    loss_total = small[-1]
    gain_grad = small[:-1].reshape(gain_count, width)
    squares = all_sum(squares) + jnp.sum(gain_grad * gain_grad)
    grad_norm = jnp.sqrt(squares)
    clip_factor = CLIP_NORM / jnp.maximum(grad_norm, CLIP_NORM)

    def stacked(name, n):
        return wide(jnp.stack([reduced[name, i] for i in range(n)]))

    gradients = (
        stacked("qkv", ENC + 2 * LAYERS),
        stacked("out", ENC + 2 * LAYERS),
        stacked("up", ENC + LAYERS),
        stacked("down", ENC + LAYERS),
        lax.dynamic_slice_in_dim(gain_grad, (2 * z + c) * gain_dev, gain_dev, 1),
        wide(reduced["table", 0]),
    )
    masters = (qkv_weight, out_weight, up_weight, down_weight, norm_gains, embed_table)
    firsts = (qkv_first, out_first, up_first, down_first, gains_first, table_first)
    seconds = (qkv_second, out_second, up_second, down_second, gains_second, table_second)
    results = [
        adam_update(masters[i], firsts[i], seconds[i], gradients[i] * clip_factor) for i in range(6)
    ]
    gains_grad = gradients[4] * clip_factor
    return (
        loss_total,
        grad_norm,
        results[0][0],
        results[1][0],
        results[2][0],
        results[3][0],
        gains_grad,
        results[5][0],
        results[0][1],
        results[1][1],
        results[2][1],
        results[3][1],
        results[4][1],
        results[5][1],
        results[0][2],
        results[1][2],
        results[2][2],
        results[3][2],
        results[4][2],
        results[5][2],
    )


def solution(mesh):
    seq, vocab = mesh.devices.shape
    fine = Mesh(mesh.devices.reshape(2, seq // 2, vocab // 2, 2), ("sy", "sx", "z", "c"))
    ints = P(None, LINE, PLANE)
    block = P(None, LINE, None)
    gains = P(None, LINE)
    rows = P(LINE, None)
    arrays = (block, block, block, block, gains, rows)
    return jax.shard_map(
        shards,
        mesh=fine,
        in_specs=(ints,) * 6 + arrays * 3,
        out_specs=(P(), P(), block, block, block, block, gains, rows) + arrays * 2,
        check_vma=False,
    )
```

```python
import functools
import math

import jax
import jax.numpy as jnp
from jax import lax
from jax.experimental import pallas as pl
from jax.experimental.pallas import tpu as pltpu
from jax.sharding import Mesh
from jax.sharding import PartitionSpec as P

HEADS = 8
HEAD = 64
ENC = 1
LAYERS = 2
MICRO = 2
COL = 512

NORM_EPS = 1e-06
CLIP_NORM = 0.01
LEARN_RATE = 0.05
BETA_ONE = 0.9
BETA_TWO = 0.999
ADAM_EPS = 1e-08
WEIGHT_DECAY = 0.01
ADAM_STEP = 10
LOGIT_SCALE = 4.0
NEGATIVE = -1e30

PLANE = ("sy", "sx")
LINE = ("z", "c")

BUCKETS = (
    (("table", 0, "blk"), ("qkv", 0, "row"), ("out", 0, "row")),
    (("up", 0, "row"), ("down", 0, "blk"), ("qkv", 1, "row"), ("out", 1, "row")),
    (("qkv", 2, "row"), ("out", 2, "row"), ("up", 1, "row"), ("down", 1, "blk")),
    (
        ("qkv", 3, "row"),
        ("out", 3, "row"),
        ("qkv", 4, "row"),
        ("out", 4, "row"),
        ("up", 2, "row"),
        ("down", 2, "blk"),
    ),
)


def flip(x, axis, bit=1):
    if isinstance(axis, tuple):
        n = math.prod(lax.axis_size(a) for a in axis)
    else:
        n = lax.axis_size(axis)
    return lax.ppermute(x, axis, [(i, i ^ bit) for i in range(n)])


def bits(axis):
    n = lax.axis_size(axis)
    return [1 << k for k in range(n.bit_length() - 1)]


def all_sum(x):
    for axis in ("c", "sx", "sy", "z"):
        for bit in bits(axis):
            x = x + flip(x, axis, bit)
    return x


def doubling(x, axes):
    x = x[None]
    for axis in axes:
        for bit in bits(axis):
            x = jnp.concatenate([x, flip(x, axis, bit)], axis=0)
    return x


def normalize(v, g):
    return v * lax.rsqrt(jnp.mean(v * v, axis=-1, keepdims=True) + NORM_EPS) * g


def norm_back(v, g, cotangent):
    _, pullback = jax.vjp(normalize, v, g)
    return pullback(cotangent)


def product(a, b):
    return jnp.dot(a, b, preferred_element_type=jnp.float32)


def outer_sum(a, b):
    return lax.dot_general(a, b, (((0,), (0,)), ((), ())), preferred_element_type=jnp.float32)


def against_rows(a, b):
    return lax.dot_general(a, b, (((1,), (1,)), ((), ())), preferred_element_type=jnp.float32)


def split_heads(v):
    return v.reshape(v.shape[0], HEADS, HEAD)


def low(v):
    return v.astype(jnp.bfloat16)


def wide(v):
    return v.astype(jnp.float32)


def adam_update(master, first, second, grad):
    first = BETA_ONE * first + (1.0 - BETA_ONE) * grad
    second = BETA_TWO * second + (1.0 - BETA_TWO) * grad * grad
    fixed_first = first / (1.0 - BETA_ONE**ADAM_STEP)
    fixed_second = second / (1.0 - BETA_TWO**ADAM_STEP)
    master = master - LEARN_RATE * (
        fixed_first / (jnp.sqrt(fixed_second) + ADAM_EPS) + WEIGHT_DECAY * master
    )
    return (master, first, second)


def owned_blocks(array, kind, unit):
    if kind == "row":
        rows, columns = array.shape
        return array.reshape(rows, columns // COL, COL).transpose(1, 0, 2)
    rows = array.shape[0]
    per = rows // (4 * unit)
    return array.reshape(4, per, unit, COL).transpose(1, 0, 2, 3).reshape(per, 4 * unit, COL)


def block_counts(entries, shard_shapes, unit):
    counts = []
    for name, _, kind in entries:
        rows, columns = shard_shapes[name]
        counts.append(columns // COL if kind == "row" else rows // (4 * unit))
    return counts


def natural_shape(kind, count, unit, owners):
    if kind == "row":
        return (count, owners * 4 * unit, COL)
    return (owners, 4, count, unit, COL)


def scatter_kernel(plan, unit, half, me_ref, *refs):
    pieces, outs, sem = refs[:12], refs[12:-1], refs[-1]
    c, z, s = me_ref[0], me_ref[1], me_ref[2]

    def put(out, kind, owner, part, rows, source):
        if kind == "row":
            start = pl.multiple_of(owner * (4 * unit) + part * unit, unit)
            target = outs[out].at[:, pl.ds(start, rows), :]
        else:
            target = outs[out].at[owner, part]
        pltpu.make_async_copy(source, target, sem.at[out]).start()

    for c_rel in range(2):
        shard, mine, from_x, from_y, diag_x, diag_y = pieces[6 * c_rel : 6 * c_rel + 6]
        for z_rel in range(4):
            owner = (z ^ z_rel) * 2 + (c ^ c_rel)
            for out, (kind, first, count) in enumerate(plan):
                last = first + count
                if z_rel == 0:
                    if kind == "row":
                        put(out, kind, owner, 0, 4 * unit, shard.at[first:last])
                    else:
                        for part in range(4):
                            rows = pl.ds(part * unit, unit)
                            put(out, kind, owner, part, unit, shard.at[first:last, rows, :])
                    continue
                i = z_rel - 1
                put(out, kind, owner, s, unit, mine.at[i, first:last])
                put(out, kind, owner, s ^ 1, unit, from_x.at[i, first:last])
                put(out, kind, owner, s ^ 2, unit, from_y.at[i, first:last])
                for piece, low_k, high_k in ((diag_x, 0, half), (diag_y, half, 2 * half)):
                    a, b = max(first, low_k), min(last, high_k)
                    if a >= b:
                        continue
                    source = piece.at[i, a - low_k : b - low_k]
                    part = s ^ 3
                    if kind == "row":
                        start = pl.multiple_of(owner * (4 * unit) + part * unit, unit)
                        target = outs[out].at[a - first : b - first, pl.ds(start, unit), :]
                    else:
                        target = outs[out].at[owner, part, a - first : b - first]
                    pltpu.make_async_copy(source, target, sem.at[out]).start()
    for out in range(len(plan)):
        pltpu.make_async_copy(outs[out], outs[out], sem.at[out]).wait()


def collect_kernel(plan, unit, me_ref, *refs):
    grads, keep, send, sem = refs[: len(plan)], refs[len(plan)], refs[len(plan) + 1], refs[-1]
    c, z, s = me_ref[0], me_ref[1], me_ref[2]
    for c_rel, out in ((0, keep), (1, send)):
        for z_rel in range(4):
            owner = (z ^ z_rel) * 2 + (c ^ c_rel)
            for s_rel in range(4):
                part = s ^ s_rel
                for grad, (kind, first, count) in zip(grads, plan):
                    if kind == "row":
                        start = pl.multiple_of(owner * (4 * unit) + part * unit, unit)
                        source = grad.at[:, pl.ds(start, unit), :]
                    else:
                        source = grad.at[owner, part]
                    target = out.at[z_rel, s_rel // 2, s_rel % 2, first : first + count]
                    pltpu.make_async_copy(source, target, sem.at[c_rel]).start()
    for c_rel, out in ((0, keep), (1, send)):
        pltpu.make_async_copy(out, out, sem.at[c_rel]).wait()


ANY = pl.BlockSpec(memory_space=pl.ANY)
ONCHIP = pl.BlockSpec(memory_space=pltpu.VMEM)
SCALAR = pl.BlockSpec(memory_space=pltpu.SMEM)


def gather_bucket(me, shard, kinds, counts, unit, owners):
    total = sum(counts)
    starts = [sum(counts[:i]) for i in range(len(counts))]
    half = total // 2
    s = me[2]
    part = lax.dynamic_slice_in_dim(shard, s * unit, unit, axis=1)
    mine = jnp.stack([flip(part, "z", bit) for bit in (1, 2, 3)])
    from_x = flip(mine, "sx")
    from_y = flip(mine, "sy")
    diag_x = flip(from_x[:, :half], "sy")
    diag_y = flip(from_y[:, half:], "sx")
    held = (shard, mine, from_x, from_y, diag_x, diag_y)
    other = tuple(flip(piece, "c") for piece in held)
    plan = tuple(zip(kinds, starts, counts))
    return pl.pallas_call(
        functools.partial(scatter_kernel, plan, unit, half),
        out_shape=[
            jax.ShapeDtypeStruct(natural_shape(kind, count, unit, owners), jnp.bfloat16)
            for kind, count in zip(kinds, counts)
        ],
        in_specs=[SCALAR] + [ANY] * 12,
        out_specs=[ONCHIP] * len(plan),
        scratch_shapes=[pltpu.SemaphoreType.DMA((len(plan),))],
        name="place_weights",
    )(me, *held, *other)


def reduce_bucket(me, grads, kinds, counts, unit):
    total = sum(counts)
    starts = [sum(counts[:i]) for i in range(len(counts))]
    half = total // 2
    plan = tuple(zip(kinds, starts, counts))
    shape = jax.ShapeDtypeStruct((4, 2, 2, total, unit, COL), jnp.bfloat16)
    keep, send = pl.pallas_call(
        functools.partial(collect_kernel, plan, unit),
        out_shape=[shape, shape],
        in_specs=[SCALAR] + [ANY] * len(plan),
        out_specs=[ONCHIP, ONCHIP],
        scratch_shapes=[pltpu.SemaphoreType.DMA((2,))],
        name="collect_gradients",
    )(me, *grads)
    chip = wide(keep) + wide(flip(send, "c"))
    got_a = flip(low(chip[:, :, 1, :half]), "sx")
    got_b = flip(low(chip[:, 1, :, half:]), "sy")
    pair_a = chip[:, :, 0, :half] + wide(got_a)
    pair_b = chip[:, 0, :, half:] + wide(got_b)
    got_a = flip(low(pair_a[:, 1]), "sy")
    got_b = flip(low(pair_b[:, 1]), "sx")
    plane_a = pair_a[:, 0] + wide(got_a)
    plane_b = pair_b[:, 0] + wide(got_b)
    plane = jnp.concatenate([plane_a, plane_b], axis=1)
    whole = plane[0]
    for bit in (1, 2, 3):
        whole = whole + wide(flip(low(plane[bit]), "z", bit))
    return whole


def share_rows(me, whole):
    own = low(whole)
    parts = jnp.stack([own, flip(own, "sx"), flip(own, "sy"), flip(own, PLANE, 3)])
    order = jnp.arange(4) ^ me[2]
    return jnp.concatenate(
        [lax.dynamic_index_in_dim(parts, order[i], 0, keepdims=True) for i in range(4)], axis=0
    )


def owned_natural(parts, kind):
    if kind == "row":
        four, count, unit, _ = parts.shape
        return parts.transpose(0, 2, 1, 3).reshape(four * unit, count * COL)
    return parts.reshape(-1, COL)


BQ = 128
NT = (((1,), (1,)), ((), ()))
TN = (((0,), (0,)), ((), ()))
NN = (((1,), (0,)), ((), ()))


def dot32(a, b, dims):
    return lax.dot_general(a, b, dims, preferred_element_type=jnp.float32)


def load_halves(own, other, whole, sem):
    half = whole.shape[0] // 2
    copies = [
        pltpu.make_async_copy(own, whole.at[pl.ds(0, half)], sem.at[0]),
        pltpu.make_async_copy(other, whole.at[pl.ds(half, half)], sem.at[1]),
    ]
    for copy in copies:
        copy.start()
    return copies


def pair_rows(block, scale=None):
    lane = lax.broadcasted_iota(jnp.int32, block.shape, 1)
    zero = jnp.zeros_like(block)
    if scale is not None:
        block = block * jnp.asarray(scale, block.dtype)
    return jnp.concatenate(
        [jnp.where(lane < HEAD, block, zero), jnp.where(lane < HEAD, zero, block)], axis=0
    )


def pair_lanes(stacked):
    rows = stacked.shape[0] // 2
    lane = lax.broadcasted_iota(jnp.int32, (rows, 2 * HEAD), 1)
    return jnp.where(lane < HEAD, stacked[:rows], stacked[rows:])


def attend_kernel(
    causal, act, q_seg, k_seg, q_pos, k_pos, q, k_own, k_oth, v_own, v_oth, o, lse,
    k_all, v_all, scores, queries, top, total, acc, sem_k, sem_v,
):
    pairs = q.shape[1] // (2 * HEAD)
    blocks = q.shape[0] // BQ
    chunks = k_all.shape[0] // BQ
    waits = load_halves(k_own, k_oth, k_all, sem_k) + load_halves(v_own, v_oth, v_all, sem_v)
    for copy in waits:
        copy.wait()

    def one_block(b, _):
        rows = pl.ds(pl.multiple_of(b * BQ, BQ), BQ)
        for h in range(pairs):
            queries[h] = pair_rows(q[rows, h * 128 : h * 128 + 128], HEAD ** (-0.5))
        top[...] = jnp.full_like(top, NEGATIVE)
        total[...] = jnp.zeros_like(total)
        acc[...] = jnp.zeros_like(acc)

        def first(j, _):
            @pl.when(act[b * chunks + j] > 0)
            def _():
                keys = pl.ds(pl.multiple_of(j * BQ, BQ), BQ)
                open_ = q_seg[rows, :] == k_seg[0:1, keys]
                if causal:
                    open_ = open_ & (q_pos[rows, :] >= k_pos[0:1, keys])
                open_ = jnp.concatenate([open_, open_], axis=0)
                for h in range(pairs):
                    s = dot32(queries[h], k_all[keys, h * 128 : h * 128 + 128], NT)
                    s = jnp.where(open_, s, NEGATIVE)
                    scores[h, j] = s
                    top[h] = jnp.maximum(top[h], s)

            return 0

        lax.fori_loop(0, chunks, first, 0)
        for h in range(pairs):
            top[h] = jnp.broadcast_to(jnp.max(top[h], axis=1, keepdims=True), top.shape[1:])

        def second(j, _):
            @pl.when(act[b * chunks + j] > 0)
            def _():
                keys = pl.ds(pl.multiple_of(j * BQ, BQ), BQ)
                for h in range(pairs):
                    e = jnp.exp(scores[h, j] - top[h])
                    total[h] = total[h] + e
                    acc[h] = acc[h] + dot32(
                        e.astype(jnp.bfloat16), v_all[keys, h * 128 : h * 128 + 128], NN
                    )

            return 0

        lax.fori_loop(0, chunks, second, 0)
        for h in range(pairs):
            denom = jnp.broadcast_to(
                jnp.sum(total[h], axis=1, keepdims=True), total.shape[1:]
            )
            o[rows, h * 128 : h * 128 + 128] = pair_lanes(acc[h] / denom).astype(o.dtype)
            line = (top[h] + jnp.log(denom)).T[0:1]
            lse[2 * h : 2 * h + 1, rows] = line[:, :BQ]
            lse[2 * h + 1 : 2 * h + 2, rows] = line[:, BQ:]
        return 0

    lax.fori_loop(0, blocks, one_block, 0)


def attend_back_kernel(
    causal, act, k_seg, q_seg, k_pos, q_pos, q, k_own, k_oth, v_own, v_oth, o, grad, lse,
    grad_q, grad_own, grad_oth,
    k_all, v_all, queries, grads, deltas, grad_queries, sem_k, sem_v,
):
    pairs = q.shape[1] // (2 * HEAD)
    blocks = q.shape[0] // BQ
    chunks = k_all.shape[0] // BQ
    waits = load_halves(k_own, k_oth, k_all, sem_k) + load_halves(v_own, v_oth, v_all, sem_v)
    grad_own[...] = jnp.zeros_like(grad_own)
    grad_oth[...] = jnp.zeros_like(grad_oth)
    head_of = lax.broadcasted_iota(jnp.int32, (HEADS, q.shape[1]), 1) // HEAD
    ones = (head_of == lax.broadcasted_iota(jnp.int32, head_of.shape, 0)).astype(jnp.float32)
    deltas[...] = lax.dot_general(
        ones,
        o[...].astype(jnp.float32) * grad[...].astype(jnp.float32),
        NT,
        precision=lax.Precision.HIGHEST,
        preferred_element_type=jnp.float32,
    )
    for copy in waits:
        copy.wait()

    def one_block(b, _):
        rows = pl.ds(pl.multiple_of(b * BQ, BQ), BQ)
        for h in range(pairs):
            queries[h] = pair_rows(q[rows, h * 128 : h * 128 + 128], HEAD ** (-0.5))
            grads[h] = pair_rows(grad[rows, h * 128 : h * 128 + 128])
        grad_queries[...] = jnp.zeros_like(grad_queries)

        def both_heads(ref, h):
            return jnp.concatenate([ref[2 * h : 2 * h + 1, rows], ref[2 * h + 1 : 2 * h + 2, rows]], axis=1)

        def one_chunk(j, target, local):
            keys = pl.ds(pl.multiple_of(j * BQ, BQ), BQ)
            own_keys = pl.ds(pl.multiple_of(local * BQ, BQ), BQ)
            open_ = k_seg[keys, :] == q_seg[0:1, rows]
            if causal:
                open_ = open_ & (k_pos[keys, :] <= q_pos[0:1, rows])
            open_ = jnp.concatenate([open_, open_], axis=1)
            for h in range(pairs):
                lanes = slice(h * 128, h * 128 + 128)
                k, v = k_all[keys, lanes], v_all[keys, lanes]
                s = jnp.where(open_, dot32(k, queries[h], NT), NEGATIVE)
                p = jnp.exp(s - both_heads(lse, h))
                ds = p * (dot32(v, grads[h], NT) - both_heads(deltas, h))
                p = p.astype(jnp.bfloat16)
                ds = ds.astype(jnp.bfloat16)
                target[0, own_keys, lanes] += dot32(ds, queries[h], NN)
                target[1, own_keys, lanes] += dot32(p, grads[h], NN)
                grad_queries[h] += dot32(ds, k, TN)

        def own_chunk(j, _):
            @pl.when(act[b * chunks + j] > 0)
            def _():
                one_chunk(j, grad_own, j)

            return 0

        def oth_chunk(j, _):
            @pl.when(act[b * chunks + j] > 0)
            def _():
                one_chunk(j, grad_oth, j - chunks // 2)

            return 0

        lax.fori_loop(0, chunks // 2, own_chunk, 0)
        lax.fori_loop(chunks // 2, chunks, oth_chunk, 0)
        for h in range(pairs):
            grad_q[rows, h * 128 : h * 128 + 128] = (
                pair_lanes(grad_queries[h]) * HEAD ** (-0.5)
            ).astype(grad_q.dtype)
        return 0

    lax.fori_loop(0, blocks, one_block, 0)


def attend_masks(sentence, other, spots, other_spots):
    n = sentence.shape[0]
    seg = jnp.concatenate([sentence, other])
    pos = jnp.concatenate([spots, other_spots])

    def down(v):
        return jnp.broadcast_to(v[:, None], (v.shape[0], BQ))

    def across(v):
        return jnp.broadcast_to(v[None, :], (8, v.shape[0]))

    blocks = sentence.reshape(-1, BQ)
    keys = seg.reshape(-1, BQ)
    live = (blocks.min(1)[:, None] <= keys.max(1)[None, :]) & (
        blocks.max(1)[:, None] >= keys.min(1)[None, :]
    )
    early = spots.reshape(-1, BQ).max(1)[:, None] >= pos.reshape(-1, BQ).min(1)[None, :]
    return {
        "forward": (down(sentence), across(seg), down(spots), across(pos)),
        "backward": (down(seg), across(sentence), down(pos), across(spots)),
        False: live.astype(jnp.int32).reshape(-1),
        True: (live & early).astype(jnp.int32).reshape(-1),
    }


def attend(masks, causal, q, k, v, k_oth, v_oth):
    n, width = q.shape
    pairs = width // (2 * HEAD)
    chunks = 2 * n // BQ
    return pl.pallas_call(
        functools.partial(attend_kernel, causal),
        out_shape=[
            jax.ShapeDtypeStruct((n, width), jnp.bfloat16),
            jax.ShapeDtypeStruct((HEADS, n), jnp.float32),
        ],
        in_specs=[SCALAR] + [ONCHIP] * 5 + [ANY] * 4,
        out_specs=[ONCHIP, ONCHIP],
        scratch_shapes=[
            pltpu.VMEM((2 * n, width), jnp.bfloat16),
            pltpu.VMEM((2 * n, width), jnp.bfloat16),
            pltpu.VMEM((pairs, chunks, 2 * BQ, BQ), jnp.float32),
            pltpu.VMEM((pairs, 2 * BQ, 128), jnp.bfloat16),
            pltpu.VMEM((pairs, 2 * BQ, 128), jnp.float32),
            pltpu.VMEM((pairs, 2 * BQ, 128), jnp.float32),
            pltpu.VMEM((pairs, 2 * BQ, 128), jnp.float32),
            pltpu.SemaphoreType.DMA((2,)),
            pltpu.SemaphoreType.DMA((2,)),
        ],
        name="attend",
    )(masks[causal], *masks["forward"], q, k, k_oth, v, v_oth)


def attend_back(masks, causal, q, k, v, k_oth, v_oth, o, lse, grad):
    n, width = q.shape
    pairs = width // (2 * HEAD)
    return pl.pallas_call(
        functools.partial(attend_back_kernel, causal),
        out_shape=[
            jax.ShapeDtypeStruct((n, width), jnp.bfloat16),
            jax.ShapeDtypeStruct((2, n, width), jnp.float32),
            jax.ShapeDtypeStruct((2, n, width), jnp.float32),
        ],
        in_specs=[SCALAR] + [ONCHIP] * 5 + [ANY] * 4 + [ONCHIP] * 3,
        out_specs=[ONCHIP] * 3,
        scratch_shapes=[
            pltpu.VMEM((2 * n, width), jnp.bfloat16),
            pltpu.VMEM((2 * n, width), jnp.bfloat16),
            pltpu.VMEM((pairs, 2 * BQ, 128), jnp.bfloat16),
            pltpu.VMEM((pairs, 2 * BQ, 128), jnp.bfloat16),
            pltpu.VMEM((HEADS, n), jnp.float32),
            pltpu.VMEM((pairs, 2 * BQ, 128), jnp.float32),
            pltpu.SemaphoreType.DMA((2,)),
            pltpu.SemaphoreType.DMA((2,)),
        ],
        name="attend_back",
    )(masks[causal], *masks["backward"], q, k, k_oth, v, v_oth, o, grad, lse)


def attend_forward(masks, causal, q, k, v):
    other = flip(jnp.stack([k, v]), "c")
    o, lse = attend(masks, causal, q, k, v, other[0], other[1])
    return (o, (q, k, v, other[0], other[1], o, lse))


def attend_backward(saved, masks, causal, grad):
    grad_q, own, other = attend_back(masks, causal, *saved, grad)
    both = own + flip(other, "c")
    return (grad_q, low(both[0]), low(both[1]))


def self_forward(x, wqkv, wout, gain, masks, causal):
    normed = low(normalize(x, gain))
    q, k, v = (low(product(normed, wqkv[i])) for i in range(3))
    attended, saved = attend_forward(masks, causal, q, k, v)
    return (x + product(attended, wout[0]), (x, normed, saved))


def self_backward(kept, wqkv, wout, gain, masks, causal, grad_out):
    x, normed, saved = kept
    grad_low = low(grad_out)
    grad_wout = low(outer_sum(saved[5], grad_low))[None]
    parts = attend_backward(saved, masks, causal, low(against_rows(grad_low, wout[0])))
    grad_wqkv = jnp.stack([low(outer_sum(normed, part)) for part in parts])
    back = sum(against_rows(part, wqkv[i]) for i, part in enumerate(parts))
    grad_in, grad_gain = norm_back(x, gain, back)
    return (grad_out + grad_in, grad_wqkv, grad_wout, grad_gain)


def cross_forward(x, memory, wqkv, wout, gain, masks):
    normed = low(normalize(x, gain))
    q = low(product(normed, wqkv[0]))
    k, v = (low(product(memory, wqkv[i])) for i in (1, 2))
    attended, saved = attend_forward(masks, False, q, k, v)
    return (x + product(attended, wout[0]), (x, normed, saved))


def cross_backward(kept, memory, wqkv, wout, gain, masks, grad_out):
    x, normed, saved = kept
    grad_low = low(grad_out)
    grad_wout = low(outer_sum(saved[5], grad_low))[None]
    grad_q, grad_k, grad_v = attend_backward(
        saved, masks, False, low(against_rows(grad_low, wout[0]))
    )
    grad_wqkv = jnp.stack(
        [
            low(outer_sum(normed, grad_q)),
            low(outer_sum(memory, grad_k)),
            low(outer_sum(memory, grad_v)),
        ]
    )
    grad_memory = against_rows(grad_k, wqkv[1]) + against_rows(grad_v, wqkv[2])
    grad_in, grad_gain = norm_back(x, gain, against_rows(grad_q, wqkv[0]))
    return (grad_out + grad_in, grad_memory, grad_wqkv, grad_wout, grad_gain)


def ffn_forward(x, wup, wdown, gain):
    normed = low(normalize(x, gain))
    hidden = [low(jnp.maximum(product(normed, wup[i]), 0.0)) for i in range(wup.shape[0])]
    y = x + sum(product(r, wdown[i]) for i, r in enumerate(hidden))
    return (y, (x, normed, hidden))


def ffn_backward(kept, wup, wdown, gain, grad_out):
    x, normed, hidden = kept
    grad_low = low(grad_out)
    grad_down = jnp.stack([low(outer_sum(r, grad_low)) for r in hidden])
    grad_hidden = [
        low(jnp.where(r > 0.0, against_rows(grad_low, wdown[i]), 0.0))
        for i, r in enumerate(hidden)
    ]
    grad_up = jnp.stack([low(outer_sum(normed, g)) for g in grad_hidden])
    back = sum(against_rows(g, wup[i]) for i, g in enumerate(grad_hidden))
    grad_in, grad_gain = norm_back(x, gain, back)
    return (grad_out + grad_in, grad_up, grad_down, grad_gain)


def shards(
    tokens,
    source,
    segments,
    loss_rows,
    targets,
    exit_depth,
    qkv_weight,
    out_weight,
    up_weight,
    down_weight,
    norm_gains,
    embed_table,
    qkv_first,
    out_first,
    up_first,
    down_first,
    gains_first,
    table_first,
    qkv_second,
    out_second,
    up_second,
    down_second,
    gains_second,
    table_second,
):
    sy, sx = lax.axis_index("sy"), lax.axis_index("sx")
    z, c = lax.axis_index("z"), lax.axis_index("c")
    s = sy * 2 + sx
    me = jnp.stack([c, z, s]).astype(jnp.int32)
    owners = lax.axis_size("z") * 2
    tok_dev = tokens.shape[2]
    loss_dev = targets.shape[2]
    voc_dev, width = embed_table.shape
    gain_count, gain_dev = norm_gains.shape
    vocabulary = voc_dev * owners
    root_width = math.sqrt(width)
    half_row = 2 * tok_dev
    unit = qkv_weight.shape[1] // 4
    fast = lax.axis_size("z") == 4 and unit % 16 == 0

    shard_of = {
        "table": embed_table[None],
        "qkv": qkv_weight,
        "out": out_weight,
        "up": up_weight,
        "down": down_weight,
    }
    shard_shapes = {name: array.shape[1:] for name, array in shard_of.items()}
    weights = {}
    for entries in BUCKETS:
        kinds = [kind for _, _, kind in entries]
        counts = block_counts(entries, shard_shapes, unit)
        shard = jnp.concatenate(
            [owned_blocks(low(shard_of[name][i]), kind, unit) for name, i, kind in entries]
        )
        if fast:
            outs = gather_bucket(me, shard, kinds, counts, unit, owners)
        else:
            everything = lax.all_gather(shard, LINE)
            outs = []
            first = 0
            for kind, count in zip(kinds, counts):
                piece = everything[:, first : first + count]
                first += count
                if kind == "row":
                    outs.append(piece.transpose(1, 0, 2, 3).reshape(count, -1, COL))
                else:
                    outs.append(
                        piece.reshape(owners, count, 4, unit, COL).transpose(0, 2, 1, 3, 4)
                    )
        for (name, i, kind), out in zip(entries, outs):
            weights[name, i] = out.reshape(-1, COL, COL) if kind == "blk" else out
    table = weights["table", 0].reshape(vocabulary, width)

    numbers = jnp.concatenate(
        [array[:, 0] for array in (tokens, source, segments, loss_rows, targets, exit_depth)],
        axis=1,
    )
    plane = doubling(numbers, ("c", "sx", "sy")).reshape(2, 2, 2, MICRO, -1)
    depths_seen = plane[..., 3 * tok_dev + 2 * loss_dev :]
    reached = jnp.stack(
        [
            jnp.sum((depths_seen >= layer_id).astype(jnp.float32), axis=(0, 1, 2, 4))
            for layer_id in range(LAYERS)
        ],
        axis=1,
    )
    small = jnp.concatenate([norm_gains.reshape(-1), reached.reshape(-1)])
    small = doubling(small, ("c", "z"))
    reach = jnp.maximum(
        jnp.sum(small[::2, gain_count * gain_dev :], axis=0).reshape(MICRO, LAYERS), 1.0
    )
    reach = lax.dynamic_index_in_dim(reach, sy, 0, False)
    gains_seen = small[:, : gain_count * gain_dev].reshape(owners, gain_count, gain_dev)
    order = jnp.arange(owners)
    rel = ((order // 2) ^ z) * 2 + ((order % 2) ^ c)
    gains_full = gains_seen[rel].transpose(1, 0, 2).reshape(gain_count, width)
    gains_full = wide(low(gains_full))

    row = lax.dynamic_index_in_dim(plane, sx ^ c, 2, False)
    row = lax.dynamic_index_in_dim(row, sy, 2, False).reshape(4, -1)
    row = row[jnp.arange(4) ^ s]
    mine = lax.dynamic_slice_in_dim(row, 2 * c, 2, 0)
    theirs = lax.dynamic_slice_in_dim(row, 2 * (1 - c), 2, 0)
    target_ids = mine[:, :tok_dev].reshape(-1)
    source_ids = mine[:, tok_dev : 2 * tok_dev].reshape(-1)
    sentence = mine[:, 2 * tok_dev : 3 * tok_dev].reshape(-1)
    other_sentence = theirs[:, 2 * tok_dev : 3 * tok_dev].reshape(-1)
    rest = 3 * tok_dev
    places = (
        mine[:, rest : rest + loss_dev] + (jnp.arange(2, dtype=jnp.int32) * tok_dev)[:, None]
    ).reshape(-1)
    wanted = mine[:, rest + loss_dev : rest + 2 * loss_dev].reshape(-1)
    depth = mine[:, rest + 2 * loss_dev :].reshape(-1)
    spots = c * half_row + jnp.arange(half_row)
    other_spots = (1 - c) * half_row + jnp.arange(half_row)
    masks = attend_masks(sentence, other_sentence, spots, other_spots)

    looked_up = table[jnp.concatenate([source_ids, target_ids])].astype(jnp.float32) * root_width
    xe = looked_up[:half_row]
    x = looked_up[half_row:]
    xe, kept_enc_self = self_forward(
        xe, weights["qkv", 0], weights["out", 0], gains_full[0], masks, False
    )
    xe, kept_enc_ffn = ffn_forward(xe, weights["up", 0], weights["down", 0], gains_full[1])
    final_gain = gains_full[2 * ENC]
    memory = low(normalize(xe, final_gain))
    kept = []
    states = []
    for layer_id in range(LAYERS):
        base = 2 * ENC + 1 + 4 * layer_id
        slot = ENC + 2 * layer_id
        x, kept_self = self_forward(
            x, weights["qkv", slot], weights["out", slot], gains_full[base], masks, True
        )
        x, kept_cross = cross_forward(
            x,
            memory,
            weights["qkv", slot + 1],
            weights["out", slot + 1],
            gains_full[base + 1],
            masks,
        )
        x, kept_ffn = ffn_forward(
            x, weights["up", ENC + layer_id], weights["down", ENC + layer_id], gains_full[base + 2]
        )
        kept.append((kept_self, kept_cross, kept_ffn))
        states.append(x)

    pick = (places[:, None] == jnp.arange(half_row)[None, :]).astype(jnp.bfloat16)
    exit_gains = [gains_full[2 * ENC + 4 + 4 * layer_id] for layer_id in range(LAYERS)]
    exits = jnp.concatenate(
        [low(product(pick, low(normalize(states[i], exit_gains[i])))) for i in range(LAYERS)]
    )
    logits = against_rows(exits, table) * LOGIT_SCALE
    wanted_all = jnp.concatenate([wanted] * LAYERS)
    hit = jnp.arange(vocabulary)[None, :] == wanted_all[:, None]
    picked = jnp.sum(jnp.where(hit, logits, 0.0), axis=-1)
    top = jnp.max(logits, axis=-1)
    lse = top + jnp.log(jnp.sum(jnp.exp(logits - top[:, None]), axis=-1))
    shares = jnp.concatenate(
        [(depth >= i).astype(jnp.float32) / reach[i] / MICRO for i in range(LAYERS)]
    )
    loss_part = jnp.sum((lse - picked) * shares)
    grad_logits = low(
        (jnp.exp(logits - lse[:, None]) - hit.astype(jnp.float32))
        * shares[:, None]
        * LOGIT_SCALE
    )
    grad_exits = product(grad_logits, table)
    table_grad = outer_sum(grad_logits, exits)

    grads = {}
    gain_parts = [None] * gain_count
    grad_x = None
    grad_memory = None
    for layer_id in reversed(range(LAYERS)):
        slot = ENC + 2 * layer_id
        base = 2 * ENC + 1 + 4 * layer_id
        count = places.shape[0]
        grad_rows = lax.dot_general(
            wide(pick),
            grad_exits[layer_id * count : (layer_id + 1) * count],
            (((0,), (0,)), ((), ())),
            precision=lax.Precision.HIGHEST,
            preferred_element_type=jnp.float32,
        )
        grad_here, gain_parts[base + 3] = norm_back(
            states[layer_id], exit_gains[layer_id], grad_rows
        )
        grad_x = grad_here if grad_x is None else grad_x + grad_here
        kept_self, kept_cross, kept_ffn = kept[layer_id]
        up, down = ("up", ENC + layer_id), ("down", ENC + layer_id)
        grad_x, grads[up], grads[down], gain_parts[base + 2] = ffn_backward(
            kept_ffn, weights[up], weights[down], gains_full[base + 2], grad_x
        )
        qkv, out = ("qkv", slot + 1), ("out", slot + 1)
        grad_x, more, grads[qkv], grads[out], gain_parts[base + 1] = cross_backward(
            kept_cross, memory, weights[qkv], weights[out], gains_full[base + 1], masks, grad_x
        )
        grad_memory = more if grad_memory is None else grad_memory + more
        qkv, out = ("qkv", slot), ("out", slot)
        grad_x, grads[qkv], grads[out], gain_parts[base] = self_backward(
            kept_self, weights[qkv], weights[out], gains_full[base], masks, True, grad_x
        )
    grad_enc, gain_parts[2 * ENC] = norm_back(xe, final_gain, grad_memory)
    up, down, qkv, out = ("up", 0), ("down", 0), ("qkv", 0), ("out", 0)
    grad_enc, grads[up], grads[down], gain_parts[1] = ffn_backward(
        kept_enc_ffn, weights[up], weights[down], gains_full[1], grad_enc
    )
    grad_enc, grads[qkv], grads[out], gain_parts[0] = self_backward(
        kept_enc_self, weights[qkv], weights[out], gains_full[0], masks, False, grad_enc
    )
    token_ids = jnp.concatenate([source_ids, target_ids])
    token_grads = low(jnp.concatenate([grad_enc, grad_x]) * root_width)
    looked = (token_ids[:, None] == jnp.arange(vocabulary)[None, :]).astype(jnp.bfloat16)
    table_grad = low(table_grad + outer_sum(looked, token_grads))
    grads["table", 0] = table_grad

    shape_of = {}
    reduced = {}
    squares = jnp.zeros((), jnp.float32)
    for entries in reversed(BUCKETS):
        kinds = [kind for _, _, kind in entries]
        counts = block_counts(entries, shard_shapes, unit)
        own = [
            grads[name, i].reshape(natural_shape(kind, count, unit, owners))
            for (name, i, kind), count in zip(entries, counts)
        ]
        if fast:
            whole = reduce_bucket(me, own, kinds, counts, unit)
            squares = squares + jnp.sum(whole * whole)
            parts = share_rows(me, whole)
        else:
            parts = []
            for array, kind in zip(own, kinds):
                if kind == "row":
                    array = array.reshape(array.shape[0], owners, 4, unit, COL)
                    array = array.transpose(1, 2, 0, 3, 4)
                parts.append(array)
            total = jnp.concatenate([wide(part) for part in parts], axis=2)
            total = lax.psum_scatter(total, LINE, scatter_dimension=0, tiled=True)
            parts = lax.psum(total, PLANE)[0]
            squares = squares + jnp.sum(parts * parts) / 4.0
        first = 0
        for (name, i, kind), count in zip(entries, counts):
            reduced[name, i] = owned_natural(parts[:, first : first + count], kind)
            first += count
    gain_grad = jnp.stack(gain_parts)
    small = all_sum(jnp.concatenate([gain_grad.reshape(-1), loss_part[None]]))
    loss_total = small[-1]
    gain_grad = small[:-1].reshape(gain_count, width)
    squares = all_sum(squares) + jnp.sum(gain_grad * gain_grad)
    grad_norm = jnp.sqrt(squares)
    clip_factor = CLIP_NORM / jnp.maximum(grad_norm, CLIP_NORM)

    def stacked(name, n):
        return wide(jnp.stack([reduced[name, i] for i in range(n)]))

    gradients = (
        stacked("qkv", ENC + 2 * LAYERS),
        stacked("out", ENC + 2 * LAYERS),
        stacked("up", ENC + LAYERS),
        stacked("down", ENC + LAYERS),
        lax.dynamic_slice_in_dim(gain_grad, (2 * z + c) * gain_dev, gain_dev, 1),
        wide(reduced["table", 0]),
    )
    masters = (qkv_weight, out_weight, up_weight, down_weight, norm_gains, embed_table)
    firsts = (qkv_first, out_first, up_first, down_first, gains_first, table_first)
    seconds = (qkv_second, out_second, up_second, down_second, gains_second, table_second)
    results = [
        adam_update(masters[i], firsts[i], seconds[i], gradients[i] * clip_factor) for i in range(6)
    ]
    gains_grad = gradients[4] * clip_factor
    return (
        loss_total,
        grad_norm,
        results[0][0],
        results[1][0],
        results[2][0],
        results[3][0],
        gains_grad,
        results[5][0],
        results[0][1],
        results[1][1],
        results[2][1],
        results[3][1],
        results[4][1],
        results[5][1],
        results[0][2],
        results[1][2],
        results[2][2],
        results[3][2],
        results[4][2],
        results[5][2],
    )


def solution(mesh):
    seq, vocab = mesh.devices.shape
    fine = Mesh(mesh.devices.reshape(2, seq // 2, vocab // 2, 2), ("sy", "sx", "z", "c"))
    ints = P(None, LINE, PLANE)
    block = P(None, LINE, None)
    gains = P(None, LINE)
    rows = P(LINE, None)
    arrays = (block, block, block, block, gains, rows)
    return jax.shard_map(
        shards,
        mesh=fine,
        in_specs=(ints,) * 6 + arrays * 3,
        out_specs=(P(), P(), block, block, block, block, gains, rows) + arrays * 2,
        check_vma=False,
    )
```

```python
import functools
import math

import jax
import jax.numpy as jnp
from jax import lax
from jax.experimental import pallas as pl
from jax.experimental.pallas import tpu as pltpu
from jax.sharding import Mesh
from jax.sharding import PartitionSpec as P

HEADS = 8
HEAD = 64
ENC = 1
LAYERS = 2
MICRO = 2
COL = 512

NORM_EPS = 1e-06
CLIP_NORM = 0.01
LEARN_RATE = 0.05
BETA_ONE = 0.9
BETA_TWO = 0.999
ADAM_EPS = 1e-08
WEIGHT_DECAY = 0.01
ADAM_STEP = 10
LOGIT_SCALE = 4.0
NEGATIVE = -1e30

PLANE = ("sy", "sx")
LINE = ("z", "c")

TABLE = ("table", 0, "blk")


def attention_parts(i):
    return (("qkv", i, "row"), ("out", i, "row"))


def feed_parts(i):
    return (("up", i, "row"), ("down", i, "blk"))


GATHERED = (
    (TABLE,) + attention_parts(0),
    feed_parts(0),
    attention_parts(1) + attention_parts(2) + feed_parts(1),
    attention_parts(3) + attention_parts(4) + feed_parts(2),
)
REDUCED = (
    feed_parts(2),
    attention_parts(3) + attention_parts(4) + feed_parts(1),
    attention_parts(1) + attention_parts(2),
    feed_parts(0),
    (TABLE,) + attention_parts(0),
)


def flip(x, axis, bit=1):
    if isinstance(axis, tuple):
        n = math.prod(lax.axis_size(a) for a in axis)
    else:
        n = lax.axis_size(axis)
    return lax.ppermute(x, axis, [(i, i ^ bit) for i in range(n)])


def bits(axis):
    n = lax.axis_size(axis)
    return [1 << k for k in range(n.bit_length() - 1)]


def gathered(x, axis):
    if isinstance(axis, tuple) or lax.axis_size(axis) <= 4:
        n = 4 if isinstance(axis, tuple) else lax.axis_size(axis)
        return jnp.stack([x] + [flip(x, axis, r) for r in range(1, n)])
    x = x[None]
    for bit in bits(axis):
        x = jnp.concatenate([x, flip(x, axis, bit)], axis=0)
    return x


def in_order(blocks, index):
    n = blocks.shape[0]
    return jnp.concatenate(
        [lax.dynamic_index_in_dim(blocks, i ^ index, 0, keepdims=True) for i in range(n)]
    )


def all_sum(x):
    for axis in ("c", "sx", "sy", "z"):
        for bit in bits(axis):
            x = x + flip(x, axis, bit)
    return x


def hold(carry, things):
    return lax.optimization_barrier((carry, things))


def step(carry, *movers):
    for mover in movers:
        carry, (mover.held, mover.arrived) = hold(carry, (mover.held, mover.arrived))
        leaving = next(mover.stages)
        carry, (arrays, mover.held) = hold(carry, ([array for array, _ in leaving], mover.held))
        mover.arrived = [
            flip(array, *route)
            if route
            else lax.psum_scatter(array, PLANE + ("z",), scatter_dimension=0, tiled=True)
            for array, (_, route) in zip(arrays, leaving)
        ]
    return carry


class Mover:
    def __init__(self):
        self.held = []
        self.arrived = []


def normalize(v, g):
    return v * lax.rsqrt(jnp.mean(v * v, axis=-1, keepdims=True) + NORM_EPS) * g


def norm_back(v, g, cotangent):
    _, pullback = jax.vjp(normalize, v, g)
    return pullback(cotangent)


def product(a, b):
    return jnp.dot(a, b, preferred_element_type=jnp.float32)


def outer_sum(a, b):
    return lax.dot_general(a, b, (((0,), (0,)), ((), ())), preferred_element_type=jnp.float32)


def against_rows(a, b):
    return lax.dot_general(a, b, (((1,), (1,)), ((), ())), preferred_element_type=jnp.float32)


def split_heads(v):
    return v.reshape(v.shape[0], HEADS, HEAD)


def low(v):
    return v.astype(jnp.bfloat16)


def wide(v):
    return v.astype(jnp.float32)


def adam_update(master, first, second, grad):
    first = BETA_ONE * first + (1.0 - BETA_ONE) * grad
    second = BETA_TWO * second + (1.0 - BETA_TWO) * grad * grad
    fixed_first = first / (1.0 - BETA_ONE**ADAM_STEP)
    fixed_second = second / (1.0 - BETA_TWO**ADAM_STEP)
    master = master - LEARN_RATE * (
        fixed_first / (jnp.sqrt(fixed_second) + ADAM_EPS) + WEIGHT_DECAY * master
    )
    return (master, first, second)


def owned_blocks(array, kind, unit):
    if kind == "row":
        rows, columns = array.shape
        return array.reshape(rows, columns // COL, COL).transpose(1, 0, 2)
    rows = array.shape[0]
    per = rows // (4 * unit)
    return array.reshape(4, per, unit, COL).transpose(1, 0, 2, 3).reshape(per, 4 * unit, COL)


def quarter_blocks(array, kind, unit, s):
    size = array.shape[0] // 4
    array = lax.dynamic_slice_in_dim(array, s * size, size, axis=0)
    if kind == "row":
        return low(array).reshape(unit, -1, COL).transpose(1, 0, 2)
    return low(array).reshape(-1, unit, COL)


def block_counts(entries, shard_shapes, unit):
    counts = []
    for name, _, kind in entries:
        rows, columns = shard_shapes[name]
        counts.append(columns // COL if kind == "row" else rows // (4 * unit))
    return counts


def natural_shape(kind, count, unit, owners):
    if kind == "row":
        return (count, owners * 4 * unit, COL)
    return (owners, 4, count, unit, COL)


def scatter_kernel(plan, unit, me_ref, *refs):
    pieces, outs, sem = refs[:10], refs[10:-1], refs[-1]
    c, z, s = me_ref[0], me_ref[1], me_ref[2]

    def put(out, kind, owner, part, rows, source):
        if kind == "row":
            start = pl.multiple_of(owner * (4 * unit) + part * unit, unit)
            target = outs[out].at[:, pl.ds(start, rows), :]
        else:
            target = outs[out].at[owner, part]
        pltpu.make_async_copy(source, target, sem.at[out]).start()

    for c_rel in range(2):
        shard, *quarters = pieces[5 * c_rel : 5 * c_rel + 5]
        for z_rel in range(4):
            owner = (z ^ z_rel) * 2 + (c ^ c_rel)
            for out, (kind, first, count) in enumerate(plan):
                last = first + count
                if z_rel == 0:
                    if kind == "row":
                        put(out, kind, owner, 0, 4 * unit, shard.at[first:last])
                    else:
                        for part in range(4):
                            rows = pl.ds(part * unit, unit)
                            put(out, kind, owner, part, unit, shard.at[first:last, rows, :])
                else:
                    for s_rel, quarter in enumerate(quarters):
                        put(out, kind, owner, s ^ s_rel, unit, quarter.at[z_rel - 1, first:last])
    for out in range(len(plan)):
        pltpu.make_async_copy(outs[out], outs[out], sem.at[out]).wait()


def collect_kernel(plan, unit, ordered, me_ref, *refs):
    grads, keep, send, sem = refs[: len(plan)], refs[len(plan)], refs[len(plan) + 1], refs[-1]
    c, z, s = me_ref[0], me_ref[1], me_ref[2]
    for c_rel, out in ((0, keep), (1, send)):
        for z_rel in range(4):
            owner = (z ^ z_rel) * 2 + (c ^ c_rel)
            for s_rel in range(4):
                part = s ^ s_rel
                for grad, (kind, first, count) in zip(grads, plan):
                    if kind == "row":
                        start = pl.multiple_of(owner * (4 * unit) + part * unit, unit)
                        source = grad.at[:, pl.ds(start, unit), :]
                    else:
                        source = grad.at[owner, part]
                    place = (part, z ^ z_rel) if ordered else (s_rel, z_rel)
                    target = out.at[*place, first : first + count]
                    pltpu.make_async_copy(source, target, sem.at[c_rel]).start()
    for c_rel, out in ((0, keep), (1, send)):
        pltpu.make_async_copy(out, out, sem.at[c_rel]).wait()


LIGHT = pl.CostEstimate(flops=1, bytes_accessed=1, transcendentals=0)
ANY = pl.BlockSpec(memory_space=pl.ANY)
ONCHIP = pl.BlockSpec(memory_space=pltpu.VMEM)
SCALAR = pl.BlockSpec(memory_space=pltpu.SMEM)


def gather_stages(mover, me, shard, kinds, counts, unit, owners):
    starts = [sum(counts[:i]) for i in range(len(counts))]
    mover.held = [shard]
    part = lax.dynamic_slice_in_dim(shard, me[2] * unit, unit, axis=1)
    yield [(part, ("z", bit)) for bit in (1, 2, 3)]
    mine = jnp.stack(mover.arrived)
    mover.held.append(mine)
    yield [(mine, (PLANE, bit)) for bit in (1, 2, 3)]
    mover.held += mover.arrived
    yield [(piece, ("c",)) for piece in mover.held]
    plan = tuple(zip(kinds, starts, counts))
    mover.result = pl.pallas_call(
        functools.partial(scatter_kernel, plan, unit),
        out_shape=[
            jax.ShapeDtypeStruct(natural_shape(kind, count, unit, owners), jnp.bfloat16)
            for kind, count in zip(kinds, counts)
        ],
        in_specs=[SCALAR] + [ANY] * 10,
        out_specs=[ONCHIP] * len(plan),
        scratch_shapes=[pltpu.SemaphoreType.DMA((len(plan),))],
        cost_estimate=LIGHT,
        name="place_weights",
    )(me, *mover.held, *mover.arrived)
    mover.held = []
    yield []


def unpack_kernel(plan, pieces, *refs):
    outs, sem = refs[:-1], refs[-1]
    for out, (kind, first, count) in enumerate(plan):
        for part in range(4):
            if kind == "blk":
                source = pieces.at[part, :, first : first + count]
                pltpu.make_async_copy(source, outs[out].at[:, part], sem.at[out]).start()
                continue
            for k in range(count):
                source = pieces.at[part, :, first + k]
                pltpu.make_async_copy(source, outs[out].at[k, :, part], sem.at[out]).start()
    for out in range(len(plan)):
        pltpu.make_async_copy(outs[out], outs[out], sem.at[out]).wait()


def unpack(pieces, kinds, counts, unit, owners):
    starts = [sum(counts[:i]) for i in range(len(counts))]
    shapes = [
        (count, owners, 4, unit, COL) if kind == "row" else (owners, 4, count, unit, COL)
        for kind, count in zip(kinds, counts)
    ]
    placed = pl.pallas_call(
        functools.partial(unpack_kernel, tuple(zip(kinds, starts, counts))),
        out_shape=[jax.ShapeDtypeStruct(shape, jnp.bfloat16) for shape in shapes],
        in_specs=[ANY],
        out_specs=[ONCHIP] * len(shapes),
        scratch_shapes=[pltpu.SemaphoreType.DMA((len(shapes),))],
        cost_estimate=LIGHT,
        name="place_gathered",
    )(pieces)
    return [
        out.reshape(count, -1, COL) if kind == "row" else out
        for out, kind, count in zip(placed, kinds, counts)
    ]


def added(arrays):
    total = wide(arrays[0])
    for array in arrays[1:]:
        total = total + wide(array)
    return total


def collect(me, grads, kinds, counts, unit, ordered):
    starts = [sum(counts[:i]) for i in range(len(counts))]
    plan = tuple(zip(kinds, starts, counts))
    shape = jax.ShapeDtypeStruct((4, 4, sum(counts), unit, COL), jnp.bfloat16)
    return pl.pallas_call(
        functools.partial(collect_kernel, plan, unit, ordered),
        out_shape=[shape, shape],
        in_specs=[SCALAR] + [ANY] * len(plan),
        out_specs=[ONCHIP, ONCHIP],
        scratch_shapes=[pltpu.SemaphoreType.DMA((2,))],
        cost_estimate=LIGHT,
        name="collect_gradients",
    )(me, *grads)


def long_reduce_stages(mover, me, grads, kinds, counts, unit):
    keep, send = collect(me, grads, kinds, counts, unit, True)
    mover.held = [keep]
    yield [(send, ("c",))]
    chip = low(added(mover.held + mover.arrived))
    mover.held = []
    yield [(chip.reshape(16, *chip.shape[2:]), None)]
    own = mover.arrived[0][0]
    mover.squares = jnp.sum(wide(own) * wide(own))
    mover.held = [own]
    yield [(own, (PLANE, bit)) for bit in (1, 2, 3)]
    mover.result = mover.held + mover.arrived
    mover.held = []
    yield []


def reduce_stages(mover, me, grads, kinds, counts, unit):
    total = sum(counts)
    keep, send = collect(me, grads, kinds, counts, unit, False)
    mover.held = [keep]
    half = total // 2
    yield [(send, ("c",))]
    mover.held = [a.reshape(2, 2, *a.shape[1:]) for a in mover.held + mover.arrived]
    yield [
        (low(added([a[:, 1, :, :half] for a in mover.held])), ("sx",)),
        (low(added([a[1, :, :, half:] for a in mover.held])), ("sy",)),
    ]
    mover.held += mover.arrived

    def sides():
        both, (come_x, come_y) = mover.held[:2], mover.held[2:4]
        return (
            [a[:, 0, :, :half] for a in both] + [come_x],
            [a[0, :, :, half:] for a in both] + [come_y],
        )

    left, right = sides()
    yield [(low(added([a[1] for a in left])), ("sy",)), (low(added([a[1] for a in right])), ("sx",))]
    mover.held += mover.arrived

    def plane(bit):
        left, right = sides()
        left = [a[0, bit] for a in left] + [mover.held[4][bit]]
        right = [a[0, bit] for a in right] + [mover.held[5][bit]]
        return jnp.concatenate([added(left), added(right)], axis=0)

    yield [(low(plane(bit)), ("z", bit)) for bit in (1, 2, 3)]
    own = plane(0)
    mover.arrived.insert(0, own)
    whole = added(mover.arrived)
    mover.squares = jnp.sum(whole * whole)
    mover.held = [low(whole)]
    yield [(mover.held[0], (PLANE, bit)) for bit in (1, 2, 3)]
    mover.result = mover.held + mover.arrived
    mover.held = []
    yield []


def settle_kernel(sizes, plan, unit, me_ref, *refs):
    buckets, outs, sem = refs[:sizes], refs[sizes:-1], refs[-1]
    s = me_ref[2]
    for bucket, first, count, kind, out, i in plan:
        for s_rel in range(4):
            source = buckets[4 * bucket + s_rel]
            part = s ^ s_rel
            if kind == "blk":
                for k in range(count):
                    start = pl.multiple_of((part * count + k) * unit, unit)
                    target = outs[out].at[i, pl.ds(start, unit), :]
                    pltpu.make_async_copy(source.at[first + k], target, sem.at[out]).start()
                continue
            rows = pl.ds(pl.multiple_of(part * unit, unit), unit)
            for k in range(count):
                target = outs[out].at[i, rows, k * COL : k * COL + COL]
                pltpu.make_async_copy(source.at[first + k], target, sem.at[out]).start()
    for out, ref in enumerate(outs):
        pltpu.make_async_copy(ref, ref, sem.at[out]).wait()


def owned_natural(parts, kind):
    if kind == "row":
        four, count, unit, _ = parts.shape
        return parts.transpose(0, 2, 1, 3).reshape(four * unit, count * COL)
    return parts.reshape(-1, COL)


BQ = 128
CK = 256
CF = 256
NT = (((1,), (1,)), ((), ()))
TN = (((0,), (0,)), ((), ()))
NN = (((1,), (0,)), ((), ()))


def dot32(a, b, dims):
    return lax.dot_general(a, b, dims, preferred_element_type=jnp.float32)


def load_halves(own, other, whole, sem):
    half = whole.shape[0] // 2
    copies = [
        pltpu.make_async_copy(own, whole.at[pl.ds(0, half)], sem.at[0]),
        pltpu.make_async_copy(other, whole.at[pl.ds(half, half)], sem.at[1]),
    ]
    for copy in copies:
        copy.start()
    return copies


def pair_rows(block, scale=None):
    lane = lax.broadcasted_iota(jnp.int32, block.shape, 1)
    zero = jnp.zeros_like(block)
    if scale is not None:
        block = block * jnp.asarray(scale, block.dtype)
    return jnp.concatenate(
        [jnp.where(lane < HEAD, block, zero), jnp.where(lane < HEAD, zero, block)], axis=0
    )


def pair_lanes(stacked):
    rows = stacked.shape[0] // 2
    lane = lax.broadcasted_iota(jnp.int32, (rows, 2 * HEAD), 1)
    return jnp.where(lane < HEAD, stacked[:rows], stacked[rows:])


def open_to(act, bounds, rows, j, chunks):
    half = chunks // 2
    base = jnp.where(j < half, act[0] + j * CK, act[1] + (j - half) * CK)
    spot = base + lax.broadcasted_iota(jnp.int32, (CK, BQ), 0)
    open_ = (spot >= bounds[0:1, rows]) & (spot <= bounds[1:2, rows])
    return jnp.concatenate([open_, open_], axis=1)


def attend_kernel(
    act, bounds, q, kv_own, kv_oth, o, lse,
    k_all, v_all, scores, queries, top, total, acc, sem_k, sem_v,
):
    pairs = q.shape[1] // (2 * HEAD)
    blocks = q.shape[0] // BQ
    chunks = k_all.shape[0] // CF
    half = chunks // 2
    waits = load_halves(kv_own.at[0], kv_oth.at[0], k_all, sem_k)
    waits += load_halves(kv_own.at[1], kv_oth.at[1], v_all, sem_v)
    for copy in waits:
        copy.wait()
    square = lax.broadcasted_iota(jnp.int32, (BQ, BQ), 0)
    along = lax.broadcasted_iota(jnp.int32, (BQ, BQ), 1)

    def one_block(b, _):
        rows = pl.ds(pl.multiple_of(b * BQ, BQ), BQ)
        for h in range(pairs):
            queries[h] = pair_rows(q[rows, h * 128 : h * 128 + 128], HEAD ** (-0.5))
        top[...] = jnp.full_like(top, NEGATIVE)
        total[...] = jnp.zeros_like(total)
        acc[...] = jnp.zeros_like(acc)
        least = jnp.broadcast_to(bounds[0:1, rows], (BQ, BQ)).T
        most = jnp.broadcast_to(bounds[1:2, rows], (BQ, BQ)).T

        def first(j, _):
            @pl.when(act[2 + b * chunks + j] > 0)
            def _():
                keys = pl.ds(pl.multiple_of(j * CF, CF), CF)
                base = jnp.where(j < half, act[0] + j * CF, act[1] + (j - half) * CF)
                open_ = []
                for part in range(CF // 128):
                    spot = base + part * 128 + along
                    one = (spot >= least) & (spot <= most)
                    open_.append(jnp.concatenate([one, one], axis=0))
                for h in range(pairs):
                    s = dot32(queries[h], k_all[keys, h * 128 : h * 128 + 128], NT)
                    best = top[h]
                    for part, one in enumerate(open_):
                        t = jnp.where(one, s[:, part * 128 : part * 128 + 128], NEGATIVE)
                        scores[h, j, :, part * 128 : part * 128 + 128] = t
                        best = jnp.maximum(best, t)
                    top[h] = best

            return 0

        lax.fori_loop(0, chunks, first, 0)
        for h in range(pairs):
            top[h] = jnp.broadcast_to(jnp.max(top[h], axis=1, keepdims=True), top.shape[1:])

        def second(j, _):
            @pl.when(act[2 + b * chunks + j] > 0)
            def _():
                keys = pl.ds(pl.multiple_of(j * CF, CF), CF)
                for h in range(pairs):
                    parts = []
                    more = total[h]
                    for part in range(CF // 128):
                        e = jnp.exp(scores[h, j, :, part * 128 : part * 128 + 128] - top[h])
                        more = more + e
                        parts.append(e.astype(jnp.bfloat16))
                    total[h] = more
                    e = parts[0] if len(parts) == 1 else jnp.concatenate(parts, axis=1)
                    acc[h] = acc[h] + dot32(e, v_all[keys, h * 128 : h * 128 + 128], NN)

            return 0

        lax.fori_loop(0, chunks, second, 0)
        for h in range(pairs):
            denom = jnp.broadcast_to(
                jnp.sum(total[h], axis=1, keepdims=True), total.shape[1:]
            )
            o[rows, h * 128 : h * 128 + 128] = pair_lanes(acc[h] / denom).astype(o.dtype)
            level = top[h] + jnp.log(denom)
            for part in range(2):
                own = jnp.where(square == along, level[part * BQ : part * BQ + BQ], 0.0)
                lse[b, h, :, part * BQ : part * BQ + BQ] = jnp.sum(own, axis=0, keepdims=True)
        return 0

    lax.fori_loop(0, blocks, one_block, 0)


def attend_back_kernel(
    act, bounds, q, kv_own, kv_oth, o, lse, grad,
    grad_q, grad_own, grad_oth,
    k_all, v_all, k_turned, queries, grads, delta, grad_queries, sem_k, sem_v,
):
    pairs = q.shape[1] // (2 * HEAD)
    blocks = q.shape[0] // BQ
    chunks = k_all.shape[0] // CK
    waits = load_halves(kv_own.at[0], kv_oth.at[0], k_all, sem_k)
    waits += load_halves(kv_own.at[1], kv_oth.at[1], v_all, sem_v)
    grad_own[...] = jnp.zeros_like(grad_own)
    grad_oth[...] = jnp.zeros_like(grad_oth)
    for copy in waits:
        copy.wait()

    def turn(j, _):
        for h in range(pairs):
            for part in range(CK // 128):
                keys = pl.ds(pl.multiple_of(j * CK + part * 128, 128), 128)
                k_turned[j, h, :, part * 128 : part * 128 + 128] = k_all[
                    keys, h * 128 : h * 128 + 128
                ].T
        return 0

    lax.fori_loop(0, chunks, turn, 0)

    def one_block(b, _):
        rows = pl.ds(pl.multiple_of(b * BQ, BQ), BQ)
        for h in range(pairs):
            lanes = slice(h * 128, h * 128 + 128)
            queries[h] = pair_rows(q[rows, lanes], HEAD ** (-0.5))
            grads[h] = pair_rows(grad[rows, lanes])
            both = (o[rows, lanes].astype(jnp.float32) * grad[rows, lanes].astype(jnp.float32)).T
            delta[h] = jnp.concatenate(
                [
                    jnp.sum(both[:HEAD], axis=0, keepdims=True),
                    jnp.sum(both[HEAD:], axis=0, keepdims=True),
                ],
                axis=1,
            )
        grad_queries[...] = jnp.zeros_like(grad_queries)

        def one_chunk(j, target, local):
            keys = pl.ds(pl.multiple_of(j * CK, CK), CK)
            own_keys = pl.ds(pl.multiple_of(local * CK, CK), CK)
            open_ = open_to(act, bounds, rows, j, chunks)
            for h in range(pairs):
                lanes = slice(h * 128, h * 128 + 128)
                s = jnp.where(open_, dot32(k_all[keys, lanes], queries[h], NT), NEGATIVE)
                p = jnp.exp(s - lse[b, h])
                ds = p * (dot32(v_all[keys, lanes], grads[h], NT) - delta[h])
                p = p.astype(jnp.bfloat16)
                ds = ds.astype(jnp.bfloat16)
                target[0, own_keys, lanes] += dot32(ds, queries[h], NN)
                target[1, own_keys, lanes] += dot32(p, grads[h], NN)
                grad_queries[h] += dot32(k_turned[j, h], ds, NN)

        def own_chunk(j, _):
            @pl.when(act[2 + b * chunks + j] > 0)
            def _():
                one_chunk(j, grad_own, j)

            return 0

        def oth_chunk(j, _):
            @pl.when(act[2 + b * chunks + j] > 0)
            def _():
                one_chunk(j, grad_oth, j - chunks // 2)

            return 0

        lax.fori_loop(0, chunks // 2, own_chunk, 0)
        lax.fori_loop(chunks // 2, chunks, oth_chunk, 0)
        for h in range(pairs):
            grad_q[rows, h * 128 : h * 128 + 128] = (
                pair_lanes(grad_queries[h].T) * HEAD ** (-0.5)
            ).astype(grad_q.dtype)
        return 0

    lax.fori_loop(0, blocks, one_block, 0)


def attend_masks(sentence, other, start, other_start):
    n = sentence.shape[0]
    seg = jnp.concatenate([sentence, other])
    spots = start + jnp.arange(n, dtype=jnp.int32)
    pos = jnp.concatenate([spots, other_start + jnp.arange(n, dtype=jnp.int32)])
    begin = jnp.sum((seg[None, :] < sentence[:, None]).astype(jnp.int32), axis=1)
    end = jnp.sum((seg[None, :] <= sentence[:, None]).astype(jnp.int32), axis=1) - 1
    made = {}
    for causal, last, size in ((c, l, k) for c, l in ((False, end), (True, spots)) for k in (CF, CK)):
        keys = pos.reshape(-1, size)
        live = (begin.reshape(-1, BQ).min(1)[:, None] <= keys.max(1)[None, :]) & (
            last.reshape(-1, BQ).max(1)[:, None] >= keys.min(1)[None, :]
        )
        starts = jnp.stack([start, other_start]).astype(jnp.int32)
        act = jnp.concatenate([starts, live.astype(jnp.int32).reshape(-1)])
        made[causal, size] = (act, jnp.pad(jnp.stack([begin, last]), ((0, 6), (0, 0))))
    return made


def attend(masks, causal, q, kv, kv_oth):
    n, width = q.shape
    pairs = width // (2 * HEAD)
    return pl.pallas_call(
        attend_kernel,
        out_shape=[
            jax.ShapeDtypeStruct((n, width), jnp.bfloat16),
            jax.ShapeDtypeStruct((n // BQ, pairs, 1, 2 * BQ), jnp.float32),
        ],
        in_specs=[SCALAR] + [ONCHIP] * 2 + [ANY] * 2,
        out_specs=[ONCHIP, ONCHIP],
        scratch_shapes=[
            pltpu.VMEM((2 * n, width), jnp.bfloat16),
            pltpu.VMEM((2 * n, width), jnp.bfloat16),
            pltpu.VMEM((pairs, 2 * n // CF, 2 * BQ, CF), jnp.float32),
            pltpu.VMEM((pairs, 2 * BQ, 128), jnp.bfloat16),
            pltpu.VMEM((pairs, 2 * BQ, 128), jnp.float32),
            pltpu.VMEM((pairs, 2 * BQ, 128), jnp.float32),
            pltpu.VMEM((pairs, 2 * BQ, 128), jnp.float32),
            pltpu.SemaphoreType.DMA((2,)),
            pltpu.SemaphoreType.DMA((2,)),
        ],
        cost_estimate=LIGHT,
        name="attend",
    )(*masks[causal, CF], q, kv, kv_oth)


def attend_back(masks, causal, q, kv, kv_oth, o, lse, grad):
    n, width = q.shape
    pairs = width // (2 * HEAD)
    chunks = 2 * n // CK
    return pl.pallas_call(
        attend_back_kernel,
        out_shape=[
            jax.ShapeDtypeStruct((n, width), jnp.bfloat16),
            jax.ShapeDtypeStruct((2, n, width), jnp.float32),
            jax.ShapeDtypeStruct((2, n, width), jnp.float32),
        ],
        in_specs=[SCALAR] + [ONCHIP] * 2 + [ANY] * 2 + [ONCHIP] * 3,
        out_specs=[ONCHIP] * 3,
        scratch_shapes=[
            pltpu.VMEM((2 * n, width), jnp.bfloat16),
            pltpu.VMEM((2 * n, width), jnp.bfloat16),
            pltpu.VMEM((chunks, pairs, 128, CK), jnp.bfloat16),
            pltpu.VMEM((pairs, 2 * BQ, 128), jnp.bfloat16),
            pltpu.VMEM((pairs, 2 * BQ, 128), jnp.bfloat16),
            pltpu.VMEM((pairs, 1, 2 * BQ), jnp.float32),
            pltpu.VMEM((pairs, 128, 2 * BQ), jnp.float32),
            pltpu.SemaphoreType.DMA((2,)),
            pltpu.SemaphoreType.DMA((2,)),
        ],
        cost_estimate=LIGHT,
        name="attend_back",
    )(*masks[causal, CK], q, kv, kv_oth, o, lse, grad)


def rms(v, gain):
    scale = lax.rsqrt(jnp.mean(v * v, axis=-1, keepdims=True) + NORM_EPS)
    return v * scale * gain


def rms_back(v, gain, grad):
    scale = lax.rsqrt(jnp.mean(v * v, axis=-1, keepdims=True) + NORM_EPS)
    scaled = grad * gain
    lean = jnp.mean(scaled * v, axis=-1, keepdims=True) * (scale * scale * scale)
    return scaled * scale - v * lean, jnp.sum(grad * v * scale, axis=0, keepdims=True)


def project_kernel(x, gain, w, normed, q, kv):
    a = low(rms(x[...], gain[...]))
    normed[...] = a
    q[...] = low(dot32(a, w[0], NN))
    kv[0] = low(dot32(a, w[1], NN))
    kv[1] = low(dot32(a, w[2], NN))


def between_kernel(o, w_out, x, gain, w, y, normed, q):
    state = x[...] + dot32(o[...], w_out[0], NN)
    y[...] = state
    c = low(rms(state, gain[...]))
    normed[...] = c
    q[...] = low(dot32(c, w[0], NN))


def feed_kernel(o, w_out, x, gain, w_up, w_down, y, normed, hidden, z):
    state = x[...] + dot32(o[...], w_out[0], NN)
    y[...] = state
    f = low(rms(state, gain[...]))
    normed[...] = f
    for i in range(w_up.shape[0]):
        r = low(jnp.maximum(dot32(f, w_up[i], NN), 0.0))
        hidden[i] = r
        state = state + dot32(r, w_down[i], NN)
    z[...] = state


def out_back(g, o, w_out, grad_o, grad_out):
    grad_o[...] = low(dot32(g, w_out[0], NT))
    grad_out[0] = low(dot32(o[...], g, TN))


def feed_back_kernel(
    grad, y, normed, hidden, gain, w_up, w_down, o, w_out,
    grad_up, grad_down, grad_y, grad_gain, grad_o, grad_out,
):
    g = low(grad[...])
    f = normed[...]
    back = jnp.zeros(grad.shape, jnp.float32)
    for i in range(w_up.shape[0]):
        r = hidden[i]
        grad_down[i] = low(dot32(r, g, TN))
        h = low(jnp.where(r > 0, dot32(g, w_down[i], NT), 0.0))
        grad_up[i] = low(dot32(f, h, TN))
        back = back + dot32(h, w_up[i], NT)
    more, grad_gain[...] = rms_back(y[...], gain[...], back)
    total = grad[...] + more
    grad_y[...] = total
    out_back(low(total), o, w_out, grad_o, grad_out)


def between_back_kernel(
    grad_q, normed, y, gain, w, grad, o, w_out,
    grad_w, grad_x, grad_gain, grad_o, grad_out,
):
    g = grad_q[...]
    grad_w[0] = low(dot32(normed[...], g, TN))
    more, grad_gain[...] = rms_back(y[...], gain[...], dot32(g, w[0], NT))
    total = grad[...] + more
    grad_x[...] = total
    out_back(low(total), o, w_out, grad_o, grad_out)


def memory_back_kernel(own, other, memory, w, grad_w, grad_memory):
    m = memory[...]
    total = None
    for i in range(2):
        g = low(own[i] + other[i])
        grad_w[i] = low(dot32(m, g, TN))
        part = dot32(g, w[i + 1], NT)
        total = part if total is None else total + part
    grad_memory[...] = total


def project_back_kernel(
    grad_q, own, other, normed, x, gain, w, grad,
    grad_w, grad_x, grad_gain,
):
    a = normed[...]
    back = None
    for i in range(3):
        g = grad_q[...] if i == 0 else low(own[i - 1] + other[i - 1])
        grad_w[i] = low(dot32(a, g, TN))
        part = dot32(g, w[i], NT)
        back = part if back is None else back + part
    more, grad_gain[...] = rms_back(x[...], gain[...], back)
    grad_x[...] = grad[...] + more


def on_chip(kernel, name, outs, *args):
    return pl.pallas_call(
        kernel,
        out_shape=[jax.ShapeDtypeStruct(shape, kind) for shape, kind in outs],
        in_specs=[ONCHIP] * len(args),
        out_specs=[ONCHIP] * len(outs),
        cost_estimate=LIGHT,
        name=name,
    )(*args)


def shaped(lead, like, kind):
    return (lead + like.shape, kind)


HALF, FULL = jnp.bfloat16, jnp.float32


def attend_forward(masks, causal, q, kv):
    other = flip(kv, "c")
    o, lse = attend(masks, causal, q, kv, other)
    return o, (q, kv, other, o, lse)


def attend_backward(saved, masks, causal, grad):
    grad_q, own, other = attend_back(masks, causal, *saved, grad)
    return grad_q, own, flip(other, "c")


def project(x, gain, w):
    return on_chip(
        project_kernel,
        "project",
        [shaped((), x, HALF), shaped((), x, HALF), shaped((2,), x, HALF)],
        x, gain[None], w,
    )


def between(o, w_out, x, gain, w):
    return on_chip(
        between_kernel,
        "between",
        [shaped((), x, FULL), shaped((), x, HALF), shaped((), x, HALF)],
        o, w_out, x, gain[None], w,
    )


def feed(o, w_out, x, gain, w_up, w_down):
    return on_chip(
        feed_kernel,
        "feed",
        [
            shaped((), x, FULL),
            shaped((), x, HALF),
            shaped((w_up.shape[0],), x, HALF),
            shaped((), x, FULL),
        ],
        o, w_out, x, gain[None], w_up, w_down,
    )


def feed_back(grad, kept, gain, w_up, w_down, o, w_out):
    y, normed, hidden = kept
    return on_chip(
        feed_back_kernel,
        "feed_back",
        [
            (w_up.shape, HALF),
            (w_down.shape, HALF),
            shaped((), y, FULL),
            ((1, y.shape[1]), FULL),
            shaped((), y, HALF),
            (w_out.shape, HALF),
        ],
        grad, y, normed, hidden, gain[None], w_up, w_down, o, w_out,
    )


def between_back(grad_q, normed, y, gain, w, grad, o, w_out):
    return on_chip(
        between_back_kernel,
        "between_back",
        [
            (w_out.shape, HALF),
            shaped((), y, FULL),
            ((1, y.shape[1]), FULL),
            shaped((), y, HALF),
            (w_out.shape, HALF),
        ],
        grad_q, normed, y, gain[None], w, grad, o, w_out,
    )


def memory_back(own, other, memory, w):
    return on_chip(
        memory_back_kernel,
        "memory_back",
        [((2,) + w.shape[1:], HALF), shaped((), memory, FULL)],
        own, other, memory, w,
    )


def project_back(grad_q, own, other, normed, x, gain, w, grad):
    return on_chip(
        project_back_kernel,
        "project_back",
        [(w.shape, HALF), shaped((), x, FULL), ((1, x.shape[1]), FULL)],
        grad_q, own, other, normed, x, gain[None], w, grad,
    )


def shards(
    tokens,
    source,
    segments,
    loss_rows,
    targets,
    exit_depth,
    qkv_weight,
    out_weight,
    up_weight,
    down_weight,
    norm_gains,
    embed_table,
    qkv_first,
    out_first,
    up_first,
    down_first,
    gains_first,
    table_first,
    qkv_second,
    out_second,
    up_second,
    down_second,
    gains_second,
    table_second,
):
    sy, sx = lax.axis_index("sy"), lax.axis_index("sx")
    z, c = lax.axis_index("z"), lax.axis_index("c")
    s = sy * 2 + sx
    me = jnp.stack([c, z, s]).astype(jnp.int32)
    owners = lax.axis_size("z") * 2
    tok_dev = tokens.shape[2]
    loss_dev = targets.shape[2]
    voc_dev, width = embed_table.shape
    gain_count, gain_dev = norm_gains.shape
    vocabulary = voc_dev * owners
    root_width = math.sqrt(width)
    half_row = 2 * tok_dev
    unit = qkv_weight.shape[1] // 4
    fast = lax.axis_size("z") == 4 and unit % 16 == 0

    shard_of = {
        "table": embed_table[None],
        "qkv": qkv_weight,
        "out": out_weight,
        "up": up_weight,
        "down": down_weight,
    }
    shard_shapes = {name: array.shape[1:] for name, array in shard_of.items()}
    weights = {}

    def layout(entries):
        kinds = [kind for _, _, kind in entries]
        return kinds, block_counts(entries, shard_shapes, unit)

    def packed(entries):
        return jnp.concatenate(
            [owned_blocks(low(shard_of[name][i]), kind, unit) for name, i, kind in entries]
        )

    def gather(entries):
        mover = Mover()
        mover.stages = gather_stages(mover, me, packed(entries), *layout(entries), unit, owners)
        return mover

    def settle(entries, outs):
        for (name, i, kind), out in zip(entries, outs):
            weights[name, i] = out.reshape(-1, COL, COL) if kind == "blk" else out

    def gather_plainly(entries):
        everything = lax.all_gather(packed(entries), LINE)
        outs = []
        first = 0
        for kind, count in zip(*layout(entries)):
            piece = everything[:, first : first + count]
            first += count
            if kind == "row":
                outs.append(piece.transpose(1, 0, 2, 3).reshape(count, -1, COL))
            else:
                outs.append(piece.reshape(owners, count, 4, unit, COL).transpose(0, 2, 1, 3, 4))
        settle(entries, outs)

    def pieces(entries):
        arrays, kinds, counts = [], [], []
        for (name, i, kind), count in zip(entries, layout(entries)[1]):
            held = grads[name, i]
            for array in held if isinstance(held, tuple) else (held,):
                blocks = array.shape[0] if isinstance(held, tuple) else count
                arrays.append(array.reshape(natural_shape(kind, blocks, unit, owners)))
                kinds.append(kind)
                counts.append(blocks)
        return arrays, kinds, counts

    def reduce(entries, stages=reduce_stages):
        arrays, kinds, counts = pieces(entries)
        mover = Mover()
        mover.stages = stages(mover, me, arrays, kinds, counts, unit)
        return mover

    def take(entries, parts):
        first = 0
        for (name, i, kind), count in zip(entries, layout(entries)[1]):
            reduced[name, i] = owned_natural(parts[:, first : first + count], kind)
            first += count

    def reduce_plainly(entries):
        parts = []
        for array, kind, count in zip(*pieces(entries)):
            if kind == "row":
                array = array.reshape(count, owners, 4, unit, COL).transpose(1, 2, 0, 3, 4)
            parts.append(wide(array))
        total = jnp.concatenate(parts, axis=2)
        total = lax.psum_scatter(total, LINE, scatter_dimension=0, tiled=True)
        total = lax.psum(total, PLANE)[0]
        take(entries, total)
        return jnp.sum(total * total) / 4.0

    if fast:
        first = gather(GATHERED[0])
        ints = [tokens, source, segments, loss_rows, targets, exit_depth]
        ints, shard_of = step((ints, shard_of), first)
        tokens, source, segments, loss_rows, targets, exit_depth = ints
        second = gather(GATHERED[1])

        def gather_long(entries):
            return jnp.concatenate(
                [quarter_blocks(shard_of[name][i], kind, unit, s) for name, i, kind in entries]
            )

        third, fourth = gather_long(GATHERED[2]), gather_long(GATHERED[3])
    if not fast:
        for entries in GATHERED:
            gather_plainly(entries)

    numbers = jnp.concatenate(
        [array[:, 0] for array in (tokens, source, segments, loss_rows, targets, exit_depth)],
        axis=1,
    )
    plane = gathered(gathered(numbers, "c"), PLANE)
    depths_seen = plane[..., 3 * tok_dev + 2 * loss_dev :]
    reached = jnp.stack(
        [
            jnp.sum((depths_seen >= layer_id).astype(jnp.float32), axis=(0, 1, 3))
            for layer_id in range(LAYERS)
        ],
        axis=1,
    )
    if fast:
        reached, norm_gains_now, third = step((reached, norm_gains, third), first)
        third = lax.all_gather(third, PLANE + LINE).reshape(4, owners, *third.shape)
        reached, norm_gains_now = step((reached, norm_gains_now), second)
    else:
        norm_gains_now = norm_gains
    small = jnp.concatenate([norm_gains_now.reshape(-1), reached.reshape(-1)])
    small = gathered(gathered(small, "c"), "z").reshape(owners, -1)
    reach = jnp.maximum(
        jnp.sum(small[::2, gain_count * gain_dev :], axis=0).reshape(MICRO, LAYERS), 1.0
    )
    reach = lax.dynamic_index_in_dim(reach, sy, 0, False)
    gains_seen = small[:, : gain_count * gain_dev].reshape(owners, gain_count, gain_dev)
    order = jnp.arange(owners)
    rel = ((order // 2) ^ z) * 2 + ((order % 2) ^ c)
    gains_full = gains_seen[rel].transpose(1, 0, 2).reshape(gain_count, width)
    gains_full = wide(low(gains_full))

    row = lax.dynamic_index_in_dim(plane, sx ^ c, 1, False)
    row = in_order(lax.dynamic_index_in_dim(row, sy, 1, False), s)
    mine = lax.dynamic_slice_in_dim(row, 2 * c, 2, 0)
    theirs = lax.dynamic_slice_in_dim(row, 2 * (1 - c), 2, 0)
    target_ids = mine[:, :tok_dev].reshape(-1)
    source_ids = mine[:, tok_dev : 2 * tok_dev].reshape(-1)
    sentence = mine[:, 2 * tok_dev : 3 * tok_dev].reshape(-1)
    other_sentence = theirs[:, 2 * tok_dev : 3 * tok_dev].reshape(-1)
    rest = 3 * tok_dev
    places = (
        mine[:, rest : rest + loss_dev] + (jnp.arange(2, dtype=jnp.int32) * tok_dev)[:, None]
    ).reshape(-1)
    wanted = mine[:, rest + loss_dev : rest + 2 * loss_dev].reshape(-1)
    depth = mine[:, rest + 2 * loss_dev :].reshape(-1)
    masks = attend_masks(sentence, other_sentence, c * half_row, (1 - c) * half_row)

    ids = jnp.concatenate([source_ids, target_ids])
    if fast:
        ids = step(ids, first)
        ids = step(ids, second, first)
        settle(GATHERED[0], first.result)
    table = weights["table", 0].reshape(vocabulary, width)
    looked_up = table[ids].astype(jnp.float32) * root_width
    xe = looked_up[:half_row]
    x = looked_up[half_row:]
    kept_enc = (xe, *project(xe, gains_full[0], weights["qkv", 0]))
    if fast:
        xe, kept_enc, x = step((xe, kept_enc, x), second)
    o, saved_enc = attend_forward(masks, False, *kept_enc[2:])
    if fast:
        o, fourth = step((o, fourth), second)
        fourth = lax.all_gather(fourth, PLANE + LINE).reshape(4, owners, *fourth.shape)
        settle(GATHERED[1], second.result)
    *kept_enc_feed, xe = feed(
        o, weights["out", 0], xe, gains_full[1], weights["up", 0], weights["down", 0]
    )
    final_gain = gains_full[2 * ENC]
    memory = low(normalize(xe, final_gain))
    kept = []
    states = []
    for layer_id in range(LAYERS):
        base = 2 * ENC + 1 + 4 * layer_id
        slot = ENC + 2 * layer_id
        if fast and layer_id == 0:
            (x, memory), third = hold((x, memory), third)
            settle(GATHERED[2], unpack(third, *layout(GATHERED[2]), unit, owners))
        if fast and layer_id == 1:
            x, fourth = hold(x, fourth)
            settle(GATHERED[3], unpack(fourth, *layout(GATHERED[3]), unit, owners))
        cross = weights["qkv", slot + 1]
        pair = jnp.stack([low(product(memory, cross[1])), low(product(memory, cross[2]))])
        kept_self = (x, *project(x, gains_full[base], weights["qkv", slot]))
        o, saved_self = attend_forward(masks, True, *kept_self[2:])
        *kept_cross, q = between(o, weights["out", slot], x, gains_full[base + 1], cross)
        o, saved_cross = attend_forward(masks, False, q, pair)
        feed_at = ENC + layer_id
        *kept_feed, x = feed(
            o,
            weights["out", slot + 1],
            kept_cross[0],
            gains_full[base + 2],
            weights["up", feed_at],
            weights["down", feed_at],
        )
        kept.append((kept_self, saved_self, kept_cross, saved_cross, kept_feed))
        states.append(x)

    pick = (places[:, None] == jnp.arange(half_row)[None, :]).astype(jnp.bfloat16)
    exit_gains = [gains_full[2 * ENC + 4 + 4 * layer_id] for layer_id in range(LAYERS)]
    exits = jnp.concatenate(
        [low(product(pick, low(normalize(states[i], exit_gains[i])))) for i in range(LAYERS)]
    )
    logits = against_rows(exits, table) * LOGIT_SCALE
    wanted_all = jnp.concatenate([wanted] * LAYERS)
    hit = jnp.arange(vocabulary)[None, :] == wanted_all[:, None]
    picked = jnp.sum(jnp.where(hit, logits, 0.0), axis=-1)
    top = jnp.max(logits, axis=-1)
    lse = top + jnp.log(jnp.sum(jnp.exp(logits - top[:, None]), axis=-1))
    shares = jnp.concatenate(
        [(depth >= i).astype(jnp.float32) / reach[i] / MICRO for i in range(LAYERS)]
    )
    loss_part = jnp.sum((lse - picked) * shares)
    grad_logits = low(
        (jnp.exp(logits - lse[:, None]) - hit.astype(jnp.float32))
        * shares[:, None]
        * LOGIT_SCALE
    )
    grad_exits = product(grad_logits, table)
    table_grad = outer_sum(grad_logits, exits)

    grads = {}
    gain_parts = [None] * gain_count
    grad_x = None
    grad_memory = None
    for layer_id in reversed(range(LAYERS)):
        slot = ENC + 2 * layer_id
        base = 2 * ENC + 1 + 4 * layer_id
        count = places.shape[0]
        grad_rows = lax.dot_general(
            wide(pick),
            grad_exits[layer_id * count : (layer_id + 1) * count],
            (((0,), (0,)), ((), ())),
            precision=lax.Precision.HIGHEST,
            preferred_element_type=jnp.float32,
        )
        grad_here, gain_parts[base + 3] = norm_back(
            states[layer_id], exit_gains[layer_id], grad_rows
        )
        grad_x = grad_here if grad_x is None else grad_x + grad_here
        kept_self, saved_self, kept_cross, saved_cross, kept_feed = kept[layer_id]
        up, down = ("up", ENC + layer_id), ("down", ENC + layer_id)
        qkv, out = ("qkv", slot + 1), ("out", slot + 1)
        grads[up], grads[down], grad_x, gain_parts[base + 2], grad_o, grads[out] = feed_back(
            grad_x,
            kept_feed,
            gains_full[base + 2],
            weights[up],
            weights[down],
            saved_cross[3],
            weights[out],
        )
        if fast and layer_id == 1:
            feed_mover = reduce(REDUCED[0], long_reduce_stages)
            grad_x, grad_o = step((grad_x, grad_o), feed_mover, feed_mover)
        if fast and layer_id == 0:
            late = reduce(REDUCED[1], long_reduce_stages)
            grad_x, grad_o = step((grad_x, grad_o), feed_mover, late, late)
        grad_q, own, other = attend_backward(saved_cross, masks, False, grad_o)
        grad_pair, more = memory_back(own, other, memory, weights[qkv])
        grad_memory = more if grad_memory is None else grad_memory + more
        out = ("out", slot)
        grad_query, grad_x, gain_parts[base + 1], grad_o, grads[out] = between_back(
            grad_q,
            kept_cross[1],
            kept_cross[0],
            gains_full[base + 1],
            weights[qkv],
            grad_x,
            saved_self[3],
            weights[out],
        )
        grads[qkv] = (grad_query, grad_pair)
        grad_q, own, other = attend_backward(saved_self, masks, True, grad_o)
        qkv = ("qkv", slot)
        grads[qkv], grad_x, gain_parts[base] = project_back(
            grad_q,
            own,
            other,
            kept_self[1],
            kept_self[0],
            gains_full[base],
            weights[qkv],
            grad_x,
        )
    if fast:
        middle = reduce(REDUCED[2], long_reduce_stages)
        grad_x, grad_memory = step((grad_x, grad_memory), middle, middle)
    grad_enc, gain_parts[2 * ENC] = norm_back(xe, final_gain, grad_memory)
    up, down, qkv, out = ("up", 0), ("down", 0), ("qkv", 0), ("out", 0)
    grads[up], grads[down], grad_enc, gain_parts[1], grad_o, grads[out] = feed_back(
        grad_enc,
        kept_enc_feed,
        gains_full[1],
        weights[up],
        weights[down],
        saved_enc[3],
        weights[out],
    )
    if fast:
        early = reduce(REDUCED[3])
        grad_enc, grad_o = step((grad_enc, grad_o), feed_mover, early)
    grad_q, own, other = attend_backward(saved_enc, masks, False, grad_o)
    if fast:
        grad_q, own, grad_enc = step((grad_q, own, grad_enc), late, early)
    grads[qkv], grad_enc, gain_parts[0] = project_back(
        grad_q, own, other, kept_enc[1], kept_enc[0], gains_full[0], weights[qkv], grad_enc
    )
    token_ids = jnp.concatenate([source_ids, target_ids])
    token_grads = low(jnp.concatenate([grad_enc, grad_x]) * root_width)
    looked = (token_ids[:, None] == jnp.arange(vocabulary)[None, :]).astype(jnp.bfloat16)
    table_grad = low(table_grad + outer_sum(looked, token_grads))
    grads["table", 0] = table_grad

    reduced = {}
    gain_grad = jnp.concatenate([part.reshape(1, -1) for part in gain_parts])
    small = jnp.concatenate([gain_grad, jnp.full((1, width), loss_part)])
    if fast:
        last = reduce(REDUCED[4])
        small = step(small, last, early)
        small = step(small, last, early)
        small = all_sum(small)
        small = step(small, last, early, late, middle)
        small = step(small, last, early)
        movers = (feed_mover, late, middle, early, last)
        squares = sum(mover.squares for mover in movers[:4])
        squares = step(squares, last)
        squares = all_sum(squares + last.squares)
        squares = step(squares, middle, last)
    else:
        small = all_sum(small)
        squares = all_sum(sum(reduce_plainly(entries) for entries in REDUCED))
    loss_total = small[-1, 0]
    gain_grad = small[:-1]
    squares = squares + jnp.sum(gain_grad * gain_grad)
    grad_norm = jnp.sqrt(squares)
    clip_factor = CLIP_NORM / jnp.maximum(grad_norm, CLIP_NORM)

    names = ("qkv", "out", "up", "down", "table")
    if fast:
        plan = []
        for bucket, entries in enumerate(REDUCED):
            first = 0
            for (name, i, kind), count in zip(entries, layout(entries)[1]):
                plan.append((bucket, first, count, kind, names.index(name), i))
                first += count
        parts = [part for mover in movers for part in mover.result]
        shapes = [shard_of[name].shape for name in names]
        placed = pl.pallas_call(
            functools.partial(settle_kernel, len(parts), tuple(plan), unit),
            out_shape=[jax.ShapeDtypeStruct(shape, jnp.bfloat16) for shape in shapes],
            in_specs=[SCALAR] + [ANY] * len(parts),
            out_specs=[ONCHIP] * len(shapes),
            scratch_shapes=[pltpu.SemaphoreType.DMA((len(shapes),))],
            cost_estimate=LIGHT,
            name="place_gradients",
        )(me, *parts)
        ready = [wide(array) for array in placed]
    else:
        ready = [
            wide(jnp.stack([reduced[name, i] for i in range(shard_of[name].shape[0])]))
            for name in names
        ]
    gradients = (
        *ready[:4],
        lax.dynamic_slice_in_dim(gain_grad, (2 * z + c) * gain_dev, gain_dev, 1),
        ready[4][0],
    )
    masters = (qkv_weight, out_weight, up_weight, down_weight, norm_gains, embed_table)
    firsts = (qkv_first, out_first, up_first, down_first, gains_first, table_first)
    seconds = (qkv_second, out_second, up_second, down_second, gains_second, table_second)
    results = [
        adam_update(masters[i], firsts[i], seconds[i], gradients[i] * clip_factor) for i in range(6)
    ]
    gains_grad = gradients[4] * clip_factor
    return (
        loss_total,
        grad_norm,
        results[0][0],
        results[1][0],
        results[2][0],
        results[3][0],
        gains_grad,
        results[5][0],
        results[0][1],
        results[1][1],
        results[2][1],
        results[3][1],
        results[4][1],
        results[5][1],
        results[0][2],
        results[1][2],
        results[2][2],
        results[3][2],
        results[4][2],
        results[5][2],
    )


def solution(mesh):
    seq, vocab = mesh.devices.shape
    fine = Mesh(mesh.devices.reshape(2, seq // 2, vocab // 2, 2), ("sy", "sx", "z", "c"))
    ints = P(None, LINE, PLANE)
    block = P(None, LINE, None)
    gains = P(None, LINE)
    rows = P(LINE, None)
    arrays = (block, block, block, block, gains, rows)
    return jax.shard_map(
        shards,
        mesh=fine,
        in_specs=(ints,) * 6 + arrays * 3,
        out_specs=(P(), P(), block, block, block, block, gains, rows) + arrays * 2,
        check_vma=False,
    )
```

```python
import functools
import math

import jax
import jax.numpy as jnp
from jax import lax
from jax.experimental import pallas as pl
from jax.experimental.pallas import tpu as pltpu
from jax.sharding import Mesh
from jax.sharding import PartitionSpec as P

HEADS = 8
HEAD = 64
ENC = 1
LAYERS = 2
MICRO = 2
COL = 512
HALF, FULL = jnp.bfloat16, jnp.float32

NORM_EPS = 1e-06
CLIP_NORM = 0.01
LEARN_RATE = 0.05
BETA_ONE = 0.9
BETA_TWO = 0.999
ADAM_EPS = 1e-08
WEIGHT_DECAY = 0.01
ADAM_STEP = 10
LOGIT_SCALE = 4.0
NEGATIVE = -1e30

PLANE = ("sy", "sx")
LINE = ("z", "c")

TABLE = ("table", 0, "blk")


def attention_parts(i):
    return (("qkv", i, "row"), ("out", i, "row"))


def feed_parts(i):
    return (("up", i, "row"), ("down", i, "blk"))


GATHERED = (
    (TABLE,) + attention_parts(0),
    feed_parts(0),
    attention_parts(1) + attention_parts(2) + feed_parts(1),
    attention_parts(3) + attention_parts(4) + feed_parts(2),
)
REDUCED = (
    feed_parts(2),
    attention_parts(3) + attention_parts(4) + feed_parts(1),
    attention_parts(1) + attention_parts(2) + feed_parts(0),
    (TABLE,) + attention_parts(0) + (("gains", 0, "row"),),
)


def flip(x, axis, bit=1):
    if isinstance(axis, tuple):
        n = math.prod(lax.axis_size(a) for a in axis)
    else:
        n = lax.axis_size(axis)
    return lax.ppermute(x, axis, [(i, i ^ bit) for i in range(n)])


def bits(axis):
    n = lax.axis_size(axis)
    return [1 << k for k in range(n.bit_length() - 1)]


def gathered(x, axis):
    if isinstance(axis, tuple) or lax.axis_size(axis) <= 4:
        n = 4 if isinstance(axis, tuple) else lax.axis_size(axis)
        return jnp.stack([x] + [flip(x, axis, r) for r in range(1, n)])
    x = x[None]
    for bit in bits(axis):
        x = jnp.concatenate([x, flip(x, axis, bit)], axis=0)
    return x


def in_order(blocks, index):
    n = blocks.shape[0]
    return jnp.concatenate(
        [lax.dynamic_index_in_dim(blocks, i ^ index, 0, keepdims=True) for i in range(n)]
    )


def all_sum(x):
    for axis in ("c", "sx", "sy", "z"):
        for bit in bits(axis):
            x = x + flip(x, axis, bit)
    return x


def hold(carry, things):
    return lax.optimization_barrier((carry, things))


def step(carry, *movers):
    for mover in movers:
        carry, (mover.held, mover.arrived) = hold(carry, (mover.held, mover.arrived))
        leaving = next(mover.stages)
        carry, (arrays, mover.held) = hold(carry, ([array for array, _ in leaving], mover.held))
        mover.arrived = [
            flip(array, *route)
            if route
            else lax.psum_scatter(array, PLANE + ("z",), scatter_dimension=0, tiled=True)
            for array, (_, route) in zip(arrays, leaving)
        ]
    return carry


class Mover:
    def __init__(self):
        self.held = []
        self.arrived = []


def normalize(v, g):
    return v * lax.rsqrt(jnp.mean(v * v, axis=-1, keepdims=True) + NORM_EPS) * g


def norm_back(v, g, cotangent):
    _, pullback = jax.vjp(normalize, v, g)
    return pullback(cotangent)


def product(a, b):
    return jnp.dot(a, b, preferred_element_type=jnp.float32)


def outer_sum(a, b):
    return lax.dot_general(a, b, (((0,), (0,)), ((), ())), preferred_element_type=jnp.float32)


def against_rows(a, b):
    return lax.dot_general(a, b, (((1,), (1,)), ((), ())), preferred_element_type=jnp.float32)


def split_heads(v):
    return v.reshape(v.shape[0], HEADS, HEAD)


def low(v):
    return v.astype(jnp.bfloat16)


def wide(v):
    return v.astype(jnp.float32)


def adam_update(master, first, second, grad):
    first = BETA_ONE * first + (1.0 - BETA_ONE) * grad
    second = BETA_TWO * second + (1.0 - BETA_TWO) * grad * grad
    fixed_first = first / (1.0 - BETA_ONE**ADAM_STEP)
    fixed_second = second / (1.0 - BETA_TWO**ADAM_STEP)
    master = master - LEARN_RATE * (
        fixed_first / (jnp.sqrt(fixed_second) + ADAM_EPS) + WEIGHT_DECAY * master
    )
    return (master, first, second)


def owned_blocks(array, kind, unit):
    if kind == "row":
        rows, columns = array.shape
        return array.reshape(rows, columns // COL, COL).transpose(1, 0, 2)
    rows = array.shape[0]
    per = rows // (4 * unit)
    return array.reshape(4, per, unit, COL).transpose(1, 0, 2, 3).reshape(per, 4 * unit, COL)


def quarter_blocks(array, kind, unit, s):
    size = array.shape[0] // 4
    array = lax.dynamic_slice_in_dim(array, s * size, size, axis=0)
    if kind == "row":
        return low(array).reshape(unit, -1, COL).transpose(1, 0, 2)
    return low(array).reshape(-1, unit, COL)


def block_counts(entries, shard_shapes, unit):
    counts = []
    for name, _, kind in entries:
        rows, columns = shard_shapes[name]
        counts.append(columns // COL if kind == "row" else rows // (4 * unit))
    return counts


def natural_shape(kind, count, unit, owners):
    if kind == "row":
        return (count, owners * 4 * unit, COL)
    return (owners, 4, count, unit, COL)


def scatter_kernel(plan, unit, me_ref, *refs):
    pieces, outs, sem = refs[:10], refs[10:-1], refs[-1]
    c, z, s = me_ref[0], me_ref[1], me_ref[2]

    def put(out, kind, owner, part, rows, source):
        if kind == "row":
            start = pl.multiple_of(owner * (4 * unit) + part * unit, unit)
            target = outs[out].at[:, pl.ds(start, rows), :]
        else:
            target = outs[out].at[owner, part]
        pltpu.make_async_copy(source, target, sem.at[out]).start()

    for c_rel in range(2):
        shard, *quarters = pieces[5 * c_rel : 5 * c_rel + 5]
        for z_rel in range(4):
            owner = (z ^ z_rel) * 2 + (c ^ c_rel)
            for out, (kind, first, count) in enumerate(plan):
                last = first + count
                if z_rel == 0:
                    if kind == "row":
                        put(out, kind, owner, 0, 4 * unit, shard.at[first:last])
                    else:
                        for part in range(4):
                            rows = pl.ds(part * unit, unit)
                            put(out, kind, owner, part, unit, shard.at[first:last, rows, :])
                else:
                    for s_rel, quarter in enumerate(quarters):
                        put(out, kind, owner, s ^ s_rel, unit, quarter.at[z_rel - 1, first:last])
    for out in range(len(plan)):
        pltpu.make_async_copy(outs[out], outs[out], sem.at[out]).wait()


def collect_kernel(plan, unit, ordered, me_ref, *refs):
    grads, keep, send, sem = refs[: len(plan)], refs[len(plan)], refs[len(plan) + 1], refs[-1]
    c, z, s = me_ref[0], me_ref[1], me_ref[2]
    for c_rel, out in ((0, keep), (1, send)):
        for z_rel in range(4):
            owner = (z ^ z_rel) * 2 + (c ^ c_rel)
            for s_rel in range(4):
                part = s ^ s_rel
                for grad, (kind, first, count) in zip(grads, plan):
                    if kind == "row":
                        start = pl.multiple_of(owner * (4 * unit) + part * unit, unit)
                        source = grad.at[:, pl.ds(start, unit), :]
                    else:
                        source = grad.at[owner, part]
                    place = (part, z ^ z_rel) if ordered else (s_rel, z_rel)
                    target = out.at[*place, first : first + count]
                    pltpu.make_async_copy(source, target, sem.at[c_rel]).start()
    for c_rel, out in ((0, keep), (1, send)):
        pltpu.make_async_copy(out, out, sem.at[c_rel]).wait()


LIGHT = pl.CostEstimate(flops=1, bytes_accessed=1, transcendentals=0)
ANY = pl.BlockSpec(memory_space=pl.ANY)
ONCHIP = pl.BlockSpec(memory_space=pltpu.VMEM)
SCALAR = pl.BlockSpec(memory_space=pltpu.SMEM)


def gather_stages(mover, me, shard, kinds, counts, unit, owners):
    starts = [sum(counts[:i]) for i in range(len(counts))]
    mover.held = [shard]
    part = lax.dynamic_slice_in_dim(shard, me[2] * unit, unit, axis=1)
    yield [(part, ("z", bit)) for bit in (1, 2, 3)]
    mine = jnp.stack(mover.arrived)
    mover.held.append(mine)
    yield [(mine, (PLANE, bit)) for bit in (1, 2, 3)]
    mover.held += mover.arrived
    yield [(piece, ("c",)) for piece in mover.held]
    plan = tuple(zip(kinds, starts, counts))
    mover.result = pl.pallas_call(
        functools.partial(scatter_kernel, plan, unit),
        out_shape=[
            jax.ShapeDtypeStruct(natural_shape(kind, count, unit, owners), jnp.bfloat16)
            for kind, count in zip(kinds, counts)
        ],
        in_specs=[SCALAR] + [ANY] * 10,
        out_specs=[ONCHIP] * len(plan),
        scratch_shapes=[pltpu.SemaphoreType.DMA((len(plan),))],
        cost_estimate=LIGHT,
        name="place_weights",
    )(me, *mover.held, *mover.arrived)
    mover.held = []
    yield []


def unpack_kernel(plan, pieces, *refs):
    outs, sem = refs[:-1], refs[-1]
    for out, (kind, first, count) in enumerate(plan):
        for part in range(4):
            if kind == "blk":
                source = pieces.at[part, :, first : first + count]
                pltpu.make_async_copy(source, outs[out].at[:, part], sem.at[out]).start()
                continue
            for k in range(count):
                source = pieces.at[part, :, first + k]
                pltpu.make_async_copy(source, outs[out].at[k, :, part], sem.at[out]).start()
    for out in range(len(plan)):
        pltpu.make_async_copy(outs[out], outs[out], sem.at[out]).wait()


def unpack(pieces, kinds, counts, unit, owners):
    starts = [sum(counts[:i]) for i in range(len(counts))]
    shapes = [
        (count, owners, 4, unit, COL) if kind == "row" else (owners, 4, count, unit, COL)
        for kind, count in zip(kinds, counts)
    ]
    placed = pl.pallas_call(
        functools.partial(unpack_kernel, tuple(zip(kinds, starts, counts))),
        out_shape=[jax.ShapeDtypeStruct(shape, jnp.bfloat16) for shape in shapes],
        in_specs=[ANY],
        out_specs=[ONCHIP] * len(shapes),
        scratch_shapes=[pltpu.SemaphoreType.DMA((len(shapes),))],
        cost_estimate=LIGHT,
        name="place_gathered",
    )(pieces)
    return [
        out.reshape(count, -1, COL) if kind == "row" else out
        for out, kind, count in zip(placed, kinds, counts)
    ]


def added(arrays):
    total = wide(arrays[0])
    for array in arrays[1:]:
        total = total + wide(array)
    return total


def plane_sum_kernel(keep, core, from_x, from_y, left, right, own, *sends):
    half = left.shape[1]
    for bit in range(4):
        for part, (one, two) in ((slice(0, half), (from_x, left)), (slice(half, None), (from_y, right))):
            total = added([keep[bit, part], core[bit, part], one[bit], two[bit]])
            if bit == 0:
                own[part] = total
            else:
                sends[bit - 1][part] = low(total)


def line_sum_kernel(own, one, two, three, whole, squares):
    total = added([own[...], one[...], two[...], three[...]])
    whole[...] = low(total)
    squares[0, 0] = jnp.sum(total * total)


def collect(me, grads, kinds, counts, unit, ordered):
    starts = [sum(counts[:i]) for i in range(len(counts))]
    plan = tuple(zip(kinds, starts, counts))
    shape = jax.ShapeDtypeStruct((4, 4, sum(counts), unit, COL), jnp.bfloat16)
    return pl.pallas_call(
        functools.partial(collect_kernel, plan, unit, ordered),
        out_shape=[shape, shape],
        in_specs=[SCALAR] + [ANY] * len(plan),
        out_specs=[ONCHIP, ONCHIP],
        scratch_shapes=[pltpu.SemaphoreType.DMA((2,))],
        cost_estimate=LIGHT,
        name="collect_gradients",
    )(me, *grads)


def long_reduce_stages(mover, me, grads, kinds, counts, unit):
    keep, send = collect(me, grads, kinds, counts, unit, True)
    mover.held = [keep]
    yield [(send, ("c",))]
    chip = low(added(mover.held + mover.arrived))
    mover.held = []
    yield [(chip.reshape(16, *chip.shape[2:]), None)]
    own = mover.arrived[0][0]
    mover.squares = jnp.sum(wide(own) * wide(own))
    mover.held = [own]
    yield [(own, (PLANE, bit)) for bit in (1, 2, 3)]
    mover.result = mover.held + mover.arrived
    mover.held = []
    yield []


def reduce_stages(mover, me, grads, kinds, counts, unit):
    total = sum(counts)
    keep, send = collect(me, grads, kinds, counts, unit, False)
    mover.held = [keep]
    half = total // 2
    yield [(send, ("c",))]
    mover.held = [a.reshape(2, 2, *a.shape[1:]) for a in mover.held + mover.arrived]
    yield [
        (low(added([a[:, 1, :, :half] for a in mover.held])), ("sx",)),
        (low(added([a[1, :, :, half:] for a in mover.held])), ("sy",)),
    ]
    mover.held += mover.arrived

    def sides():
        both, (come_x, come_y) = mover.held[:2], mover.held[2:4]
        return (
            [a[:, 0, :, :half] for a in both] + [come_x],
            [a[0, :, :, half:] for a in both] + [come_y],
        )

    left, right = sides()
    yield [(low(added([a[1] for a in left])), ("sy",)), (low(added([a[1] for a in right])), ("sx",))]
    mover.held += mover.arrived

    block = (total, unit, COL)
    first_part = pl.BlockSpec((None, None, 4, *block), lambda i: (0, 0, 0, 0, 0, 0))
    half_part = [pl.BlockSpec((None, 4, n, unit, COL), lambda i: (0, 0, 0, 0, 0)) for n in (half, total - half)]
    own, *sends = pl.pallas_call(
        plane_sum_kernel,
        grid=(1,),
        out_shape=[jax.ShapeDtypeStruct(block, FULL)] + [jax.ShapeDtypeStruct(block, HALF)] * 3,
        in_specs=[first_part, first_part, *half_part, ONCHIP, ONCHIP],
        out_specs=[ONCHIP] * 4,
        cost_estimate=LIGHT,
        name="plane_sum",
    )(*mover.held)
    mover.held = [own]
    yield [(send, ("z", bit)) for bit, send in zip((1, 2, 3), sends)]
    own, squares = pl.pallas_call(
        line_sum_kernel,
        out_shape=[
            jax.ShapeDtypeStruct(block, HALF),
            jax.ShapeDtypeStruct((1, 1), FULL),
        ],
        in_specs=[ONCHIP] * 4,
        out_specs=[ONCHIP, SCALAR],
        cost_estimate=LIGHT,
        name="line_sum",
    )(*mover.held, *mover.arrived)
    mover.squares = squares[0, 0]
    mover.held = [own]
    yield [(own, (PLANE, bit)) for bit in (1, 2, 3)]
    mover.result = mover.held + mover.arrived
    mover.held = []
    yield []


def settle_kernel(sizes, plan, unit, me_ref, *refs):
    buckets, outs, sem = refs[:sizes], refs[sizes:-1], refs[-1]
    s = me_ref[2]
    for bucket, first, count, kind, out, i in plan:
        for s_rel in range(4):
            source = buckets[4 * bucket + s_rel]
            part = s ^ s_rel
            if kind == "blk":
                for k in range(count):
                    start = pl.multiple_of((part * count + k) * unit, unit)
                    target = outs[out].at[i, pl.ds(start, unit), :]
                    pltpu.make_async_copy(source.at[first + k], target, sem.at[out]).start()
                continue
            rows = pl.ds(pl.multiple_of(part * unit, unit), unit)
            for k in range(count):
                target = outs[out].at[i, rows, k * COL : k * COL + COL]
                pltpu.make_async_copy(source.at[first + k], target, sem.at[out]).start()
    for out, ref in enumerate(outs):
        pltpu.make_async_copy(ref, ref, sem.at[out]).wait()


def owned_natural(parts, kind):
    if kind == "row":
        four, count, unit, _ = parts.shape
        return parts.transpose(0, 2, 1, 3).reshape(four * unit, count * COL)
    return parts.reshape(-1, COL)


BQ = 128
CK = 256
CF = 256
NT = (((1,), (1,)), ((), ()))
TN = (((0,), (0,)), ((), ()))
NN = (((1,), (0,)), ((), ()))


def dot32(a, b, dims):
    return lax.dot_general(a, b, dims, preferred_element_type=jnp.float32)


def load_halves(own, other, whole, sem):
    half = whole.shape[0] // 2
    copies = [
        pltpu.make_async_copy(own, whole.at[pl.ds(0, half)], sem.at[0]),
        pltpu.make_async_copy(other, whole.at[pl.ds(half, half)], sem.at[1]),
    ]
    for copy in copies:
        copy.start()
    return copies


def pair_rows(block, scale=None):
    lane = lax.broadcasted_iota(jnp.int32, block.shape, 1)
    zero = jnp.zeros_like(block)
    if scale is not None:
        block = block * jnp.asarray(scale, block.dtype)
    return jnp.concatenate(
        [jnp.where(lane < HEAD, block, zero), jnp.where(lane < HEAD, zero, block)], axis=0
    )


def pair_lanes(stacked):
    rows = stacked.shape[0] // 2
    lane = lax.broadcasted_iota(jnp.int32, (rows, 2 * HEAD), 1)
    return jnp.where(lane < HEAD, stacked[:rows], stacked[rows:])


def open_to(act, bounds, rows, j, chunks):
    half = chunks // 2
    base = jnp.where(j < half, act[0] + j * CK, act[1] + (j - half) * CK)
    spot = base + lax.broadcasted_iota(jnp.int32, (CK, BQ), 0)
    open_ = (spot >= bounds[0:1, rows]) & (spot <= bounds[1:2, rows])
    return jnp.concatenate([open_, open_], axis=1)


def attend_kernel(
    act, bounds, q, kv_own, kv_oth, o, lse,
    k_all, v_all, scores, queries, top, total, acc, sem_k, sem_v,
):
    pairs = q.shape[1] // (2 * HEAD)
    blocks = q.shape[0] // BQ
    chunks = k_all.shape[0] // CF
    half = chunks // 2
    waits = load_halves(kv_own.at[0], kv_oth.at[0], k_all, sem_k)
    waits += load_halves(kv_own.at[1], kv_oth.at[1], v_all, sem_v)
    for copy in waits:
        copy.wait()
    square = lax.broadcasted_iota(jnp.int32, (BQ, BQ), 0)
    along = lax.broadcasted_iota(jnp.int32, (BQ, BQ), 1)

    def one_block(b, _):
        rows = pl.ds(pl.multiple_of(b * BQ, BQ), BQ)
        for h in range(pairs):
            queries[h] = pair_rows(q[rows, h * 128 : h * 128 + 128], HEAD ** (-0.5))
        top[...] = jnp.full_like(top, NEGATIVE)
        total[...] = jnp.zeros_like(total)
        acc[...] = jnp.zeros_like(acc)
        least = jnp.broadcast_to(bounds[0:1, rows], (BQ, BQ)).T
        most = jnp.broadcast_to(bounds[1:2, rows], (BQ, BQ)).T

        def first(j, _):
            @pl.when(act[2 + b * chunks + j] > 0)
            def _():
                keys = pl.ds(pl.multiple_of(j * CF, CF), CF)
                base = jnp.where(j < half, act[0] + j * CF, act[1] + (j - half) * CF)
                open_ = []
                for part in range(CF // 128):
                    spot = base + part * 128 + along
                    one = (spot >= least) & (spot <= most)
                    open_.append(jnp.concatenate([one, one], axis=0))
                for h in range(pairs):
                    s = dot32(queries[h], k_all[keys, h * 128 : h * 128 + 128], NT)
                    best = top[h]
                    for part, one in enumerate(open_):
                        t = jnp.where(one, s[:, part * 128 : part * 128 + 128], NEGATIVE)
                        scores[h, j, :, part * 128 : part * 128 + 128] = t
                        best = jnp.maximum(best, t)
                    top[h] = best

            return 0

        lax.fori_loop(0, chunks, first, 0)
        for h in range(pairs):
            top[h] = jnp.broadcast_to(jnp.max(top[h], axis=1, keepdims=True), top.shape[1:])

        def second(j, _):
            @pl.when(act[2 + b * chunks + j] > 0)
            def _():
                keys = pl.ds(pl.multiple_of(j * CF, CF), CF)
                for h in range(pairs):
                    parts = []
                    more = total[h]
                    for part in range(CF // 128):
                        e = jnp.exp(scores[h, j, :, part * 128 : part * 128 + 128] - top[h])
                        more = more + e
                        parts.append(e.astype(jnp.bfloat16))
                    total[h] = more
                    e = parts[0] if len(parts) == 1 else jnp.concatenate(parts, axis=1)
                    acc[h] = acc[h] + dot32(e, v_all[keys, h * 128 : h * 128 + 128], NN)

            return 0

        lax.fori_loop(0, chunks, second, 0)
        for h in range(pairs):
            denom = jnp.broadcast_to(
                jnp.sum(total[h], axis=1, keepdims=True), total.shape[1:]
            )
            o[rows, h * 128 : h * 128 + 128] = pair_lanes(acc[h] / denom).astype(o.dtype)
            level = top[h] + jnp.log(denom)
            for part in range(2):
                own = jnp.where(square == along, level[part * BQ : part * BQ + BQ], 0.0)
                lse[b, h, :, part * BQ : part * BQ + BQ] = jnp.sum(own, axis=0, keepdims=True)
        return 0

    lax.fori_loop(0, blocks, one_block, 0)


def attend_back_kernel(
    act, bounds, q, kv_own, kv_oth, o, lse, grad,
    grad_q, grad_own, grad_oth,
    k_all, v_all, k_turned, queries, grads, delta, grad_queries, sem_k, sem_v,
):
    pairs = q.shape[1] // (2 * HEAD)
    blocks = q.shape[0] // BQ
    chunks = k_all.shape[0] // CK
    waits = load_halves(kv_own.at[0], kv_oth.at[0], k_all, sem_k)
    waits += load_halves(kv_own.at[1], kv_oth.at[1], v_all, sem_v)
    grad_own[...] = jnp.zeros_like(grad_own)
    grad_oth[...] = jnp.zeros_like(grad_oth)
    for copy in waits:
        copy.wait()

    def turn(j, _):
        for h in range(pairs):
            for part in range(CK // 128):
                keys = pl.ds(pl.multiple_of(j * CK + part * 128, 128), 128)
                k_turned[j, h, :, part * 128 : part * 128 + 128] = k_all[
                    keys, h * 128 : h * 128 + 128
                ].T
        return 0

    lax.fori_loop(0, chunks, turn, 0)

    def one_block(b, _):
        rows = pl.ds(pl.multiple_of(b * BQ, BQ), BQ)
        for h in range(pairs):
            lanes = slice(h * 128, h * 128 + 128)
            queries[h] = pair_rows(q[rows, lanes], HEAD ** (-0.5))
            grads[h] = pair_rows(grad[rows, lanes])
            both = (o[rows, lanes].astype(jnp.float32) * grad[rows, lanes].astype(jnp.float32)).T
            delta[h] = jnp.concatenate(
                [
                    jnp.sum(both[:HEAD], axis=0, keepdims=True),
                    jnp.sum(both[HEAD:], axis=0, keepdims=True),
                ],
                axis=1,
            )
        grad_queries[...] = jnp.zeros_like(grad_queries)

        def one_chunk(j, target, local):
            keys = pl.ds(pl.multiple_of(j * CK, CK), CK)
            own_keys = pl.ds(pl.multiple_of(local * CK, CK), CK)
            open_ = open_to(act, bounds, rows, j, chunks)
            for h in range(pairs):
                lanes = slice(h * 128, h * 128 + 128)
                s = jnp.where(open_, dot32(k_all[keys, lanes], queries[h], NT), NEGATIVE)
                p = jnp.exp(s - lse[b, h])
                ds = p * (dot32(v_all[keys, lanes], grads[h], NT) - delta[h])
                p = p.astype(jnp.bfloat16)
                ds = ds.astype(jnp.bfloat16)
                target[0, own_keys, lanes] += dot32(ds, queries[h], NN)
                target[1, own_keys, lanes] += dot32(p, grads[h], NN)
                grad_queries[h] += dot32(k_turned[j, h], ds, NN)

        def own_chunk(j, _):
            @pl.when(act[2 + b * chunks + j] > 0)
            def _():
                one_chunk(j, grad_own, j)

            return 0

        def oth_chunk(j, _):
            @pl.when(act[2 + b * chunks + j] > 0)
            def _():
                one_chunk(j, grad_oth, j - chunks // 2)

            return 0

        lax.fori_loop(0, chunks // 2, own_chunk, 0)
        lax.fori_loop(chunks // 2, chunks, oth_chunk, 0)
        for h in range(pairs):
            grad_q[rows, h * 128 : h * 128 + 128] = (
                pair_lanes(grad_queries[h].T) * HEAD ** (-0.5)
            ).astype(grad_q.dtype)
        return 0

    lax.fori_loop(0, blocks, one_block, 0)


def attend_masks(sentence, other, start, other_start):
    n = sentence.shape[0]
    seg = jnp.concatenate([sentence, other])
    spots = start + jnp.arange(n, dtype=jnp.int32)
    pos = jnp.concatenate([spots, other_start + jnp.arange(n, dtype=jnp.int32)])
    begin = jnp.sum((seg[None, :] < sentence[:, None]).astype(jnp.int32), axis=1)
    end = jnp.sum((seg[None, :] <= sentence[:, None]).astype(jnp.int32), axis=1) - 1
    made = {}
    for causal, last, size in ((c, l, k) for c, l in ((False, end), (True, spots)) for k in (CF, CK)):
        keys = pos.reshape(-1, size)
        live = (begin.reshape(-1, BQ).min(1)[:, None] <= keys.max(1)[None, :]) & (
            last.reshape(-1, BQ).max(1)[:, None] >= keys.min(1)[None, :]
        )
        starts = jnp.stack([start, other_start]).astype(jnp.int32)
        act = jnp.concatenate([starts, live.astype(jnp.int32).reshape(-1)])
        made[causal, size] = (act, jnp.pad(jnp.stack([begin, last]), ((0, 6), (0, 0))))
    return made


def attend(masks, causal, q, kv, kv_oth):
    n, width = q.shape
    pairs = width // (2 * HEAD)
    return pl.pallas_call(
        attend_kernel,
        out_shape=[
            jax.ShapeDtypeStruct((n, width), jnp.bfloat16),
            jax.ShapeDtypeStruct((n // BQ, pairs, 1, 2 * BQ), jnp.float32),
        ],
        in_specs=[SCALAR] + [ONCHIP] * 2 + [ANY] * 2,
        out_specs=[ONCHIP, ONCHIP],
        scratch_shapes=[
            pltpu.VMEM((2 * n, width), jnp.bfloat16),
            pltpu.VMEM((2 * n, width), jnp.bfloat16),
            pltpu.VMEM((pairs, 2 * n // CF, 2 * BQ, CF), jnp.float32),
            pltpu.VMEM((pairs, 2 * BQ, 128), jnp.bfloat16),
            pltpu.VMEM((pairs, 2 * BQ, 128), jnp.float32),
            pltpu.VMEM((pairs, 2 * BQ, 128), jnp.float32),
            pltpu.VMEM((pairs, 2 * BQ, 128), jnp.float32),
            pltpu.SemaphoreType.DMA((2,)),
            pltpu.SemaphoreType.DMA((2,)),
        ],
        cost_estimate=LIGHT,
        name="attend",
    )(*masks[causal, CF], q, kv, kv_oth)


def attend_back(masks, causal, q, kv, kv_oth, o, lse, grad):
    n, width = q.shape
    pairs = width // (2 * HEAD)
    chunks = 2 * n // CK
    return pl.pallas_call(
        attend_back_kernel,
        out_shape=[
            jax.ShapeDtypeStruct((n, width), jnp.bfloat16),
            jax.ShapeDtypeStruct((2, n, width), jnp.float32),
            jax.ShapeDtypeStruct((2, n, width), jnp.float32),
        ],
        in_specs=[SCALAR] + [ONCHIP] * 2 + [ANY] * 2 + [ONCHIP] * 3,
        out_specs=[ONCHIP] * 3,
        scratch_shapes=[
            pltpu.VMEM((2 * n, width), jnp.bfloat16),
            pltpu.VMEM((2 * n, width), jnp.bfloat16),
            pltpu.VMEM((chunks, pairs, 128, CK), jnp.bfloat16),
            pltpu.VMEM((pairs, 2 * BQ, 128), jnp.bfloat16),
            pltpu.VMEM((pairs, 2 * BQ, 128), jnp.bfloat16),
            pltpu.VMEM((pairs, 1, 2 * BQ), jnp.float32),
            pltpu.VMEM((pairs, 128, 2 * BQ), jnp.float32),
            pltpu.SemaphoreType.DMA((2,)),
            pltpu.SemaphoreType.DMA((2,)),
        ],
        cost_estimate=LIGHT,
        name="attend_back",
    )(*masks[causal, CK], q, kv, kv_oth, o, lse, grad)


def rms(v, gain):
    scale = lax.rsqrt(jnp.mean(v * v, axis=-1, keepdims=True) + NORM_EPS)
    return v * scale * gain


def rms_back(v, gain, grad):
    scale = lax.rsqrt(jnp.mean(v * v, axis=-1, keepdims=True) + NORM_EPS)
    scaled = grad * gain
    lean = jnp.mean(scaled * v, axis=-1, keepdims=True) * (scale * scale * scale)
    return scaled * scale - v * lean, jnp.sum(grad * v * scale, axis=0, keepdims=True)


def project_kernel(x, gain, w, normed, q, kv):
    a = low(rms(x[...], gain[...]))
    normed[...] = a
    q[...] = low(dot32(a, w[0], NN))
    kv[0] = low(dot32(a, w[1], NN))
    kv[1] = low(dot32(a, w[2], NN))


def between_kernel(o, w_out, x, gain, w, y, normed, q):
    state = x[...] + dot32(o[...], w_out[0], NN)
    y[...] = state
    c = low(rms(state, gain[...]))
    normed[...] = c
    q[...] = low(dot32(c, w[0], NN))


def feed_kernel(o, w_out, x, gain, w_up, w_down, y, normed, hidden, z):
    state = x[...] + dot32(o[...], w_out[0], NN)
    y[...] = state
    f = low(rms(state, gain[...]))
    normed[...] = f
    for i in range(w_up.shape[0]):
        r = low(jnp.maximum(dot32(f, w_up[i], NN), 0.0))
        hidden[i] = r
        state = state + dot32(r, w_down[i], NN)
    z[...] = state


def out_back(g, o, w_out, grad_o, grad_out):
    grad_o[...] = low(dot32(g, w_out[0], NT))
    grad_out[0] = low(dot32(o[...], g, TN))


def feed_back_kernel(
    grad, y, normed, hidden, gain, w_up, w_down, o, w_out,
    grad_up, grad_down, grad_y, grad_gain, grad_o, grad_out,
):
    g = low(grad[...])
    f = normed[...]
    back = jnp.zeros(grad.shape, jnp.float32)
    for i in range(w_up.shape[0]):
        r = hidden[i]
        grad_down[i] = low(dot32(r, g, TN))
        h = low(jnp.where(r > 0, dot32(g, w_down[i], NT), 0.0))
        grad_up[i] = low(dot32(f, h, TN))
        back = back + dot32(h, w_up[i], NT)
    more, grad_gain[...] = rms_back(y[...], gain[...], back)
    total = grad[...] + more
    grad_y[...] = total
    out_back(low(total), o, w_out, grad_o, grad_out)


def between_back_kernel(
    grad_q, normed, y, gain, w, grad, o, w_out,
    grad_w, grad_x, grad_gain, grad_o, grad_out,
):
    g = grad_q[...]
    grad_w[0] = low(dot32(normed[...], g, TN))
    more, grad_gain[...] = rms_back(y[...], gain[...], dot32(g, w[0], NT))
    total = grad[...] + more
    grad_x[...] = total
    out_back(low(total), o, w_out, grad_o, grad_out)


def memory_back_kernel(own, other, memory, w, grad_w, grad_memory):
    m = memory[...]
    total = None
    for i in range(2):
        g = low(own[i] + other[i])
        grad_w[i] = low(dot32(m, g, TN))
        part = dot32(g, w[i + 1], NT)
        total = part if total is None else total + part
    grad_memory[...] = total


def project_back_kernel(
    grad_q, own, other, normed, x, gain, w, grad,
    grad_w, grad_x, grad_gain,
):
    a = normed[...]
    back = None
    for i in range(3):
        g = grad_q[...] if i == 0 else low(own[i - 1] + other[i - 1])
        grad_w[i] = low(dot32(a, g, TN))
        part = dot32(g, w[i], NT)
        back = part if back is None else back + part
    more, grad_gain[...] = rms_back(x[...], gain[...], back)
    grad_x[...] = grad[...] + more


def on_chip(kernel, name, outs, *args):
    return pl.pallas_call(
        kernel,
        out_shape=[jax.ShapeDtypeStruct(shape, kind) for shape, kind in outs],
        in_specs=[ONCHIP] * len(args),
        out_specs=[ONCHIP] * len(outs),
        cost_estimate=LIGHT,
        name=name,
    )(*args)


def shaped(lead, like, kind):
    return (lead + like.shape, kind)


def attend_forward(masks, causal, q, kv):
    other = flip(kv, "c")
    o, lse = attend(masks, causal, q, kv, other)
    return o, (q, kv, other, o, lse)


def attend_backward(saved, masks, causal, grad):
    grad_q, own, other = attend_back(masks, causal, *saved, grad)
    return grad_q, own, flip(other, "c")


def project(x, gain, w):
    return on_chip(
        project_kernel,
        "project",
        [shaped((), x, HALF), shaped((), x, HALF), shaped((2,), x, HALF)],
        x, gain[None], w,
    )


def between(o, w_out, x, gain, w):
    return on_chip(
        between_kernel,
        "between",
        [shaped((), x, FULL), shaped((), x, HALF), shaped((), x, HALF)],
        o, w_out, x, gain[None], w,
    )


def feed(o, w_out, x, gain, w_up, w_down):
    return on_chip(
        feed_kernel,
        "feed",
        [
            shaped((), x, FULL),
            shaped((), x, HALF),
            shaped((w_up.shape[0],), x, HALF),
            shaped((), x, FULL),
        ],
        o, w_out, x, gain[None], w_up, w_down,
    )


def feed_back(grad, kept, gain, w_up, w_down, o, w_out):
    y, normed, hidden = kept
    return on_chip(
        feed_back_kernel,
        "feed_back",
        [
            (w_up.shape, HALF),
            (w_down.shape, HALF),
            shaped((), y, FULL),
            ((1, y.shape[1]), FULL),
            shaped((), y, HALF),
            (w_out.shape, HALF),
        ],
        grad, y, normed, hidden, gain[None], w_up, w_down, o, w_out,
    )


def between_back(grad_q, normed, y, gain, w, grad, o, w_out):
    return on_chip(
        between_back_kernel,
        "between_back",
        [
            (w_out.shape, HALF),
            shaped((), y, FULL),
            ((1, y.shape[1]), FULL),
            shaped((), y, HALF),
            (w_out.shape, HALF),
        ],
        grad_q, normed, y, gain[None], w, grad, o, w_out,
    )


def memory_back(own, other, memory, w):
    return on_chip(
        memory_back_kernel,
        "memory_back",
        [((2,) + w.shape[1:], HALF), shaped((), memory, FULL)],
        own, other, memory, w,
    )


def project_back(grad_q, own, other, normed, x, gain, w, grad):
    return on_chip(
        project_back_kernel,
        "project_back",
        [(w.shape, HALF), shaped((), x, FULL), ((1, x.shape[1]), FULL)],
        grad_q, own, other, normed, x, gain[None], w, grad,
    )


def shards(
    tokens,
    source,
    segments,
    loss_rows,
    targets,
    exit_depth,
    qkv_weight,
    out_weight,
    up_weight,
    down_weight,
    norm_gains,
    embed_table,
    qkv_first,
    out_first,
    up_first,
    down_first,
    gains_first,
    table_first,
    qkv_second,
    out_second,
    up_second,
    down_second,
    gains_second,
    table_second,
):
    sy, sx = lax.axis_index("sy"), lax.axis_index("sx")
    z, c = lax.axis_index("z"), lax.axis_index("c")
    s = sy * 2 + sx
    me = jnp.stack([c, z, s]).astype(jnp.int32)
    owners = lax.axis_size("z") * 2
    tok_dev = tokens.shape[2]
    loss_dev = targets.shape[2]
    voc_dev, width = embed_table.shape
    gain_count, gain_dev = norm_gains.shape
    vocabulary = voc_dev * owners
    root_width = math.sqrt(width)
    half_row = 2 * tok_dev
    unit = qkv_weight.shape[1] // 4
    fast = lax.axis_size("z") == 4 and unit % 16 == 0

    shard_of = {
        "table": embed_table[None],
        "qkv": qkv_weight,
        "out": out_weight,
        "up": up_weight,
        "down": down_weight,
    }
    shard_shapes = {name: array.shape[1:] for name, array in shard_of.items()}
    shard_shapes["gains"] = (gain_dev, COL)
    weights = {}

    def layout(entries):
        kinds = [kind for _, _, kind in entries]
        return kinds, block_counts(entries, shard_shapes, unit)

    def packed(entries):
        return jnp.concatenate(
            [owned_blocks(low(shard_of[name][i]), kind, unit) for name, i, kind in entries]
        )

    def gather(entries):
        mover = Mover()
        mover.stages = gather_stages(mover, me, packed(entries), *layout(entries), unit, owners)
        return mover

    def settle(entries, outs):
        for (name, i, kind), out in zip(entries, outs):
            weights[name, i] = out.reshape(-1, COL, COL) if kind == "blk" else out

    def gather_plainly(entries):
        everything = lax.all_gather(packed(entries), LINE)
        outs = []
        first = 0
        for kind, count in zip(*layout(entries)):
            piece = everything[:, first : first + count]
            first += count
            if kind == "row":
                outs.append(piece.transpose(1, 0, 2, 3).reshape(count, -1, COL))
            else:
                outs.append(piece.reshape(owners, count, 4, unit, COL).transpose(0, 2, 1, 3, 4))
        settle(entries, outs)

    def pieces(entries):
        arrays, kinds, counts = [], [], []
        for (name, i, kind), count in zip(entries, layout(entries)[1]):
            held = grads[name, i]
            for array in held if isinstance(held, tuple) else (held,):
                blocks = array.shape[0] if isinstance(held, tuple) else count
                arrays.append(array.reshape(natural_shape(kind, blocks, unit, owners)))
                kinds.append(kind)
                counts.append(blocks)
        return arrays, kinds, counts

    def reduce(entries, stages=reduce_stages):
        arrays, kinds, counts = pieces(entries)
        mover = Mover()
        mover.stages = stages(mover, me, arrays, kinds, counts, unit)
        return mover

    def take(entries, parts):
        first = 0
        for (name, i, kind), count in zip(entries, layout(entries)[1]):
            reduced[name, i] = owned_natural(parts[:, first : first + count], kind)
            first += count

    def reduce_plainly(entries):
        parts = []
        for array, kind, count in zip(*pieces(entries)):
            if kind == "row":
                array = array.reshape(count, owners, 4, unit, COL).transpose(1, 2, 0, 3, 4)
            parts.append(wide(array))
        total = jnp.concatenate(parts, axis=2)
        total = lax.psum_scatter(total, LINE, scatter_dimension=0, tiled=True)
        total = lax.psum(total, PLANE)[0]
        take(entries, total)
        return jnp.sum(total * total) / 4.0

    if fast:
        first = gather(GATHERED[0])
        ints = [tokens, source, segments, loss_rows, targets, exit_depth]
        ints, shard_of = step((ints, shard_of), first)
        tokens, source, segments, loss_rows, targets, exit_depth = ints
        second = gather(GATHERED[1])

        def gather_long(entries):
            return jnp.concatenate(
                [quarter_blocks(shard_of[name][i], kind, unit, s) for name, i, kind in entries]
            )

        third, fourth = gather_long(GATHERED[2]), gather_long(GATHERED[3])
    if not fast:
        for entries in GATHERED:
            gather_plainly(entries)

    numbers = jnp.concatenate(
        [array[:, 0] for array in (tokens, source, segments, loss_rows, targets, exit_depth)],
        axis=1,
    )
    plane = gathered(gathered(numbers, "c"), PLANE)
    depths_seen = plane[..., 3 * tok_dev + 2 * loss_dev :]
    reached = jnp.stack(
        [
            jnp.sum((depths_seen >= layer_id).astype(jnp.float32), axis=(0, 1, 3))
            for layer_id in range(LAYERS)
        ],
        axis=1,
    )
    gains_now = norm_gains
    if fast:
        reached, gains_now, third = step((reached, gains_now, third), first)
        third = lax.all_gather(third, PLANE + LINE).reshape(4, owners, *third.shape)
        reached, gains_now = step((reached, gains_now), second)
    small = jnp.concatenate([gains_now.reshape(-1), reached.reshape(-1)])
    small = gathered(gathered(small, "c"), "z").reshape(owners, -1)
    reach = jnp.maximum(
        jnp.sum(small[::2, gain_count * gain_dev :], axis=0).reshape(MICRO, LAYERS), 1.0
    )
    reach = lax.dynamic_index_in_dim(reach, sy, 0, False)
    gains_seen = small[:, : gain_count * gain_dev].reshape(owners, gain_count, gain_dev)
    order = jnp.arange(owners)
    rel = ((order // 2) ^ z) * 2 + ((order % 2) ^ c)
    gains_full = gains_seen[rel].transpose(1, 0, 2).reshape(gain_count, width)
    gains_full = wide(low(gains_full))

    row = lax.dynamic_index_in_dim(plane, sx ^ c, 1, False)
    row = in_order(lax.dynamic_index_in_dim(row, sy, 1, False), s)
    mine = lax.dynamic_slice_in_dim(row, 2 * c, 2, 0)
    theirs = lax.dynamic_slice_in_dim(row, 2 * (1 - c), 2, 0)
    target_ids = mine[:, :tok_dev].reshape(-1)
    source_ids = mine[:, tok_dev : 2 * tok_dev].reshape(-1)
    sentence = mine[:, 2 * tok_dev : 3 * tok_dev].reshape(-1)
    other_sentence = theirs[:, 2 * tok_dev : 3 * tok_dev].reshape(-1)
    rest = 3 * tok_dev
    places = (
        mine[:, rest : rest + loss_dev] + (jnp.arange(2, dtype=jnp.int32) * tok_dev)[:, None]
    ).reshape(-1)
    wanted = mine[:, rest + loss_dev : rest + 2 * loss_dev].reshape(-1)
    depth = mine[:, rest + 2 * loss_dev : rest + 3 * loss_dev].reshape(-1)
    masks = attend_masks(sentence, other_sentence, c * half_row, (1 - c) * half_row)

    ids = jnp.concatenate([source_ids, target_ids])
    if fast:
        ids, small = step((ids, small), first)
        ids = step(ids, second, first)
        settle(GATHERED[0], first.result)
    table = weights["table", 0].reshape(vocabulary, width)
    looked_up = table[ids].astype(jnp.float32) * root_width
    xe = looked_up[:half_row]
    x = looked_up[half_row:]
    kept_enc = (xe, *project(xe, gains_full[0], weights["qkv", 0]))
    if fast:
        xe, kept_enc, x = step((xe, kept_enc, x), second)
    o, saved_enc = attend_forward(masks, False, *kept_enc[2:])
    if fast:
        o, fourth = step((o, fourth), second)
        fourth = lax.all_gather(fourth, PLANE + LINE).reshape(4, owners, *fourth.shape)
        settle(GATHERED[1], second.result)
    *kept_enc_feed, xe = feed(
        o, weights["out", 0], xe, gains_full[1], weights["up", 0], weights["down", 0]
    )
    final_gain = gains_full[2 * ENC]
    memory = low(normalize(xe, final_gain))
    kept = []
    states = []
    for layer_id in range(LAYERS):
        base = 2 * ENC + 1 + 4 * layer_id
        slot = ENC + 2 * layer_id
        if fast and layer_id == 0:
            (x, memory), third = hold((x, memory), third)
            settle(GATHERED[2], unpack(third, *layout(GATHERED[2]), unit, owners))
        if fast and layer_id == 1:
            x, fourth = hold(x, fourth)
            settle(GATHERED[3], unpack(fourth, *layout(GATHERED[3]), unit, owners))
        cross = weights["qkv", slot + 1]
        pair = jnp.stack([low(product(memory, cross[1])), low(product(memory, cross[2]))])
        kept_self = (x, *project(x, gains_full[base], weights["qkv", slot]))
        o, saved_self = attend_forward(masks, True, *kept_self[2:])
        *kept_cross, q = between(o, weights["out", slot], x, gains_full[base + 1], cross)
        o, saved_cross = attend_forward(masks, False, q, pair)
        feed_at = ENC + layer_id
        *kept_feed, x = feed(
            o,
            weights["out", slot + 1],
            kept_cross[0],
            gains_full[base + 2],
            weights["up", feed_at],
            weights["down", feed_at],
        )
        kept.append((kept_self, saved_self, kept_cross, saved_cross, kept_feed))
        states.append(x)

    pick = (places[:, None] == jnp.arange(half_row)[None, :]).astype(jnp.bfloat16)
    exit_gains = [gains_full[2 * ENC + 4 + 4 * layer_id] for layer_id in range(LAYERS)]
    exits = jnp.concatenate(
        [low(product(pick, low(normalize(states[i], exit_gains[i])))) for i in range(LAYERS)]
    )
    logits = against_rows(exits, table) * LOGIT_SCALE
    wanted_all = jnp.concatenate([wanted] * LAYERS)
    hit = jnp.arange(vocabulary)[None, :] == wanted_all[:, None]
    picked = jnp.sum(jnp.where(hit, logits, 0.0), axis=-1)
    top = jnp.max(logits, axis=-1)
    lse = top + jnp.log(jnp.sum(jnp.exp(logits - top[:, None]), axis=-1))
    shares = jnp.concatenate(
        [(depth >= i).astype(jnp.float32) / reach[i] / MICRO for i in range(LAYERS)]
    )
    loss_part = jnp.sum((lse - picked) * shares)
    grad_logits = low(
        (jnp.exp(logits - lse[:, None]) - hit.astype(jnp.float32))
        * shares[:, None]
        * LOGIT_SCALE
    )
    grad_exits = product(grad_logits, table)
    table_grad = outer_sum(grad_logits, exits)

    grads = {}
    gain_parts = [None] * gain_count
    grad_x = None
    grad_memory = None
    for layer_id in reversed(range(LAYERS)):
        slot = ENC + 2 * layer_id
        base = 2 * ENC + 1 + 4 * layer_id
        count = places.shape[0]
        grad_rows = lax.dot_general(
            wide(pick),
            grad_exits[layer_id * count : (layer_id + 1) * count],
            (((0,), (0,)), ((), ())),
            precision=lax.Precision.HIGHEST,
            preferred_element_type=jnp.float32,
        )
        grad_here, gain_parts[base + 3] = norm_back(
            states[layer_id], exit_gains[layer_id], grad_rows
        )
        grad_x = grad_here if grad_x is None else grad_x + grad_here
        kept_self, saved_self, kept_cross, saved_cross, kept_feed = kept[layer_id]
        up, down = ("up", ENC + layer_id), ("down", ENC + layer_id)
        qkv, out = ("qkv", slot + 1), ("out", slot + 1)
        grads[up], grads[down], grad_x, gain_parts[base + 2], grad_o, grads[out] = feed_back(
            grad_x,
            kept_feed,
            gains_full[base + 2],
            weights[up],
            weights[down],
            saved_cross[3],
            weights[out],
        )
        if fast and layer_id == 1:
            feed_mover = reduce(REDUCED[0], long_reduce_stages)
            grad_x, grad_o = step((grad_x, grad_o), feed_mover, feed_mover)
        if fast and layer_id == 0:
            late = reduce(REDUCED[1], long_reduce_stages)
            grad_x, grad_o = step((grad_x, grad_o), feed_mover, late, late)
        grad_q, own, other = attend_backward(saved_cross, masks, False, grad_o)
        grad_pair, more = memory_back(own, other, memory, weights[qkv])
        grad_memory = more if grad_memory is None else grad_memory + more
        out = ("out", slot)
        grad_query, grad_x, gain_parts[base + 1], grad_o, grads[out] = between_back(
            grad_q,
            kept_cross[1],
            kept_cross[0],
            gains_full[base + 1],
            weights[qkv],
            grad_x,
            saved_self[3],
            weights[out],
        )
        grads[qkv] = (grad_query, grad_pair)
        grad_q, own, other = attend_backward(saved_self, masks, True, grad_o)
        qkv = ("qkv", slot)
        grads[qkv], grad_x, gain_parts[base] = project_back(
            grad_q,
            own,
            other,
            kept_self[1],
            kept_self[0],
            gains_full[base],
            weights[qkv],
            grad_x,
        )
    if fast:
        grad_x, grad_memory = step((grad_x, grad_memory), feed_mover)
    grad_enc, gain_parts[2 * ENC] = norm_back(xe, final_gain, grad_memory)
    up, down, qkv, out = ("up", 0), ("down", 0), ("qkv", 0), ("out", 0)
    grads[up], grads[down], grad_enc, gain_parts[1], grad_o, grads[out] = feed_back(
        grad_enc,
        kept_enc_feed,
        gains_full[1],
        weights[up],
        weights[down],
        saved_enc[3],
        weights[out],
    )
    if fast:
        middle = reduce(REDUCED[2], long_reduce_stages)
        grad_enc, grad_o = step((grad_enc, grad_o), middle, late, middle)
    grad_q, own, other = attend_backward(saved_enc, masks, False, grad_o)
    grads[qkv], grad_enc, gain_parts[0] = project_back(
        grad_q, own, other, kept_enc[1], kept_enc[0], gains_full[0], weights[qkv], grad_enc
    )
    token_ids = jnp.concatenate([source_ids, target_ids])
    token_grads = low(jnp.concatenate([grad_enc, grad_x]) * root_width)
    looked = (token_ids[:, None] == jnp.arange(vocabulary)[None, :]).astype(jnp.bfloat16)
    table_grad = low(table_grad + outer_sum(looked, token_grads))
    grads["table", 0] = table_grad

    gain_grad = jnp.concatenate([part.reshape(1, -1) for part in gain_parts])
    grads["gains", 0] = low(jnp.pad(gain_grad.T, ((0, 0), (0, COL - gain_count))))[None]

    reduced = {}
    if fast:
        last = reduce(REDUCED[3])
        loss_part = step(loss_part, last)
        loss_part = step(loss_part, last)
        loss_part = step(loss_part, last, middle)
        loss_part = step(loss_part, last)
        movers = (feed_mover, late, middle, last)
        loss_part = step(loss_part, last)
        squares = sum(mover.squares for mover in movers)
        squares, loss_total = all_sum(jnp.stack([squares, loss_part]))
        squares = step(squares, late, middle, last)
    else:
        squares = sum(reduce_plainly(entries) for entries in REDUCED)
        squares, loss_total = all_sum(jnp.stack([squares, loss_part]))
    grad_norm = jnp.sqrt(squares)
    clip_factor = CLIP_NORM / jnp.maximum(grad_norm, CLIP_NORM)

    names = ("qkv", "out", "up", "down", "table", "gains")
    if fast:
        plan = []
        for bucket, entries in enumerate(REDUCED):
            first = 0
            for (name, i, kind), count in zip(entries, layout(entries)[1]):
                plan.append((bucket, first, count, kind, names.index(name), i))
                first += count
        parts = [part for mover in movers for part in mover.result]
        shapes = [shard_of[name].shape for name in names[:-1]] + [(1, gain_dev, COL)]
        placed = pl.pallas_call(
            functools.partial(settle_kernel, len(parts), tuple(plan), unit),
            out_shape=[jax.ShapeDtypeStruct(shape, jnp.bfloat16) for shape in shapes],
            in_specs=[SCALAR] + [ANY] * len(parts),
            out_specs=[ONCHIP] * len(shapes),
            scratch_shapes=[pltpu.SemaphoreType.DMA((len(shapes),))],
            cost_estimate=LIGHT,
            name="place_gradients",
        )(me, *parts)
        ready = [wide(array) for array in placed]
    else:
        ready = [
            wide(jnp.stack([reduced[name, i] for i in range(len(shard_of.get(name, "1")))]))
            for name in names
        ]
    gradients = (
        *ready[:4],
        ready[5][0, :, :gain_count].T,
        ready[4][0],
    )
    masters = (qkv_weight, out_weight, up_weight, down_weight, norm_gains, embed_table)
    firsts = (qkv_first, out_first, up_first, down_first, gains_first, table_first)
    seconds = (qkv_second, out_second, up_second, down_second, gains_second, table_second)
    results = [
        adam_update(masters[i], firsts[i], seconds[i], gradients[i] * clip_factor) for i in range(6)
    ]
    gains_grad = gradients[4] * clip_factor
    return (
        loss_total,
        grad_norm,
        results[0][0],
        results[1][0],
        results[2][0],
        results[3][0],
        gains_grad,
        results[5][0],
        results[0][1],
        results[1][1],
        results[2][1],
        results[3][1],
        results[4][1],
        results[5][1],
        results[0][2],
        results[1][2],
        results[2][2],
        results[3][2],
        results[4][2],
        results[5][2],
    )


def solution(mesh):
    seq, vocab = mesh.devices.shape
    fine = Mesh(mesh.devices.reshape(2, seq // 2, vocab // 2, 2), ("sy", "sx", "z", "c"))
    ints = P(None, LINE, PLANE)
    block = P(None, LINE, None)
    gains = P(None, LINE)
    rows = P(LINE, None)
    arrays = (block, block, block, block, gains, rows)
    return jax.shard_map(
        shards,
        mesh=fine,
        in_specs=(ints,) * 6 + arrays * 3,
        out_specs=(P(), P(), block, block, block, block, gains, rows) + arrays * 2,
        check_vma=False,
    )
```

```python
import functools
import math

import jax
import jax.numpy as jnp
from jax import lax
from jax.experimental import pallas as pl
from jax.experimental.pallas import tpu as pltpu
from jax.sharding import Mesh
from jax.sharding import PartitionSpec as P

HEADS = 8
HEAD = 64
ENC = 1
LAYERS = 2
MICRO = 2
COL = 512
HALF, FULL = jnp.bfloat16, jnp.float32

NORM_EPS = 1e-06
CLIP_NORM = 0.01
LEARN_RATE = 0.05
BETA_ONE = 0.9
BETA_TWO = 0.999
ADAM_EPS = 1e-08
WEIGHT_DECAY = 0.01
ADAM_STEP = 10
LOGIT_SCALE = 4.0
NEGATIVE = -1e30

PLANE = ("sy", "sx")
LINE = ("z", "c")

TABLE = ("table", 0, "blk")


def attention_parts(i):
    return (("qkv", i, "row"), ("out", i, "row"))


def feed_parts(i):
    return (("up", i, "row"), ("down", i, "blk"))


GATHERED = (
    (TABLE,) + attention_parts(0),
    feed_parts(0),
    attention_parts(1) + attention_parts(2) + feed_parts(1) + attention_parts(3),
    attention_parts(4) + feed_parts(2),
)
REDUCED = (
    feed_parts(2),
    attention_parts(3) + attention_parts(4) + feed_parts(1),
    attention_parts(1) + attention_parts(2) + feed_parts(0),
    (TABLE,) + attention_parts(0),
)


def flip(x, axis, bit=1):
    if isinstance(axis, tuple):
        n = math.prod(lax.axis_size(a) for a in axis)
    else:
        n = lax.axis_size(axis)
    return lax.ppermute(x, axis, [(i, i ^ bit) for i in range(n)])


def bits(axis):
    n = lax.axis_size(axis)
    return [1 << k for k in range(n.bit_length() - 1)]


def gathered(x, axis):
    if isinstance(axis, tuple) or lax.axis_size(axis) <= 4:
        n = 4 if isinstance(axis, tuple) else lax.axis_size(axis)
        return jnp.stack([x] + [flip(x, axis, r) for r in range(1, n)])
    x = x[None]
    for bit in bits(axis):
        x = jnp.concatenate([x, flip(x, axis, bit)], axis=0)
    return x


def in_order(blocks, index):
    n = blocks.shape[0]
    return jnp.concatenate(
        [lax.dynamic_index_in_dim(blocks, i ^ index, 0, keepdims=True) for i in range(n)]
    )


def all_sum(x):
    for axis in ("c", "sx", "sy", "z"):
        for bit in bits(axis):
            x = x + flip(x, axis, bit)
    return x


def hold(carry, things):
    return lax.optimization_barrier((carry, things))


def step(carry, *movers):
    for mover in movers:
        carry, (mover.held, mover.arrived) = hold(carry, (mover.held, mover.arrived))
        leaving = next(mover.stages)
        carry, (arrays, mover.held) = hold(carry, ([array for array, _ in leaving], mover.held))
        mover.arrived = [
            flip(array, *route)
            if route
            else lax.psum_scatter(array, PLANE + ("z",), scatter_dimension=0, tiled=True)
            for array, (_, route) in zip(arrays, leaving)
        ]
    return carry


class Mover:
    def __init__(self):
        self.held = []
        self.arrived = []


def normalize(v, g):
    return v * lax.rsqrt(jnp.mean(v * v, axis=-1, keepdims=True) + NORM_EPS) * g


def norm_back(v, g, cotangent):
    _, pullback = jax.vjp(normalize, v, g)
    return pullback(cotangent)


def product(a, b):
    return jnp.dot(a, b, preferred_element_type=jnp.float32)


def outer_sum(a, b):
    return lax.dot_general(a, b, (((0,), (0,)), ((), ())), preferred_element_type=jnp.float32)


def against_rows(a, b):
    return lax.dot_general(a, b, (((1,), (1,)), ((), ())), preferred_element_type=jnp.float32)


def split_heads(v):
    return v.reshape(v.shape[0], HEADS, HEAD)


def low(v):
    return v.astype(jnp.bfloat16)


def wide(v):
    return v.astype(jnp.float32)


def adam_update(master, first, second, grad):
    first = BETA_ONE * first + (1.0 - BETA_ONE) * grad
    second = BETA_TWO * second + (1.0 - BETA_TWO) * grad * grad
    fixed_first = first / (1.0 - BETA_ONE**ADAM_STEP)
    fixed_second = second / (1.0 - BETA_TWO**ADAM_STEP)
    master = master - LEARN_RATE * (
        fixed_first / (jnp.sqrt(fixed_second) + ADAM_EPS) + WEIGHT_DECAY * master
    )
    return (master, first, second)


def owned_blocks(array, kind, unit):
    if kind == "row":
        rows, columns = array.shape
        return array.reshape(rows, columns // COL, COL).transpose(1, 0, 2)
    rows = array.shape[0]
    per = rows // (4 * unit)
    return array.reshape(4, per, unit, COL).transpose(1, 0, 2, 3).reshape(per, 4 * unit, COL)


def quarter_blocks(array, kind, unit, s):
    size = array.shape[0] // 4
    array = lax.dynamic_slice_in_dim(array, s * size, size, axis=0)
    if kind == "row":
        return low(array).reshape(unit, -1, COL).transpose(1, 0, 2)
    return low(array).reshape(-1, unit, COL)


def block_counts(entries, shard_shapes, unit):
    counts = []
    for name, _, kind in entries:
        rows, columns = shard_shapes[name]
        counts.append(columns // COL if kind == "row" else rows // (4 * unit))
    return counts


def natural_shape(kind, count, unit, owners):
    if kind == "row":
        return (count, owners * 4 * unit, COL)
    return (owners, 4, count, unit, COL)


def scatter_kernel(plan, unit, me_ref, *refs):
    pieces, outs, sem = refs[:10], refs[10:-1], refs[-1]
    c, z, s = me_ref[0], me_ref[1], me_ref[2]

    def put(out, kind, owner, part, rows, source):
        if kind == "row":
            start = pl.multiple_of(owner * (4 * unit) + part * unit, unit)
            target = outs[out].at[:, pl.ds(start, rows), :]
        else:
            target = outs[out].at[owner, part]
        pltpu.make_async_copy(source, target, sem.at[out]).start()

    for c_rel in range(2):
        shard, *quarters = pieces[5 * c_rel : 5 * c_rel + 5]
        for z_rel in range(4):
            owner = (z ^ z_rel) * 2 + (c ^ c_rel)
            for out, (kind, first, count) in enumerate(plan):
                last = first + count
                if z_rel == 0:
                    if kind == "row":
                        put(out, kind, owner, 0, 4 * unit, shard.at[first:last])
                    else:
                        for part in range(4):
                            rows = pl.ds(part * unit, unit)
                            put(out, kind, owner, part, unit, shard.at[first:last, rows, :])
                else:
                    for s_rel, quarter in enumerate(quarters):
                        put(out, kind, owner, s ^ s_rel, unit, quarter.at[z_rel - 1, first:last])
    for out in range(len(plan)):
        pltpu.make_async_copy(outs[out], outs[out], sem.at[out]).wait()


def collect_kernel(plan, unit, ordered, me_ref, *refs):
    grads, keep, send, sem = refs[: len(plan)], refs[len(plan)], refs[len(plan) + 1], refs[-1]
    c, z, s = me_ref[0], me_ref[1], me_ref[2]
    for c_rel, out in ((0, keep), (1, send)):
        for z_rel in range(4):
            owner = (z ^ z_rel) * 2 + (c ^ c_rel)
            for s_rel in range(4):
                part = s ^ s_rel
                for grad, (kind, first, count) in zip(grads, plan):
                    if kind == "row":
                        start = pl.multiple_of(owner * (4 * unit) + part * unit, unit)
                        source = grad.at[:, pl.ds(start, unit), :]
                    else:
                        source = grad.at[owner, part]
                    place = (part, z ^ z_rel) if ordered else (s_rel, z_rel)
                    target = out.at[*place, first : first + count]
                    pltpu.make_async_copy(source, target, sem.at[c_rel]).start()
    for c_rel, out in ((0, keep), (1, send)):
        pltpu.make_async_copy(out, out, sem.at[c_rel]).wait()


LIGHT = pl.CostEstimate(flops=1, bytes_accessed=1, transcendentals=0)
ANY = pl.BlockSpec(memory_space=pl.ANY)
ONCHIP = pl.BlockSpec(memory_space=pltpu.VMEM)
SCALAR = pl.BlockSpec(memory_space=pltpu.SMEM)


def gather_stages(mover, me, shard, kinds, counts, unit, owners):
    starts = [sum(counts[:i]) for i in range(len(counts))]
    mover.held = [shard]
    part = lax.dynamic_slice_in_dim(shard, me[2] * unit, unit, axis=1)
    yield [(part, ("z", bit)) for bit in (1, 2, 3)]
    mine = jnp.stack(mover.arrived)
    mover.held.append(mine)
    yield [(mine, (PLANE, bit)) for bit in (1, 2, 3)]
    mover.held += mover.arrived
    yield [(piece, ("c",)) for piece in mover.held]
    plan = tuple(zip(kinds, starts, counts))
    mover.result = pl.pallas_call(
        functools.partial(scatter_kernel, plan, unit),
        out_shape=[
            jax.ShapeDtypeStruct(natural_shape(kind, count, unit, owners), jnp.bfloat16)
            for kind, count in zip(kinds, counts)
        ],
        in_specs=[SCALAR] + [ANY] * 10,
        out_specs=[ONCHIP] * len(plan),
        scratch_shapes=[pltpu.SemaphoreType.DMA((len(plan),))],
        cost_estimate=LIGHT,
        name="place_weights",
    )(me, *mover.held, *mover.arrived)
    mover.held = []
    yield []


def unpack_kernel(plan, pieces, *refs):
    outs, sem = refs[:-1], refs[-1]
    for out, (kind, first, count) in enumerate(plan):
        for part in range(4):
            if kind == "blk":
                source = pieces.at[part, :, first : first + count]
                pltpu.make_async_copy(source, outs[out].at[:, part], sem.at[out]).start()
                continue
            for k in range(count):
                source = pieces.at[part, :, first + k]
                pltpu.make_async_copy(source, outs[out].at[k, :, part], sem.at[out]).start()
    for out in range(len(plan)):
        pltpu.make_async_copy(outs[out], outs[out], sem.at[out]).wait()


def unpack(pieces, kinds, counts, unit, owners):
    starts = [sum(counts[:i]) for i in range(len(counts))]
    shapes = [
        (count, owners, 4, unit, COL) if kind == "row" else (owners, 4, count, unit, COL)
        for kind, count in zip(kinds, counts)
    ]
    placed = pl.pallas_call(
        functools.partial(unpack_kernel, tuple(zip(kinds, starts, counts))),
        out_shape=[jax.ShapeDtypeStruct(shape, jnp.bfloat16) for shape in shapes],
        in_specs=[ANY],
        out_specs=[ONCHIP] * len(shapes),
        scratch_shapes=[pltpu.SemaphoreType.DMA((len(shapes),))],
        cost_estimate=LIGHT,
        name="place_gathered",
    )(pieces)
    return [
        out.reshape(count, -1, COL) if kind == "row" else out
        for out, kind, count in zip(placed, kinds, counts)
    ]


def added(arrays):
    total = wide(arrays[0])
    for array in arrays[1:]:
        total = total + wide(array)
    return total


def plane_sum_kernel(keep, core, from_x, from_y, left, right, own, *sends):
    half = left.shape[1]
    for bit in range(4):
        for part, (one, two) in ((slice(0, half), (from_x, left)), (slice(half, None), (from_y, right))):
            total = added([keep[bit, part], core[bit, part], one[bit], two[bit]])
            if bit == 0:
                own[part] = total
            else:
                sends[bit - 1][part] = low(total)


def line_sum_kernel(own, one, two, three, whole, squares):
    total = added([own[...], one[...], two[...], three[...]])
    whole[...] = low(total)
    squares[0, 0] = jnp.sum(total * total)


def collect(me, grads, kinds, counts, unit, ordered):
    starts = [sum(counts[:i]) for i in range(len(counts))]
    plan = tuple(zip(kinds, starts, counts))
    shape = jax.ShapeDtypeStruct((4, 4, sum(counts), unit, COL), jnp.bfloat16)
    return pl.pallas_call(
        functools.partial(collect_kernel, plan, unit, ordered),
        out_shape=[shape, shape],
        in_specs=[SCALAR] + [ANY] * len(plan),
        out_specs=[ONCHIP, ONCHIP],
        scratch_shapes=[pltpu.SemaphoreType.DMA((2,))],
        cost_estimate=LIGHT,
        name="collect_gradients",
    )(me, *grads)


def long_reduce_stages(mover, me, grads, kinds, counts, unit):
    keep, send = collect(me, grads, kinds, counts, unit, True)
    mover.held = [keep]
    yield [(send, ("c",))]
    chip = low(added(mover.held + mover.arrived))
    mover.held = []
    yield [(chip.reshape(16, *chip.shape[2:]), None)]
    own = mover.arrived[0][0]
    mover.squares = jnp.sum(wide(own) * wide(own))
    mover.held = [own]
    yield [(own, (PLANE, bit)) for bit in (1, 2, 3)]
    mover.result = mover.held + mover.arrived
    mover.held = []
    yield []


def reduce_stages(mover, me, grads, kinds, counts, unit):
    total = sum(counts)
    keep, send = collect(me, grads, kinds, counts, unit, False)
    mover.held = [keep]
    half = total // 2
    yield [(send, ("c",))]
    mover.held = [a.reshape(2, 2, *a.shape[1:]) for a in mover.held + mover.arrived]
    yield [
        (low(added([a[:, 1, :, :half] for a in mover.held])), ("sx",)),
        (low(added([a[1, :, :, half:] for a in mover.held])), ("sy",)),
    ]
    mover.held += mover.arrived

    def sides():
        both, (come_x, come_y) = mover.held[:2], mover.held[2:4]
        return (
            [a[:, 0, :, :half] for a in both] + [come_x],
            [a[0, :, :, half:] for a in both] + [come_y],
        )

    left, right = sides()
    yield [(low(added([a[1] for a in left])), ("sy",)), (low(added([a[1] for a in right])), ("sx",))]
    mover.held += mover.arrived

    block = (total, unit, COL)
    first_part = pl.BlockSpec((None, None, 4, *block), lambda i: (0, 0, 0, 0, 0, 0))
    half_part = [pl.BlockSpec((None, 4, n, unit, COL), lambda i: (0, 0, 0, 0, 0)) for n in (half, total - half)]
    own, *sends = pl.pallas_call(
        plane_sum_kernel,
        grid=(1,),
        out_shape=[jax.ShapeDtypeStruct(block, FULL)] + [jax.ShapeDtypeStruct(block, HALF)] * 3,
        in_specs=[first_part, first_part, *half_part, ONCHIP, ONCHIP],
        out_specs=[ONCHIP] * 4,
        cost_estimate=LIGHT,
        name="plane_sum",
    )(*mover.held)
    mover.held = [own]
    yield [(send, ("z", bit)) for bit, send in zip((1, 2, 3), sends)]
    own, squares = pl.pallas_call(
        line_sum_kernel,
        out_shape=[
            jax.ShapeDtypeStruct(block, HALF),
            jax.ShapeDtypeStruct((1, 1), FULL),
        ],
        in_specs=[ONCHIP] * 4,
        out_specs=[ONCHIP, SCALAR],
        cost_estimate=LIGHT,
        name="line_sum",
    )(*mover.held, *mover.arrived)
    mover.squares = squares[0, 0]
    mover.held = [own]
    yield [(own, (PLANE, bit)) for bit in (1, 2, 3)]
    mover.result = mover.held + mover.arrived
    mover.held = []
    yield []


def small_stages(mover, x, z):
    for axis in ("c", "sx", "sy"):
        mover.held = [x]
        yield [(x, (axis,))]
        x = mover.held[0] + mover.arrived[0]
    mover.held = [x]
    yield [(x, ("z", bit)) for bit in (1, 2, 3)]
    mover.result = jnp.sum(in_order(jnp.stack(mover.held + mover.arrived), z), axis=0)
    yield []


def settle_kernel(sizes, plan, unit, me_ref, *refs):
    buckets, outs, sem = refs[:sizes], refs[sizes:-1], refs[-1]
    s = me_ref[2]
    for bucket, first, count, kind, out, i in plan:
        for s_rel in range(4):
            source = buckets[4 * bucket + s_rel]
            part = s ^ s_rel
            if kind == "blk":
                for k in range(count):
                    start = pl.multiple_of((part * count + k) * unit, unit)
                    target = outs[out].at[i, pl.ds(start, unit), :]
                    pltpu.make_async_copy(source.at[first + k], target, sem.at[out]).start()
                continue
            rows = pl.ds(pl.multiple_of(part * unit, unit), unit)
            for k in range(count):
                target = outs[out].at[i, rows, k * COL : k * COL + COL]
                pltpu.make_async_copy(source.at[first + k], target, sem.at[out]).start()
    for out, ref in enumerate(outs):
        pltpu.make_async_copy(ref, ref, sem.at[out]).wait()


def owned_natural(parts, kind):
    if kind == "row":
        four, count, unit, _ = parts.shape
        return parts.transpose(0, 2, 1, 3).reshape(four * unit, count * COL)
    return parts.reshape(-1, COL)


BQ = 128
CK = 256
CF = 256
NT = (((1,), (1,)), ((), ()))
TN = (((0,), (0,)), ((), ()))
NN = (((1,), (0,)), ((), ()))


def dot32(a, b, dims):
    return lax.dot_general(a, b, dims, preferred_element_type=jnp.float32)


def load_halves(own, other, whole, sem):
    half = whole.shape[0] // 2
    copies = [
        pltpu.make_async_copy(own, whole.at[pl.ds(0, half)], sem.at[0]),
        pltpu.make_async_copy(other, whole.at[pl.ds(half, half)], sem.at[1]),
    ]
    for copy in copies:
        copy.start()
    return copies


def pair_rows(block, scale=None):
    lane = lax.broadcasted_iota(jnp.int32, block.shape, 1)
    zero = jnp.zeros_like(block)
    if scale is not None:
        block = block * jnp.asarray(scale, block.dtype)
    return jnp.concatenate(
        [jnp.where(lane < HEAD, block, zero), jnp.where(lane < HEAD, zero, block)], axis=0
    )


def pair_lanes(stacked):
    rows = stacked.shape[0] // 2
    lane = lax.broadcasted_iota(jnp.int32, (rows, 2 * HEAD), 1)
    return jnp.where(lane < HEAD, stacked[:rows], stacked[rows:])


def open_to(act, bounds, rows, j, chunks):
    half = chunks // 2
    base = jnp.where(j < half, act[0] + j * CK, act[1] + (j - half) * CK)
    spot = base + lax.broadcasted_iota(jnp.int32, (CK, BQ), 0)
    open_ = (spot >= bounds[0:1, rows]) & (spot <= bounds[1:2, rows])
    return jnp.concatenate([open_, open_], axis=1)


def attend_kernel(
    act, bounds, q, kv_own, kv_oth, o, lse,
    k_all, v_all, scores, queries, top, total, acc, sem_k, sem_v,
):
    pairs = q.shape[1] // (2 * HEAD)
    blocks = q.shape[0] // BQ
    chunks = k_all.shape[0] // CF
    half = chunks // 2
    waits = load_halves(kv_own.at[0], kv_oth.at[0], k_all, sem_k)
    waits += load_halves(kv_own.at[1], kv_oth.at[1], v_all, sem_v)
    for copy in waits:
        copy.wait()
    square = lax.broadcasted_iota(jnp.int32, (BQ, BQ), 0)
    along = lax.broadcasted_iota(jnp.int32, (BQ, BQ), 1)

    def one_block(b, _):
        rows = pl.ds(pl.multiple_of(b * BQ, BQ), BQ)
        for h in range(pairs):
            queries[h] = pair_rows(q[rows, h * 128 : h * 128 + 128], HEAD ** (-0.5))
        top[...] = jnp.full_like(top, NEGATIVE)
        total[...] = jnp.zeros_like(total)
        acc[...] = jnp.zeros_like(acc)
        least = jnp.broadcast_to(bounds[0:1, rows], (BQ, BQ)).T
        most = jnp.broadcast_to(bounds[1:2, rows], (BQ, BQ)).T

        def first(j, _):
            @pl.when(act[2 + b * chunks + j] > 0)
            def _():
                keys = pl.ds(pl.multiple_of(j * CF, CF), CF)
                base = jnp.where(j < half, act[0] + j * CF, act[1] + (j - half) * CF)
                open_ = []
                for part in range(CF // 128):
                    spot = base + part * 128 + along
                    one = (spot >= least) & (spot <= most)
                    open_.append(jnp.concatenate([one, one], axis=0))
                for h in range(pairs):
                    s = dot32(queries[h], k_all[keys, h * 128 : h * 128 + 128], NT)
                    best = top[h]
                    for part, one in enumerate(open_):
                        t = jnp.where(one, s[:, part * 128 : part * 128 + 128], NEGATIVE)
                        scores[h, j, :, part * 128 : part * 128 + 128] = t
                        best = jnp.maximum(best, t)
                    top[h] = best

            return 0

        lax.fori_loop(0, chunks, first, 0)
        for h in range(pairs):
            top[h] = jnp.broadcast_to(jnp.max(top[h], axis=1, keepdims=True), top.shape[1:])

        def second(j, _):
            @pl.when(act[2 + b * chunks + j] > 0)
            def _():
                keys = pl.ds(pl.multiple_of(j * CF, CF), CF)
                for h in range(pairs):
                    parts = []
                    more = total[h]
                    for part in range(CF // 128):
                        e = jnp.exp(scores[h, j, :, part * 128 : part * 128 + 128] - top[h])
                        more = more + e
                        parts.append(e.astype(jnp.bfloat16))
                    total[h] = more
                    e = parts[0] if len(parts) == 1 else jnp.concatenate(parts, axis=1)
                    acc[h] = acc[h] + dot32(e, v_all[keys, h * 128 : h * 128 + 128], NN)

            return 0

        lax.fori_loop(0, chunks, second, 0)
        for h in range(pairs):
            denom = jnp.broadcast_to(
                jnp.sum(total[h], axis=1, keepdims=True), total.shape[1:]
            )
            o[rows, h * 128 : h * 128 + 128] = pair_lanes(acc[h] / denom).astype(o.dtype)
            for part in range(2):
                span = slice(part * BQ, part * BQ + BQ)

                def line(level, span=span):
                    own = jnp.where(square == along, level[span], 0.0)
                    return jnp.sum(own, axis=0, keepdims=True)

                lse[b, h, :, span] = line(top[h]) + jnp.log(line(denom))
        return 0

    lax.fori_loop(0, blocks, one_block, 0)


def attend_back_kernel(
    act, bounds, q, kv_own, kv_oth, o, lse, grad,
    grad_q, grad_own, grad_oth,
    k_all, v_all, k_turned, queries, grads, delta, grad_queries, sem_k, sem_v,
):
    pairs = q.shape[1] // (2 * HEAD)
    blocks = q.shape[0] // BQ
    chunks = k_all.shape[0] // CK
    waits = load_halves(kv_own.at[0], kv_oth.at[0], k_all, sem_k)
    waits += load_halves(kv_own.at[1], kv_oth.at[1], v_all, sem_v)
    grad_own[...] = jnp.zeros_like(grad_own)
    grad_oth[...] = jnp.zeros_like(grad_oth)
    for copy in waits:
        copy.wait()

    def turn(j, _):
        for h in range(pairs):
            for part in range(CK // 128):
                keys = pl.ds(pl.multiple_of(j * CK + part * 128, 128), 128)
                k_turned[j, h, :, part * 128 : part * 128 + 128] = k_all[
                    keys, h * 128 : h * 128 + 128
                ].T
        return 0

    lax.fori_loop(0, chunks, turn, 0)

    def one_block(b, _):
        rows = pl.ds(pl.multiple_of(b * BQ, BQ), BQ)
        for h in range(pairs):
            lanes = slice(h * 128, h * 128 + 128)
            queries[h] = pair_rows(q[rows, lanes], HEAD ** (-0.5))
            grads[h] = pair_rows(grad[rows, lanes])
            both = (o[rows, lanes].astype(jnp.float32) * grad[rows, lanes].astype(jnp.float32)).T
            delta[h] = jnp.concatenate(
                [
                    jnp.sum(both[:HEAD], axis=0, keepdims=True),
                    jnp.sum(both[HEAD:], axis=0, keepdims=True),
                ],
                axis=1,
            )
        grad_queries[...] = jnp.zeros_like(grad_queries)

        def one_chunk(j, target, local):
            keys = pl.ds(pl.multiple_of(j * CK, CK), CK)
            own_keys = pl.ds(pl.multiple_of(local * CK, CK), CK)
            open_ = open_to(act, bounds, rows, j, chunks)
            for h in range(pairs):
                lanes = slice(h * 128, h * 128 + 128)
                s = jnp.where(open_, dot32(k_all[keys, lanes], queries[h], NT), NEGATIVE)
                p = jnp.exp(s - lse[b, h])
                ds = p * (dot32(v_all[keys, lanes], grads[h], NT) - delta[h])
                p = p.astype(jnp.bfloat16)
                ds = ds.astype(jnp.bfloat16)
                target[0, own_keys, lanes] += dot32(ds, queries[h], NN)
                target[1, own_keys, lanes] += dot32(p, grads[h], NN)
                grad_queries[h] += dot32(k_turned[j, h], ds, NN)

        def own_chunk(j, _):
            @pl.when(act[2 + b * chunks + j] > 0)
            def _():
                one_chunk(j, grad_own, j)

            return 0

        def oth_chunk(j, _):
            @pl.when(act[2 + b * chunks + j] > 0)
            def _():
                one_chunk(j, grad_oth, j - chunks // 2)

            return 0

        lax.fori_loop(0, chunks // 2, own_chunk, 0)
        lax.fori_loop(chunks // 2, chunks, oth_chunk, 0)
        for h in range(pairs):
            grad_q[rows, h * 128 : h * 128 + 128] = (
                pair_lanes(grad_queries[h].T) * HEAD ** (-0.5)
            ).astype(grad_q.dtype)
        return 0

    lax.fori_loop(0, blocks, one_block, 0)


def attend_masks(sentence, other, start, other_start):
    n = sentence.shape[0]
    seg = jnp.concatenate([sentence, other])
    spots = start + jnp.arange(n, dtype=jnp.int32)
    pos = jnp.concatenate([spots, other_start + jnp.arange(n, dtype=jnp.int32)])
    begin = jnp.sum((seg[None, :] < sentence[:, None]).astype(jnp.int32), axis=1)
    end = jnp.sum((seg[None, :] <= sentence[:, None]).astype(jnp.int32), axis=1) - 1
    made = {}
    for causal, last, size in ((c, l, k) for c, l in ((False, end), (True, spots)) for k in (CF, CK)):
        keys = pos.reshape(-1, size)
        live = (begin.reshape(-1, BQ).min(1)[:, None] <= keys.max(1)[None, :]) & (
            last.reshape(-1, BQ).max(1)[:, None] >= keys.min(1)[None, :]
        )
        starts = jnp.stack([start, other_start]).astype(jnp.int32)
        act = jnp.concatenate([starts, live.astype(jnp.int32).reshape(-1)])
        made[causal, size] = (act, jnp.pad(jnp.stack([begin, last]), ((0, 6), (0, 0))))
    return made


def attend(masks, causal, q, kv, kv_oth):
    n, width = q.shape
    pairs = width // (2 * HEAD)
    return pl.pallas_call(
        attend_kernel,
        out_shape=[
            jax.ShapeDtypeStruct((n, width), jnp.bfloat16),
            jax.ShapeDtypeStruct((n // BQ, pairs, 1, 2 * BQ), jnp.float32),
        ],
        in_specs=[SCALAR] + [ONCHIP] * 2 + [ANY] * 2,
        out_specs=[ONCHIP, ONCHIP],
        scratch_shapes=[
            pltpu.VMEM((2 * n, width), jnp.bfloat16),
            pltpu.VMEM((2 * n, width), jnp.bfloat16),
            pltpu.VMEM((pairs, 2 * n // CF, 2 * BQ, CF), jnp.float32),
            pltpu.VMEM((pairs, 2 * BQ, 128), jnp.bfloat16),
            pltpu.VMEM((pairs, 2 * BQ, 128), jnp.float32),
            pltpu.VMEM((pairs, 2 * BQ, 128), jnp.float32),
            pltpu.VMEM((pairs, 2 * BQ, 128), jnp.float32),
            pltpu.SemaphoreType.DMA((2,)),
            pltpu.SemaphoreType.DMA((2,)),
        ],
        cost_estimate=LIGHT,
        name="attend",
    )(*masks[causal, CF], q, kv, kv_oth)


def attend_back(masks, causal, q, kv, kv_oth, o, lse, grad):
    n, width = q.shape
    pairs = width // (2 * HEAD)
    chunks = 2 * n // CK
    return pl.pallas_call(
        attend_back_kernel,
        out_shape=[
            jax.ShapeDtypeStruct((n, width), jnp.bfloat16),
            jax.ShapeDtypeStruct((2, n, width), jnp.float32),
            jax.ShapeDtypeStruct((2, n, width), jnp.float32),
        ],
        in_specs=[SCALAR] + [ONCHIP] * 2 + [ANY] * 2 + [ONCHIP] * 3,
        out_specs=[ONCHIP] * 3,
        scratch_shapes=[
            pltpu.VMEM((2 * n, width), jnp.bfloat16),
            pltpu.VMEM((2 * n, width), jnp.bfloat16),
            pltpu.VMEM((chunks, pairs, 128, CK), jnp.bfloat16),
            pltpu.VMEM((pairs, 2 * BQ, 128), jnp.bfloat16),
            pltpu.VMEM((pairs, 2 * BQ, 128), jnp.bfloat16),
            pltpu.VMEM((pairs, 1, 2 * BQ), jnp.float32),
            pltpu.VMEM((pairs, 128, 2 * BQ), jnp.float32),
            pltpu.SemaphoreType.DMA((2,)),
            pltpu.SemaphoreType.DMA((2,)),
        ],
        cost_estimate=LIGHT,
        name="attend_back",
    )(*masks[causal, CK], q, kv, kv_oth, o, lse, grad)


def rms(v, gain):
    scale = lax.rsqrt(jnp.mean(v * v, axis=-1, keepdims=True) + NORM_EPS)
    return v * scale * gain


def rms_back(v, gain, grad):
    scale = lax.rsqrt(jnp.mean(v * v, axis=-1, keepdims=True) + NORM_EPS)
    scaled = grad * gain
    lean = jnp.mean(scaled * v, axis=-1, keepdims=True) * (scale * scale * scale)
    return scaled * scale - v * lean, jnp.sum(grad * v * scale, axis=0, keepdims=True)


def project_kernel(x, gain, w, normed, q, kv):
    a = low(rms(x[...], gain[...]))
    normed[...] = a
    q[...] = low(dot32(a, w[0], NN))
    kv[0] = low(dot32(a, w[1], NN))
    kv[1] = low(dot32(a, w[2], NN))


def pair_kernel(memory, w, kv):
    m = memory[...]
    kv[0] = low(dot32(m, w[1], NN))
    kv[1] = low(dot32(m, w[2], NN))


def between_kernel(o, w_out, x, gain, w, y, normed, q):
    state = x[...] + dot32(o[...], w_out[0], NN)
    y[...] = state
    c = low(rms(state, gain[...]))
    normed[...] = c
    q[...] = low(dot32(c, w[0], NN))


def feed_kernel(o, w_out, x, gain, w_up, w_down, y, normed, hidden, z):
    state = x[...] + dot32(o[...], w_out[0], NN)
    y[...] = state
    f = low(rms(state, gain[...]))
    normed[...] = f
    for i in range(w_up.shape[0]):
        r = low(jnp.maximum(dot32(f, w_up[i], NN), 0.0))
        hidden[i] = r
        state = state + dot32(r, w_down[i], NN)
    z[...] = state


def out_back(g, o, w_out, grad_o, grad_out):
    grad_o[...] = low(dot32(g, w_out[0], NT))
    grad_out[0] = low(dot32(o[...], g, TN))


def feed_back_kernel(
    grad, y, normed, hidden, gain, w_up, w_down, o, w_out,
    grad_up, grad_down, grad_y, grad_gain, grad_o, grad_out,
):
    g = low(grad[...])
    f = normed[...]
    back = jnp.zeros(grad.shape, jnp.float32)
    for i in range(w_up.shape[0]):
        r = hidden[i]
        grad_down[i] = low(dot32(r, g, TN))
        h = low(jnp.where(r > 0, dot32(g, w_down[i], NT), 0.0))
        grad_up[i] = low(dot32(f, h, TN))
        back = back + dot32(h, w_up[i], NT)
    more, grad_gain[...] = rms_back(y[...], gain[...], back)
    total = grad[...] + more
    grad_y[...] = total
    out_back(low(total), o, w_out, grad_o, grad_out)


def between_back_kernel(
    grad_q, normed, y, gain, w, grad, o, w_out,
    grad_w, grad_x, grad_gain, grad_o, grad_out,
):
    g = grad_q[...]
    grad_w[0] = low(dot32(normed[...], g, TN))
    more, grad_gain[...] = rms_back(y[...], gain[...], dot32(g, w[0], NT))
    total = grad[...] + more
    grad_x[...] = total
    out_back(low(total), o, w_out, grad_o, grad_out)


def memory_back_kernel(own, other, memory, w, grad_w, grad_memory):
    m = memory[...]
    total = None
    for i in range(2):
        g = low(own[i] + other[i])
        grad_w[i] = low(dot32(m, g, TN))
        part = dot32(g, w[i + 1], NT)
        total = part if total is None else total + part
    grad_memory[...] = total


def project_back_kernel(
    grad_q, own, other, normed, x, gain, w, grad,
    grad_w, grad_x, grad_gain,
):
    a = normed[...]
    back = None
    for i in range(3):
        g = grad_q[...] if i == 0 else low(own[i - 1] + other[i - 1])
        grad_w[i] = low(dot32(a, g, TN))
        part = dot32(g, w[i], NT)
        back = part if back is None else back + part
    more, grad_gain[...] = rms_back(x[...], gain[...], back)
    grad_x[...] = grad[...] + more


def on_chip(kernel, name, outs, *args):
    return pl.pallas_call(
        kernel,
        out_shape=[jax.ShapeDtypeStruct(shape, kind) for shape, kind in outs],
        in_specs=[ONCHIP] * len(args),
        out_specs=[ONCHIP] * len(outs),
        cost_estimate=LIGHT,
        name=name,
    )(*args)


def shaped(lead, like, kind):
    return (lead + like.shape, kind)


def attend_forward(masks, causal, q, kv):
    other = flip(kv, "c")
    o, lse = attend(masks, causal, q, kv, other)
    return o, (q, kv, other, o, lse)


def attend_backward(saved, masks, causal, grad):
    grad_q, own, other = attend_back(masks, causal, *saved, grad)
    return grad_q, own, flip(other, "c")


def project(x, gain, w):
    return on_chip(
        project_kernel,
        "project",
        [shaped((), x, HALF), shaped((), x, HALF), shaped((2,), x, HALF)],
        x, gain[None], w,
    )


def memory_pair(memory, w):
    return on_chip(pair_kernel, "memory_pair", [shaped((2,), memory, HALF)], memory, w)[0]


def between(o, w_out, x, gain, w):
    return on_chip(
        between_kernel,
        "between",
        [shaped((), x, FULL), shaped((), x, HALF), shaped((), x, HALF)],
        o, w_out, x, gain[None], w,
    )


def feed(o, w_out, x, gain, w_up, w_down):
    return on_chip(
        feed_kernel,
        "feed",
        [
            shaped((), x, FULL),
            shaped((), x, HALF),
            shaped((w_up.shape[0],), x, HALF),
            shaped((), x, FULL),
        ],
        o, w_out, x, gain[None], w_up, w_down,
    )


def feed_back(grad, kept, gain, w_up, w_down, o, w_out):
    y, normed, hidden = kept
    return on_chip(
        feed_back_kernel,
        "feed_back",
        [
            (w_up.shape, HALF),
            (w_down.shape, HALF),
            shaped((), y, FULL),
            ((1, y.shape[1]), FULL),
            shaped((), y, HALF),
            (w_out.shape, HALF),
        ],
        grad, y, normed, hidden, gain[None], w_up, w_down, o, w_out,
    )


def between_back(grad_q, normed, y, gain, w, grad, o, w_out):
    return on_chip(
        between_back_kernel,
        "between_back",
        [
            (w_out.shape, HALF),
            shaped((), y, FULL),
            ((1, y.shape[1]), FULL),
            shaped((), y, HALF),
            (w_out.shape, HALF),
        ],
        grad_q, normed, y, gain[None], w, grad, o, w_out,
    )


def memory_back(own, other, memory, w):
    return on_chip(
        memory_back_kernel,
        "memory_back",
        [((2,) + w.shape[1:], HALF), shaped((), memory, FULL)],
        own, other, memory, w,
    )


def project_back(grad_q, own, other, normed, x, gain, w, grad):
    return on_chip(
        project_back_kernel,
        "project_back",
        [(w.shape, HALF), shaped((), x, FULL), ((1, x.shape[1]), FULL)],
        grad_q, own, other, normed, x, gain[None], w, grad,
    )


def shards(
    tokens,
    source,
    segments,
    loss_rows,
    targets,
    exit_depth,
    qkv_weight,
    out_weight,
    up_weight,
    down_weight,
    norm_gains,
    embed_table,
    qkv_first,
    out_first,
    up_first,
    down_first,
    gains_first,
    table_first,
    qkv_second,
    out_second,
    up_second,
    down_second,
    gains_second,
    table_second,
):
    sy, sx = lax.axis_index("sy"), lax.axis_index("sx")
    z, c = lax.axis_index("z"), lax.axis_index("c")
    s = sy * 2 + sx
    me = jnp.stack([c, z, s]).astype(jnp.int32)
    owners = lax.axis_size("z") * 2
    tok_dev = tokens.shape[2]
    loss_dev = targets.shape[2]
    voc_dev, width = embed_table.shape
    gain_count, gain_dev = norm_gains.shape
    vocabulary = voc_dev * owners
    root_width = math.sqrt(width)
    half_row = 2 * tok_dev
    unit = qkv_weight.shape[1] // 4
    fast = lax.axis_size("z") == 4 and unit % 16 == 0

    shard_of = {
        "table": embed_table[None],
        "qkv": qkv_weight,
        "out": out_weight,
        "up": up_weight,
        "down": down_weight,
    }
    shard_shapes = {name: array.shape[1:] for name, array in shard_of.items()}
    weights = {}

    def layout(entries):
        kinds = [kind for _, _, kind in entries]
        return kinds, block_counts(entries, shard_shapes, unit)

    def packed(entries):
        return jnp.concatenate(
            [owned_blocks(low(shard_of[name][i]), kind, unit) for name, i, kind in entries]
        )

    def gather(entries):
        mover = Mover()
        mover.stages = gather_stages(mover, me, packed(entries), *layout(entries), unit, owners)
        return mover

    def settle(entries, outs):
        for (name, i, kind), out in zip(entries, outs):
            weights[name, i] = out.reshape(-1, COL, COL) if kind == "blk" else out

    def gather_plainly(entries):
        everything = lax.all_gather(packed(entries), LINE)
        outs = []
        first = 0
        for kind, count in zip(*layout(entries)):
            piece = everything[:, first : first + count]
            first += count
            if kind == "row":
                outs.append(piece.transpose(1, 0, 2, 3).reshape(count, -1, COL))
            else:
                outs.append(piece.reshape(owners, count, 4, unit, COL).transpose(0, 2, 1, 3, 4))
        settle(entries, outs)

    def pieces(entries):
        arrays, kinds, counts = [], [], []
        for (name, i, kind), count in zip(entries, layout(entries)[1]):
            held = grads[name, i]
            for array in held if isinstance(held, tuple) else (held,):
                blocks = array.shape[0] if isinstance(held, tuple) else count
                arrays.append(array.reshape(natural_shape(kind, blocks, unit, owners)))
                kinds.append(kind)
                counts.append(blocks)
        return arrays, kinds, counts

    def reduce(entries, stages=reduce_stages):
        arrays, kinds, counts = pieces(entries)
        mover = Mover()
        mover.stages = stages(mover, me, arrays, kinds, counts, unit)
        return mover

    def take(entries, parts):
        first = 0
        for (name, i, kind), count in zip(entries, layout(entries)[1]):
            reduced[name, i] = owned_natural(parts[:, first : first + count], kind)
            first += count

    def reduce_plainly(entries):
        parts = []
        for array, kind, count in zip(*pieces(entries)):
            if kind == "row":
                array = array.reshape(count, owners, 4, unit, COL).transpose(1, 2, 0, 3, 4)
            parts.append(wide(array))
        total = jnp.concatenate(parts, axis=2)
        total = lax.psum_scatter(total, LINE, scatter_dimension=0, tiled=True)
        total = lax.psum(total, PLANE)[0]
        take(entries, total)
        return jnp.sum(total * total) / 4.0

    if fast:
        first = gather(GATHERED[0])
        ints = [tokens, source, segments, loss_rows, targets, exit_depth]
        ints, shard_of = step((ints, shard_of), first)
        tokens, source, segments, loss_rows, targets, exit_depth = ints
        second = gather(GATHERED[1])

        def gather_long(entries):
            return jnp.concatenate(
                [quarter_blocks(shard_of[name][i], kind, unit, s) for name, i, kind in entries]
            )

        third, fourth = gather_long(GATHERED[2]), gather_long(GATHERED[3])
    if not fast:
        for entries in GATHERED:
            gather_plainly(entries)

    numbers = jnp.concatenate(
        [array[:, 0] for array in (tokens, source, segments, loss_rows, targets, exit_depth)],
        axis=1,
    )
    plane = gathered(gathered(numbers, "c"), PLANE)
    depths_seen = plane[..., 3 * tok_dev + 2 * loss_dev :]
    reached = jnp.stack(
        [
            jnp.sum((depths_seen >= layer_id).astype(jnp.float32), axis=(0, 1, 3))
            for layer_id in range(LAYERS)
        ],
        axis=1,
    )
    gains_now = norm_gains
    if fast:
        reached, gains_now, third = step((reached, gains_now, third), first)
        third = lax.all_gather(third, PLANE + LINE).reshape(4, owners, *third.shape)
        reached, gains_now = step((reached, gains_now), second)
    small = jnp.concatenate([gains_now.reshape(-1), reached.reshape(-1)])
    small = gathered(gathered(small, "c"), "z").reshape(owners, -1)
    reach = jnp.maximum(
        jnp.sum(small[::2, gain_count * gain_dev :], axis=0).reshape(MICRO, LAYERS), 1.0
    )
    reach = lax.dynamic_index_in_dim(reach, sy, 0, False)
    gains_seen = small[:, : gain_count * gain_dev].reshape(owners, gain_count, gain_dev)
    order = jnp.arange(owners)
    rel = ((order // 2) ^ z) * 2 + ((order % 2) ^ c)
    gains_full = gains_seen[rel].transpose(1, 0, 2).reshape(gain_count, width)
    gains_full = wide(low(gains_full))

    row = lax.dynamic_index_in_dim(plane, sx ^ c, 1, False)
    row = in_order(lax.dynamic_index_in_dim(row, sy, 1, False), s)
    mine = lax.dynamic_slice_in_dim(row, 2 * c, 2, 0)
    theirs = lax.dynamic_slice_in_dim(row, 2 * (1 - c), 2, 0)
    target_ids = mine[:, :tok_dev].reshape(-1)
    source_ids = mine[:, tok_dev : 2 * tok_dev].reshape(-1)
    sentence = mine[:, 2 * tok_dev : 3 * tok_dev].reshape(-1)
    other_sentence = theirs[:, 2 * tok_dev : 3 * tok_dev].reshape(-1)
    rest = 3 * tok_dev
    places = (
        mine[:, rest : rest + loss_dev] + (jnp.arange(2, dtype=jnp.int32) * tok_dev)[:, None]
    ).reshape(-1)
    wanted = mine[:, rest + loss_dev : rest + 2 * loss_dev].reshape(-1)
    depth = mine[:, rest + 2 * loss_dev : rest + 3 * loss_dev].reshape(-1)
    masks = attend_masks(sentence, other_sentence, c * half_row, (1 - c) * half_row)

    ids = jnp.concatenate([source_ids, target_ids])
    if fast:
        ids, small = step((ids, small), first)
        ids = step(ids, second, first)
        settle(GATHERED[0], first.result)
    table = weights["table", 0].reshape(vocabulary, width)
    looked_up = table[ids].astype(jnp.float32) * root_width
    xe = looked_up[:half_row]
    x = looked_up[half_row:]
    kept_enc = (xe, *project(xe, gains_full[0], weights["qkv", 0]))
    if fast:
        xe, kept_enc, x = step((xe, kept_enc, x), second)
    o, saved_enc = attend_forward(masks, False, *kept_enc[2:])
    if fast:
        o, fourth = step((o, fourth), second)
        fourth = lax.all_gather(fourth, PLANE + LINE).reshape(4, owners, *fourth.shape)
        settle(GATHERED[1], second.result)
    *kept_enc_feed, xe = feed(
        o, weights["out", 0], xe, gains_full[1], weights["up", 0], weights["down", 0]
    )
    final_gain = gains_full[2 * ENC]
    memory = low(normalize(xe, final_gain))
    kept = []
    states = []
    for layer_id in range(LAYERS):
        base = 2 * ENC + 1 + 4 * layer_id
        slot = ENC + 2 * layer_id
        if fast and layer_id == 0:
            (x, memory), third = hold((x, memory), third)
            settle(GATHERED[2], unpack(third, *layout(GATHERED[2]), unit, owners))
        kept_self = (x, *project(x, gains_full[base], weights["qkv", slot]))
        o, saved_self = attend_forward(masks, True, *kept_self[2:])
        if fast and layer_id == 1:
            o, fourth = hold(o, fourth)
            settle(GATHERED[3], unpack(fourth, *layout(GATHERED[3]), unit, owners))
        cross = weights["qkv", slot + 1]
        pair = memory_pair(memory, cross)
        *kept_cross, q = between(o, weights["out", slot], x, gains_full[base + 1], cross)
        o, saved_cross = attend_forward(masks, False, q, pair)
        feed_at = ENC + layer_id
        *kept_feed, x = feed(
            o,
            weights["out", slot + 1],
            kept_cross[0],
            gains_full[base + 2],
            weights["up", feed_at],
            weights["down", feed_at],
        )
        kept.append((kept_self, saved_self, kept_cross, saved_cross, kept_feed))
        states.append(x)

    pick = (places[:, None] == jnp.arange(half_row)[None, :]).astype(jnp.bfloat16)
    exit_gains = [gains_full[2 * ENC + 4 + 4 * layer_id] for layer_id in range(LAYERS)]
    exits = jnp.concatenate(
        [low(product(pick, low(normalize(states[i], exit_gains[i])))) for i in range(LAYERS)]
    )
    logits = against_rows(exits, table) * LOGIT_SCALE
    wanted_all = jnp.concatenate([wanted] * LAYERS)
    hit = jnp.arange(vocabulary)[None, :] == wanted_all[:, None]
    picked = jnp.sum(jnp.where(hit, logits, 0.0), axis=-1)
    top = jnp.max(logits, axis=-1)
    lse = top + jnp.log(jnp.sum(jnp.exp(logits - top[:, None]), axis=-1))
    shares = jnp.concatenate(
        [(depth >= i).astype(jnp.float32) / reach[i] / MICRO for i in range(LAYERS)]
    )
    loss_part = jnp.sum((lse - picked) * shares)
    grad_logits = low(
        (jnp.exp(logits - lse[:, None]) - hit.astype(jnp.float32))
        * shares[:, None]
        * LOGIT_SCALE
    )
    grad_exits = product(grad_logits, table)
    table_grad = outer_sum(grad_logits, exits)

    grads = {}
    gain_parts = [None] * gain_count
    grad_x = None
    grad_memory = None
    for layer_id in reversed(range(LAYERS)):
        slot = ENC + 2 * layer_id
        base = 2 * ENC + 1 + 4 * layer_id
        count = places.shape[0]
        grad_rows = lax.dot_general(
            wide(pick),
            grad_exits[layer_id * count : (layer_id + 1) * count],
            (((0,), (0,)), ((), ())),
            precision=lax.Precision.HIGHEST,
            preferred_element_type=jnp.float32,
        )
        grad_here, gain_parts[base + 3] = norm_back(
            states[layer_id], exit_gains[layer_id], grad_rows
        )
        grad_x = grad_here if grad_x is None else grad_x + grad_here
        kept_self, saved_self, kept_cross, saved_cross, kept_feed = kept[layer_id]
        up, down = ("up", ENC + layer_id), ("down", ENC + layer_id)
        qkv, out = ("qkv", slot + 1), ("out", slot + 1)
        grads[up], grads[down], grad_x, gain_parts[base + 2], grad_o, grads[out] = feed_back(
            grad_x,
            kept_feed,
            gains_full[base + 2],
            weights[up],
            weights[down],
            saved_cross[3],
            weights[out],
        )
        if fast and layer_id == 1:
            feed_mover = reduce(REDUCED[0], long_reduce_stages)
            grad_x, grad_o = step((grad_x, grad_o), feed_mover, feed_mover)
        if fast and layer_id == 0:
            late = reduce(REDUCED[1], long_reduce_stages)
            grad_x, grad_o = step((grad_x, grad_o), feed_mover, late, late)
        grad_q, own, other = attend_backward(saved_cross, masks, False, grad_o)
        grad_pair, more = memory_back(own, other, memory, weights[qkv])
        grad_memory = more if grad_memory is None else grad_memory + more
        out = ("out", slot)
        grad_query, grad_x, gain_parts[base + 1], grad_o, grads[out] = between_back(
            grad_q,
            kept_cross[1],
            kept_cross[0],
            gains_full[base + 1],
            weights[qkv],
            grad_x,
            saved_self[3],
            weights[out],
        )
        grads[qkv] = (grad_query, grad_pair)
        grad_q, own, other = attend_backward(saved_self, masks, True, grad_o)
        qkv = ("qkv", slot)
        grads[qkv], grad_x, gain_parts[base] = project_back(
            grad_q,
            own,
            other,
            kept_self[1],
            kept_self[0],
            gains_full[base],
            weights[qkv],
            grad_x,
        )
    if fast:
        grad_x, grad_memory = step((grad_x, grad_memory), feed_mover)
    grad_enc, gain_parts[2 * ENC] = norm_back(xe, final_gain, grad_memory)
    up, down, qkv, out = ("up", 0), ("down", 0), ("qkv", 0), ("out", 0)
    grads[up], grads[down], grad_enc, gain_parts[1], grad_o, grads[out] = feed_back(
        grad_enc,
        kept_enc_feed,
        gains_full[1],
        weights[up],
        weights[down],
        saved_enc[3],
        weights[out],
    )
    if fast:
        middle = reduce(REDUCED[2], long_reduce_stages)
        grad_enc, grad_o = step((grad_enc, grad_o), middle, late, middle)
    grad_q, own, other = attend_backward(saved_enc, masks, False, grad_o)
    grads[qkv], grad_enc, gain_parts[0] = project_back(
        grad_q, own, other, kept_enc[1], kept_enc[0], gains_full[0], weights[qkv], grad_enc
    )
    token_ids = jnp.concatenate([source_ids, target_ids])
    token_grads = low(jnp.concatenate([grad_enc, grad_x]) * root_width)
    looked = (token_ids[:, None] == jnp.arange(vocabulary)[None, :]).astype(jnp.bfloat16)
    table_grad = low(table_grad + outer_sum(looked, token_grads))
    grads["table", 0] = table_grad

    gain_grad = jnp.concatenate([part.reshape(1, -1) for part in gain_parts])
    small = jnp.concatenate([gain_grad, jnp.full((1, width), loss_part)])

    reduced = {}
    if fast:
        last = reduce(REDUCED[3])
        tiny = Mover()
        tiny.stages = small_stages(tiny, small, z)
        loss_part = step(loss_part, last, tiny)
        loss_part = step(loss_part, last, tiny)
        loss_part = step(loss_part, last, tiny, middle)
        loss_part = step(loss_part, last, tiny)
        movers = (feed_mover, late, middle, last)
        loss_part = step(loss_part, last, tiny)
        gain_grad, loss_total = tiny.result[:-1], tiny.result[-1, 0]
        squares = all_sum(sum(mover.squares for mover in movers))
        squares = step(squares, late, middle, last)
    else:
        small = all_sum(small)
        gain_grad, loss_total = small[:-1], small[-1, 0]
        squares = all_sum(sum(reduce_plainly(entries) for entries in REDUCED))
    squares = squares + jnp.sum(gain_grad * gain_grad)
    grad_norm = jnp.sqrt(squares)
    clip_factor = CLIP_NORM / jnp.maximum(grad_norm, CLIP_NORM)

    names = ("qkv", "out", "up", "down", "table")
    if fast:
        plan = []
        for bucket, entries in enumerate(REDUCED):
            first = 0
            for (name, i, kind), count in zip(entries, layout(entries)[1]):
                plan.append((bucket, first, count, kind, names.index(name), i))
                first += count
        parts = [part for mover in movers for part in mover.result]
        shapes = [shard_of[name].shape for name in names]
        placed = pl.pallas_call(
            functools.partial(settle_kernel, len(parts), tuple(plan), unit),
            out_shape=[jax.ShapeDtypeStruct(shape, jnp.bfloat16) for shape in shapes],
            in_specs=[SCALAR] + [ANY] * len(parts),
            out_specs=[ONCHIP] * len(shapes),
            scratch_shapes=[pltpu.SemaphoreType.DMA((len(shapes),))],
            cost_estimate=LIGHT,
            name="place_gradients",
        )(me, *parts)
        ready = [wide(array) for array in placed]
    else:
        ready = [
            wide(jnp.stack([reduced[name, i] for i in range(shard_of[name].shape[0])]))
            for name in names
        ]
    gradients = (
        *ready[:4],
        lax.dynamic_slice_in_dim(gain_grad, (2 * z + c) * gain_dev, gain_dev, 1),
        ready[4][0],
    )
    masters = (qkv_weight, out_weight, up_weight, down_weight, norm_gains, embed_table)
    firsts = (qkv_first, out_first, up_first, down_first, gains_first, table_first)
    seconds = (qkv_second, out_second, up_second, down_second, gains_second, table_second)
    results = [
        adam_update(masters[i], firsts[i], seconds[i], gradients[i] * clip_factor) for i in range(6)
    ]
    gains_grad = gradients[4] * clip_factor
    return (
        loss_total,
        grad_norm,
        results[0][0],
        results[1][0],
        results[2][0],
        results[3][0],
        gains_grad,
        results[5][0],
        results[0][1],
        results[1][1],
        results[2][1],
        results[3][1],
        results[4][1],
        results[5][1],
        results[0][2],
        results[1][2],
        results[2][2],
        results[3][2],
        results[4][2],
        results[5][2],
    )


def solution(mesh):
    seq, vocab = mesh.devices.shape
    fine = Mesh(mesh.devices.reshape(2, seq // 2, vocab // 2, 2), ("sy", "sx", "z", "c"))
    ints = P(None, LINE, PLANE)
    block = P(None, LINE, None)
    gains = P(None, LINE)
    rows = P(LINE, None)
    arrays = (block, block, block, block, gains, rows)
    return jax.shard_map(
        shards,
        mesh=fine,
        in_specs=(ints,) * 6 + arrays * 3,
        out_specs=(P(), P(), block, block, block, block, gains, rows) + arrays * 2,
        check_vma=False,
    )
```

```python
import functools
import math

import jax
import jax.numpy as jnp
from jax import lax
from jax.experimental import pallas as pl
from jax.experimental.pallas import tpu as pltpu
from jax.sharding import Mesh
from jax.sharding import PartitionSpec as P

HEADS = 8
HEAD = 64
ENC = 1
LAYERS = 2
MICRO = 2
COL = 512
HALF, FULL = jnp.bfloat16, jnp.float32

NORM_EPS = 1e-06
CLIP_NORM = 0.01
LEARN_RATE = 0.05
BETA_ONE = 0.9
BETA_TWO = 0.999
ADAM_EPS = 1e-08
WEIGHT_DECAY = 0.01
ADAM_STEP = 10
LOGIT_SCALE = 4.0
NEGATIVE = -1e30

PLANE = ("sy", "sx")
LINE = ("z", "c")

TABLE = ("table", 0, "blk")


def attention_parts(i):
    return (("qkv", i, "row"), ("out", i, "row"))


def feed_parts(i):
    return (("up", i, "row"), ("down", i, "blk"))


GATHERED = (
    (TABLE,) + attention_parts(0),
    feed_parts(0),
    attention_parts(1) + attention_parts(2) + feed_parts(1) + attention_parts(3),
    attention_parts(4) + feed_parts(2),
)
REDUCED = (
    feed_parts(2),
    attention_parts(3) + attention_parts(4) + feed_parts(1),
    attention_parts(1) + attention_parts(2) + feed_parts(0),
    (TABLE,) + attention_parts(0),
)


def flip(x, axis, bit=1):
    if isinstance(axis, tuple):
        n = math.prod(lax.axis_size(a) for a in axis)
    else:
        n = lax.axis_size(axis)
    return lax.ppermute(x, axis, [(i, i ^ bit) for i in range(n)])


def bits(axis):
    n = lax.axis_size(axis)
    return [1 << k for k in range(n.bit_length() - 1)]


def gathered(x, axis):
    if isinstance(axis, tuple) or lax.axis_size(axis) <= 4:
        n = 4 if isinstance(axis, tuple) else lax.axis_size(axis)
        return jnp.stack([x] + [flip(x, axis, r) for r in range(1, n)])
    x = x[None]
    for bit in bits(axis):
        x = jnp.concatenate([x, flip(x, axis, bit)], axis=0)
    return x


def in_order(blocks, index):
    n = blocks.shape[0]
    return jnp.concatenate(
        [lax.dynamic_index_in_dim(blocks, i ^ index, 0, keepdims=True) for i in range(n)]
    )


def all_sum(x):
    for axis in ("c", "sx", "sy", "z"):
        for bit in bits(axis):
            x = x + flip(x, axis, bit)
    return x


def hold(carry, things):
    return lax.optimization_barrier((carry, things))


def step(carry, *movers):
    for mover in movers:
        carry, (mover.held, mover.arrived) = hold(carry, (mover.held, mover.arrived))
        leaving = next(mover.stages)
        carry, (arrays, mover.held) = hold(carry, ([array for array, _ in leaving], mover.held))
        mover.arrived = [
            flip(array, *route)
            if route
            else lax.psum_scatter(array, PLANE + ("z",), scatter_dimension=0, tiled=True)
            for array, (_, route) in zip(arrays, leaving)
        ]
    return carry


class Mover:
    def __init__(self):
        self.held = []
        self.arrived = []


def normalize(v, g):
    return v * lax.rsqrt(jnp.mean(v * v, axis=-1, keepdims=True) + NORM_EPS) * g


def norm_back(v, g, cotangent):
    _, pullback = jax.vjp(normalize, v, g)
    return pullback(cotangent)


def product(a, b):
    return jnp.dot(a, b, preferred_element_type=jnp.float32)


def outer_sum(a, b):
    return lax.dot_general(a, b, (((0,), (0,)), ((), ())), preferred_element_type=jnp.float32)


def against_rows(a, b):
    return lax.dot_general(a, b, (((1,), (1,)), ((), ())), preferred_element_type=jnp.float32)


def split_heads(v):
    return v.reshape(v.shape[0], HEADS, HEAD)


def low(v):
    return v.astype(jnp.bfloat16)


def wide(v):
    return v.astype(jnp.float32)


def adam_update(master, first, second, grad):
    first = BETA_ONE * first + (1.0 - BETA_ONE) * grad
    second = BETA_TWO * second + (1.0 - BETA_TWO) * grad * grad
    fixed_first = first / (1.0 - BETA_ONE**ADAM_STEP)
    fixed_second = second / (1.0 - BETA_TWO**ADAM_STEP)
    master = master - LEARN_RATE * (
        fixed_first / (jnp.sqrt(fixed_second) + ADAM_EPS) + WEIGHT_DECAY * master
    )
    return (master, first, second)


def owned_blocks(array, kind, unit):
    if kind == "row":
        rows, columns = array.shape
        return array.reshape(rows, columns // COL, COL).transpose(1, 0, 2)
    rows = array.shape[0]
    per = rows // (4 * unit)
    return array.reshape(4, per, unit, COL).transpose(1, 0, 2, 3).reshape(per, 4 * unit, COL)


def quarter_blocks(array, kind, unit, s):
    size = array.shape[0] // 4
    array = lax.dynamic_slice_in_dim(array, s * size, size, axis=0)
    if kind == "row":
        return low(array).reshape(unit, -1, COL).transpose(1, 0, 2)
    return low(array).reshape(-1, unit, COL)


def block_counts(entries, shard_shapes, unit):
    counts = []
    for name, _, kind in entries:
        rows, columns = shard_shapes[name]
        counts.append(columns // COL if kind == "row" else rows // (4 * unit))
    return counts


def natural_shape(kind, count, unit, owners):
    if kind == "row":
        return (count, owners * 4 * unit, COL)
    return (owners, 4, count, unit, COL)


def scatter_kernel(plan, unit, me_ref, *refs):
    pieces, outs, sem = refs[:10], refs[10:-1], refs[-1]
    c, z, s = me_ref[0], me_ref[1], me_ref[2]

    def put(out, kind, owner, part, rows, source):
        if kind == "row":
            start = pl.multiple_of(owner * (4 * unit) + part * unit, unit)
            target = outs[out].at[:, pl.ds(start, rows), :]
        else:
            target = outs[out].at[owner, part]
        pltpu.make_async_copy(source, target, sem.at[out]).start()

    for c_rel in range(2):
        shard, *quarters = pieces[5 * c_rel : 5 * c_rel + 5]
        for z_rel in range(4):
            owner = (z ^ z_rel) * 2 + (c ^ c_rel)
            for out, (kind, first, count) in enumerate(plan):
                last = first + count
                if z_rel == 0:
                    if kind == "row":
                        put(out, kind, owner, 0, 4 * unit, shard.at[first:last])
                    else:
                        for part in range(4):
                            rows = pl.ds(part * unit, unit)
                            put(out, kind, owner, part, unit, shard.at[first:last, rows, :])
                else:
                    for s_rel, quarter in enumerate(quarters):
                        put(out, kind, owner, s ^ s_rel, unit, quarter.at[z_rel - 1, first:last])
    for out in range(len(plan)):
        pltpu.make_async_copy(outs[out], outs[out], sem.at[out]).wait()


def collect_kernel(plan, unit, ordered, me_ref, *refs):
    grads, keep, send, sem = refs[: len(plan)], refs[len(plan)], refs[len(plan) + 1], refs[-1]
    c, z, s = me_ref[0], me_ref[1], me_ref[2]
    for c_rel, out in ((0, keep), (1, send)):
        for z_rel in range(4):
            owner = (z ^ z_rel) * 2 + (c ^ c_rel)
            for s_rel in range(4):
                part = s ^ s_rel
                for grad, (kind, first, count) in zip(grads, plan):
                    if kind == "row":
                        start = pl.multiple_of(owner * (4 * unit) + part * unit, unit)
                        source = grad.at[:, pl.ds(start, unit), :]
                    else:
                        source = grad.at[owner, part]
                    place = (part, z ^ z_rel) if ordered else (s_rel, z_rel)
                    target = out.at[*place, first : first + count]
                    pltpu.make_async_copy(source, target, sem.at[c_rel]).start()
    for c_rel, out in ((0, keep), (1, send)):
        pltpu.make_async_copy(out, out, sem.at[c_rel]).wait()


LIGHT = pl.CostEstimate(flops=1, bytes_accessed=1, transcendentals=0)
ANY = pl.BlockSpec(memory_space=pl.ANY)
ONCHIP = pl.BlockSpec(memory_space=pltpu.VMEM)
SCALAR = pl.BlockSpec(memory_space=pltpu.SMEM)


def gather_stages(mover, me, shard, kinds, counts, unit, owners):
    starts = [sum(counts[:i]) for i in range(len(counts))]
    mover.held = [shard]
    part = lax.dynamic_slice_in_dim(shard, me[2] * unit, unit, axis=1)
    yield [(part, ("z", bit)) for bit in (1, 2, 3)]
    mine = jnp.stack(mover.arrived)
    mover.held.append(mine)
    yield [(mine, (PLANE, bit)) for bit in (1, 2, 3)]
    mover.held += mover.arrived
    yield [(piece, ("c",)) for piece in mover.held]
    plan = tuple(zip(kinds, starts, counts))
    mover.result = pl.pallas_call(
        functools.partial(scatter_kernel, plan, unit),
        out_shape=[
            jax.ShapeDtypeStruct(natural_shape(kind, count, unit, owners), jnp.bfloat16)
            for kind, count in zip(kinds, counts)
        ],
        in_specs=[SCALAR] + [ANY] * 10,
        out_specs=[ONCHIP] * len(plan),
        scratch_shapes=[pltpu.SemaphoreType.DMA((len(plan),))],
        cost_estimate=LIGHT,
        name="place_weights",
    )(me, *mover.held, *mover.arrived)
    mover.held = []
    yield []


def unpack_kernel(plan, pieces, *refs):
    outs, sem = refs[:-1], refs[-1]
    for out, (kind, first, count) in enumerate(plan):
        for part in range(4):
            if kind == "blk":
                source = pieces.at[part, :, first : first + count]
                pltpu.make_async_copy(source, outs[out].at[:, part], sem.at[out]).start()
                continue
            for k in range(count):
                source = pieces.at[part, :, first + k]
                pltpu.make_async_copy(source, outs[out].at[k, :, part], sem.at[out]).start()
    for out in range(len(plan)):
        pltpu.make_async_copy(outs[out], outs[out], sem.at[out]).wait()


def unpack(pieces, kinds, counts, unit, owners):
    starts = [sum(counts[:i]) for i in range(len(counts))]
    shapes = [
        (count, owners, 4, unit, COL) if kind == "row" else (owners, 4, count, unit, COL)
        for kind, count in zip(kinds, counts)
    ]
    placed = pl.pallas_call(
        functools.partial(unpack_kernel, tuple(zip(kinds, starts, counts))),
        out_shape=[jax.ShapeDtypeStruct(shape, jnp.bfloat16) for shape in shapes],
        in_specs=[ANY],
        out_specs=[ONCHIP] * len(shapes),
        scratch_shapes=[pltpu.SemaphoreType.DMA((len(shapes),))],
        cost_estimate=LIGHT,
        name="place_gathered",
    )(pieces)
    return [
        out.reshape(count, -1, COL) if kind == "row" else out
        for out, kind, count in zip(placed, kinds, counts)
    ]


def added(arrays):
    total = wide(arrays[0])
    for array in arrays[1:]:
        total = total + wide(array)
    return total


def plane_sum_kernel(keep, core, from_x, from_y, left, right, own, *sends):
    half = left.shape[1]
    for bit in range(4):
        for part, (one, two) in ((slice(0, half), (from_x, left)), (slice(half, None), (from_y, right))):
            total = added([keep[bit, part], core[bit, part], one[bit], two[bit]])
            if bit == 0:
                own[part] = total
            else:
                sends[bit - 1][part] = low(total)


def line_sum_kernel(own, one, two, three, whole, squares):
    total = added([own[...], one[...], two[...], three[...]])
    whole[...] = low(total)
    squares[0, 0] = jnp.sum(total * total)


def collect(me, grads, kinds, counts, unit, ordered):
    starts = [sum(counts[:i]) for i in range(len(counts))]
    plan = tuple(zip(kinds, starts, counts))
    shape = jax.ShapeDtypeStruct((4, 4, sum(counts), unit, COL), jnp.bfloat16)
    return pl.pallas_call(
        functools.partial(collect_kernel, plan, unit, ordered),
        out_shape=[shape, shape],
        in_specs=[SCALAR] + [ANY] * len(plan),
        out_specs=[ONCHIP, ONCHIP],
        scratch_shapes=[pltpu.SemaphoreType.DMA((2,))],
        cost_estimate=LIGHT,
        name="collect_gradients",
    )(me, *grads)


def long_reduce_stages(mover, me, grads, kinds, counts, unit):
    keep, send = collect(me, grads, kinds, counts, unit, True)
    mover.held = [keep]
    yield [(send, ("c",))]
    chip = low(added(mover.held + mover.arrived))
    mover.held = []
    yield [(chip.reshape(16, *chip.shape[2:]), None)]
    own = mover.arrived[0][0]
    mover.squares = jnp.sum(wide(own) * wide(own))
    mover.held = [own]
    yield [(own, (PLANE, bit)) for bit in (1, 2, 3)]
    mover.result = mover.held + mover.arrived
    mover.held = []
    yield []


def reduce_stages(mover, me, grads, kinds, counts, unit):
    total = sum(counts)
    keep, send = collect(me, grads, kinds, counts, unit, False)
    mover.held = [keep]
    half = total // 2
    yield [(send, ("c",))]
    mover.held = [a.reshape(2, 2, *a.shape[1:]) for a in mover.held + mover.arrived]
    yield [
        (low(added([a[:, 1, :, :half] for a in mover.held])), ("sx",)),
        (low(added([a[1, :, :, half:] for a in mover.held])), ("sy",)),
    ]
    mover.held += mover.arrived

    def sides():
        both, (come_x, come_y) = mover.held[:2], mover.held[2:4]
        return (
            [a[:, 0, :, :half] for a in both] + [come_x],
            [a[0, :, :, half:] for a in both] + [come_y],
        )

    left, right = sides()
    yield [(low(added([a[1] for a in left])), ("sy",)), (low(added([a[1] for a in right])), ("sx",))]
    mover.held += mover.arrived

    block = (total, unit, COL)
    first_part = pl.BlockSpec((None, None, 4, *block), lambda i: (0, 0, 0, 0, 0, 0))
    half_part = [pl.BlockSpec((None, 4, n, unit, COL), lambda i: (0, 0, 0, 0, 0)) for n in (half, total - half)]
    own, *sends = pl.pallas_call(
        plane_sum_kernel,
        grid=(1,),
        out_shape=[jax.ShapeDtypeStruct(block, FULL)] + [jax.ShapeDtypeStruct(block, HALF)] * 3,
        in_specs=[first_part, first_part, *half_part, ONCHIP, ONCHIP],
        out_specs=[ONCHIP] * 4,
        cost_estimate=LIGHT,
        name="plane_sum",
    )(*mover.held)
    mover.held = [own]
    yield [(send, ("z", bit)) for bit, send in zip((1, 2, 3), sends)]
    own, squares = pl.pallas_call(
        line_sum_kernel,
        out_shape=[
            jax.ShapeDtypeStruct(block, HALF),
            jax.ShapeDtypeStruct((1, 1), FULL),
        ],
        in_specs=[ONCHIP] * 4,
        out_specs=[ONCHIP, SCALAR],
        cost_estimate=LIGHT,
        name="line_sum",
    )(*mover.held, *mover.arrived)
    mover.squares = squares[0, 0]
    mover.held = [own]
    yield [(own, (PLANE, bit)) for bit in (1, 2, 3)]
    mover.result = mover.held + mover.arrived
    mover.held = []
    yield []


def small_stages(mover, x, z):
    for axis in ("c", "sx", "sy"):
        mover.held = [x]
        yield [(x, (axis,))]
        x = mover.held[0] + mover.arrived[0]
    mover.held = [x]
    yield [(x, ("z", bit)) for bit in (1, 2, 3)]
    mover.result = jnp.sum(in_order(jnp.stack(mover.held + mover.arrived), z), axis=0)
    yield []


def settle_kernel(sizes, plan, unit, me_ref, *refs):
    buckets, outs, sem = refs[:sizes], refs[sizes:-1], refs[-1]
    s = me_ref[2]
    for bucket, first, count, kind, out, i in plan:
        for s_rel in range(4):
            source = buckets[4 * bucket + s_rel]
            part = s ^ s_rel
            if kind == "blk":
                for k in range(count):
                    start = pl.multiple_of((part * count + k) * unit, unit)
                    target = outs[out].at[i, pl.ds(start, unit), :]
                    pltpu.make_async_copy(source.at[first + k], target, sem.at[out]).start()
                continue
            rows = pl.ds(pl.multiple_of(part * unit, unit), unit)
            for k in range(count):
                target = outs[out].at[i, rows, k * COL : k * COL + COL]
                pltpu.make_async_copy(source.at[first + k], target, sem.at[out]).start()
    for out, ref in enumerate(outs):
        pltpu.make_async_copy(ref, ref, sem.at[out]).wait()


def owned_natural(parts, kind):
    if kind == "row":
        four, count, unit, _ = parts.shape
        return parts.transpose(0, 2, 1, 3).reshape(four * unit, count * COL)
    return parts.reshape(-1, COL)


BQ = 128
CK = 256
CF = 256
NT = (((1,), (1,)), ((), ()))
TN = (((0,), (0,)), ((), ()))
NN = (((1,), (0,)), ((), ()))


def dot32(a, b, dims):
    return lax.dot_general(a, b, dims, preferred_element_type=jnp.float32)


def load_halves(own, other, whole, sem):
    half = whole.shape[0] // 2
    copies = [
        pltpu.make_async_copy(own, whole.at[pl.ds(0, half)], sem.at[0]),
        pltpu.make_async_copy(other, whole.at[pl.ds(half, half)], sem.at[1]),
    ]
    for copy in copies:
        copy.start()
    return copies


def pair_rows(block, scale=None):
    lane = lax.broadcasted_iota(jnp.int32, block.shape, 1)
    zero = jnp.zeros_like(block)
    if scale is not None:
        block = block * jnp.asarray(scale, block.dtype)
    return jnp.concatenate(
        [jnp.where(lane < HEAD, block, zero), jnp.where(lane < HEAD, zero, block)], axis=0
    )


def pair_lanes(stacked):
    rows = stacked.shape[0] // 2
    lane = lax.broadcasted_iota(jnp.int32, (rows, 2 * HEAD), 1)
    return jnp.where(lane < HEAD, stacked[:rows], stacked[rows:])


def open_to(act, bounds, rows, j, chunks):
    half = chunks // 2
    base = jnp.where(j < half, act[0] + j * CK, act[1] + (j - half) * CK)
    spot = base + lax.broadcasted_iota(jnp.int32, (CK, BQ), 0)
    open_ = (spot >= bounds[0:1, rows]) & (spot <= bounds[1:2, rows])
    return jnp.concatenate([open_, open_], axis=1)


def attend_kernel(
    act, bounds, q, kv_own, kv_oth, o, lse,
    k_all, v_all, scores, queries, top, total, acc, sem_k, sem_v,
):
    pairs = q.shape[1] // (2 * HEAD)
    blocks = q.shape[0] // BQ
    chunks = k_all.shape[0] // CF
    half = chunks // 2
    waits = load_halves(kv_own.at[0], kv_oth.at[0], k_all, sem_k)
    waits += load_halves(kv_own.at[1], kv_oth.at[1], v_all, sem_v)
    for copy in waits:
        copy.wait()
    square = lax.broadcasted_iota(jnp.int32, (BQ, BQ), 0)
    along = lax.broadcasted_iota(jnp.int32, (BQ, BQ), 1)

    def one_block(b, _):
        rows = pl.ds(pl.multiple_of(b * BQ, BQ), BQ)
        for h in range(pairs):
            queries[h] = pair_rows(q[rows, h * 128 : h * 128 + 128], HEAD ** (-0.5))
        top[...] = jnp.full_like(top, NEGATIVE)
        total[...] = jnp.zeros_like(total)
        acc[...] = jnp.zeros_like(acc)
        least = jnp.broadcast_to(bounds[0:1, rows], (BQ, BQ)).T
        most = jnp.broadcast_to(bounds[1:2, rows], (BQ, BQ)).T

        def first(j, _):
            @pl.when(act[2 + b * chunks + j] > 0)
            def _():
                keys = pl.ds(pl.multiple_of(j * CF, CF), CF)
                base = jnp.where(j < half, act[0] + j * CF, act[1] + (j - half) * CF)
                open_ = []
                for part in range(CF // 128):
                    spot = base + part * 128 + along
                    one = (spot >= least) & (spot <= most)
                    open_.append(jnp.concatenate([one, one], axis=0))
                for h in range(pairs):
                    s = dot32(queries[h], k_all[keys, h * 128 : h * 128 + 128], NT)
                    best = top[h]
                    for part, one in enumerate(open_):
                        t = jnp.where(one, s[:, part * 128 : part * 128 + 128], NEGATIVE)
                        scores[h, j, :, part * 128 : part * 128 + 128] = t
                        best = jnp.maximum(best, t)
                    top[h] = best

            return 0

        lax.fori_loop(0, chunks, first, 0)
        for h in range(pairs):
            top[h] = jnp.broadcast_to(jnp.max(top[h], axis=1, keepdims=True), top.shape[1:])

        def second(j, _):
            @pl.when(act[2 + b * chunks + j] > 0)
            def _():
                keys = pl.ds(pl.multiple_of(j * CF, CF), CF)
                for h in range(pairs):
                    parts = []
                    more = total[h]
                    for part in range(CF // 128):
                        e = jnp.exp(scores[h, j, :, part * 128 : part * 128 + 128] - top[h])
                        more = more + e
                        parts.append(e.astype(jnp.bfloat16))
                    total[h] = more
                    e = parts[0] if len(parts) == 1 else jnp.concatenate(parts, axis=1)
                    acc[h] = acc[h] + dot32(e, v_all[keys, h * 128 : h * 128 + 128], NN)

            return 0

        lax.fori_loop(0, chunks, second, 0)
        for h in range(pairs):
            denom = jnp.broadcast_to(
                jnp.sum(total[h], axis=1, keepdims=True), total.shape[1:]
            )
            o[rows, h * 128 : h * 128 + 128] = pair_lanes(acc[h] / denom).astype(o.dtype)
            for part in range(2):
                span = slice(part * BQ, part * BQ + BQ)

                def line(level, span=span):
                    own = jnp.where(square == along, level[span], 0.0)
                    return jnp.sum(own, axis=0, keepdims=True)

                lse[b, h, :, span] = line(top[h]) + jnp.log(line(denom))
        return 0

    lax.fori_loop(0, blocks, one_block, 0)


def attend_back_kernel(
    act, bounds, q, kv_own, kv_oth, o, lse, grad,
    grad_q, grad_own, grad_oth,
    k_all, v_all, k_turned, queries, grads, delta, grad_queries, sem_k, sem_v,
):
    pairs = q.shape[1] // (2 * HEAD)
    blocks = q.shape[0] // BQ
    chunks = k_all.shape[0] // CK
    waits = load_halves(kv_own.at[0], kv_oth.at[0], k_all, sem_k)
    waits += load_halves(kv_own.at[1], kv_oth.at[1], v_all, sem_v)
    grad_own[...] = jnp.zeros_like(grad_own)
    grad_oth[...] = jnp.zeros_like(grad_oth)
    for copy in waits:
        copy.wait()

    def turn(j, _):
        for h in range(pairs):
            for part in range(CK // 128):
                keys = pl.ds(pl.multiple_of(j * CK + part * 128, 128), 128)
                k_turned[j, h, :, part * 128 : part * 128 + 128] = k_all[
                    keys, h * 128 : h * 128 + 128
                ].T
        return 0

    lax.fori_loop(0, chunks, turn, 0)

    def one_block(b, _):
        rows = pl.ds(pl.multiple_of(b * BQ, BQ), BQ)
        for h in range(pairs):
            lanes = slice(h * 128, h * 128 + 128)
            queries[h] = pair_rows(q[rows, lanes], HEAD ** (-0.5))
            grads[h] = pair_rows(grad[rows, lanes])
            both = (o[rows, lanes].astype(jnp.float32) * grad[rows, lanes].astype(jnp.float32)).T
            delta[h] = jnp.concatenate(
                [
                    jnp.sum(both[:HEAD], axis=0, keepdims=True),
                    jnp.sum(both[HEAD:], axis=0, keepdims=True),
                ],
                axis=1,
            )
        grad_queries[...] = jnp.zeros_like(grad_queries)

        def one_chunk(j, target, local):
            keys = pl.ds(pl.multiple_of(j * CK, CK), CK)
            own_keys = pl.ds(pl.multiple_of(local * CK, CK), CK)
            open_ = open_to(act, bounds, rows, j, chunks)
            for h in range(pairs):
                lanes = slice(h * 128, h * 128 + 128)
                s = jnp.where(open_, dot32(k_all[keys, lanes], queries[h], NT), NEGATIVE)
                p = jnp.exp(s - lse[b, h])
                ds = p * (dot32(v_all[keys, lanes], grads[h], NT) - delta[h])
                p = p.astype(jnp.bfloat16)
                ds = ds.astype(jnp.bfloat16)
                target[0, own_keys, lanes] += dot32(ds, queries[h], NN)
                target[1, own_keys, lanes] += dot32(p, grads[h], NN)
                grad_queries[h] += dot32(k_turned[j, h], ds, NN)

        def own_chunk(j, _):
            @pl.when(act[2 + b * chunks + j] > 0)
            def _():
                one_chunk(j, grad_own, j)

            return 0

        def oth_chunk(j, _):
            @pl.when(act[2 + b * chunks + j] > 0)
            def _():
                one_chunk(j, grad_oth, j - chunks // 2)

            return 0

        lax.fori_loop(0, chunks // 2, own_chunk, 0)
        lax.fori_loop(chunks // 2, chunks, oth_chunk, 0)
        for h in range(pairs):
            grad_q[rows, h * 128 : h * 128 + 128] = (
                pair_lanes(grad_queries[h].T) * HEAD ** (-0.5)
            ).astype(grad_q.dtype)
        return 0

    lax.fori_loop(0, blocks, one_block, 0)


def attend_masks(sentence, other, start, other_start):
    n = sentence.shape[0]
    seg = jnp.concatenate([sentence, other])
    spots = start + jnp.arange(n, dtype=jnp.int32)
    pos = jnp.concatenate([spots, other_start + jnp.arange(n, dtype=jnp.int32)])
    begin = jnp.sum((seg[None, :] < sentence[:, None]).astype(jnp.int32), axis=1)
    end = jnp.sum((seg[None, :] <= sentence[:, None]).astype(jnp.int32), axis=1) - 1
    made = {}
    for causal, last, size in ((c, l, k) for c, l in ((False, end), (True, spots)) for k in (CF, CK)):
        keys = pos.reshape(-1, size)
        live = (begin.reshape(-1, BQ).min(1)[:, None] <= keys.max(1)[None, :]) & (
            last.reshape(-1, BQ).max(1)[:, None] >= keys.min(1)[None, :]
        )
        starts = jnp.stack([start, other_start]).astype(jnp.int32)
        act = jnp.concatenate([starts, live.astype(jnp.int32).reshape(-1)])
        made[causal, size] = (act, jnp.pad(jnp.stack([begin, last]), ((0, 6), (0, 0))))
    return made


def attend(masks, causal, q, kv, kv_oth):
    n, width = q.shape
    pairs = width // (2 * HEAD)
    return pl.pallas_call(
        attend_kernel,
        out_shape=[
            jax.ShapeDtypeStruct((n, width), jnp.bfloat16),
            jax.ShapeDtypeStruct((n // BQ, pairs, 1, 2 * BQ), jnp.float32),
        ],
        in_specs=[SCALAR] + [ONCHIP] * 2 + [ANY] * 2,
        out_specs=[ONCHIP, ONCHIP],
        scratch_shapes=[
            pltpu.VMEM((2 * n, width), jnp.bfloat16),
            pltpu.VMEM((2 * n, width), jnp.bfloat16),
            pltpu.VMEM((pairs, 2 * n // CF, 2 * BQ, CF), jnp.float32),
            pltpu.VMEM((pairs, 2 * BQ, 128), jnp.bfloat16),
            pltpu.VMEM((pairs, 2 * BQ, 128), jnp.float32),
            pltpu.VMEM((pairs, 2 * BQ, 128), jnp.float32),
            pltpu.VMEM((pairs, 2 * BQ, 128), jnp.float32),
            pltpu.SemaphoreType.DMA((2,)),
            pltpu.SemaphoreType.DMA((2,)),
        ],
        cost_estimate=LIGHT,
        name="attend",
    )(*masks[causal, CF], q, kv, kv_oth)


def attend_back(masks, causal, q, kv, kv_oth, o, lse, grad):
    n, width = q.shape
    pairs = width // (2 * HEAD)
    chunks = 2 * n // CK
    return pl.pallas_call(
        attend_back_kernel,
        out_shape=[
            jax.ShapeDtypeStruct((n, width), jnp.bfloat16),
            jax.ShapeDtypeStruct((2, n, width), jnp.float32),
            jax.ShapeDtypeStruct((2, n, width), jnp.float32),
        ],
        in_specs=[SCALAR] + [ONCHIP] * 2 + [ANY] * 2 + [ONCHIP] * 3,
        out_specs=[ONCHIP] * 3,
        scratch_shapes=[
            pltpu.VMEM((2 * n, width), jnp.bfloat16),
            pltpu.VMEM((2 * n, width), jnp.bfloat16),
            pltpu.VMEM((chunks, pairs, 128, CK), jnp.bfloat16),
            pltpu.VMEM((pairs, 2 * BQ, 128), jnp.bfloat16),
            pltpu.VMEM((pairs, 2 * BQ, 128), jnp.bfloat16),
            pltpu.VMEM((pairs, 1, 2 * BQ), jnp.float32),
            pltpu.VMEM((pairs, 128, 2 * BQ), jnp.float32),
            pltpu.SemaphoreType.DMA((2,)),
            pltpu.SemaphoreType.DMA((2,)),
        ],
        cost_estimate=LIGHT,
        name="attend_back",
    )(*masks[causal, CK], q, kv, kv_oth, o, lse, grad)


def rms(v, gain):
    scale = lax.rsqrt(jnp.mean(v * v, axis=-1, keepdims=True) + NORM_EPS)
    return v * scale * gain


def rms_back(v, gain, grad):
    scale = lax.rsqrt(jnp.mean(v * v, axis=-1, keepdims=True) + NORM_EPS)
    scaled = grad * gain
    lean = jnp.mean(scaled * v, axis=-1, keepdims=True) * (scale * scale * scale)
    return scaled * scale - v * lean, jnp.sum(grad * v * scale, axis=0, keepdims=True)


def project_kernel(x, gain, w, normed, q, kv):
    a = low(rms(x[...], gain[...]))
    normed[...] = a
    q[...] = low(dot32(a, w[0], NN))
    kv[0] = low(dot32(a, w[1], NN))
    kv[1] = low(dot32(a, w[2], NN))


def pair_kernel(memory, w, kv):
    m = memory[...]
    kv[0] = low(dot32(m, w[1], NN))
    kv[1] = low(dot32(m, w[2], NN))


def between_kernel(o, w_out, x, gain, w, y, normed, q):
    state = x[...] + dot32(o[...], w_out[0], NN)
    y[...] = state
    c = low(rms(state, gain[...]))
    normed[...] = c
    q[...] = low(dot32(c, w[0], NN))


def feed_kernel(o, w_out, x, gain, w_up, w_down, y, normed, hidden, z):
    state = x[...] + dot32(o[...], w_out[0], NN)
    y[...] = state
    f = low(rms(state, gain[...]))
    normed[...] = f
    for i in range(w_up.shape[0]):
        r = low(jnp.maximum(dot32(f, w_up[i], NN), 0.0))
        hidden[i] = r
        state = state + dot32(r, w_down[i], NN)
    z[...] = state


def out_back(g, o, w_out, grad_o, grad_out):
    grad_o[...] = low(dot32(g, w_out[0], NT))
    grad_out[0] = low(dot32(o[...], g, TN))


def feed_back_kernel(
    grad, y, normed, hidden, gain, w_up, w_down, o, w_out,
    grad_up, grad_down, grad_y, grad_gain, grad_o, grad_out,
):
    g = low(grad[...])
    f = normed[...]
    back = jnp.zeros(grad.shape, jnp.float32)
    for i in range(w_up.shape[0]):
        r = hidden[i]
        grad_down[i] = low(dot32(r, g, TN))
        h = low(jnp.where(r > 0, dot32(g, w_down[i], NT), 0.0))
        grad_up[i] = low(dot32(f, h, TN))
        back = back + dot32(h, w_up[i], NT)
    more, grad_gain[...] = rms_back(y[...], gain[...], back)
    total = grad[...] + more
    grad_y[...] = total
    out_back(low(total), o, w_out, grad_o, grad_out)


def between_back_kernel(
    grad_q, normed, y, gain, w, grad, o, w_out,
    grad_w, grad_x, grad_gain, grad_o, grad_out,
):
    g = grad_q[...]
    grad_w[0] = low(dot32(normed[...], g, TN))
    more, grad_gain[...] = rms_back(y[...], gain[...], dot32(g, w[0], NT))
    total = grad[...] + more
    grad_x[...] = total
    out_back(low(total), o, w_out, grad_o, grad_out)


def memory_back_kernel(own, other, memory, w, grad_w, grad_memory):
    m = memory[...]
    total = None
    for i in range(2):
        g = low(own[i] + other[i])
        grad_w[i] = low(dot32(m, g, TN))
        part = dot32(g, w[i + 1], NT)
        total = part if total is None else total + part
    grad_memory[...] = total


def project_back_kernel(
    grad_q, own, other, normed, x, gain, w, grad,
    grad_w, grad_x, grad_gain,
):
    a = normed[...]
    back = None
    for i in range(3):
        g = grad_q[...] if i == 0 else low(own[i - 1] + other[i - 1])
        grad_w[i] = low(dot32(a, g, TN))
        part = dot32(g, w[i], NT)
        back = part if back is None else back + part
    more, grad_gain[...] = rms_back(x[...], gain[...], back)
    grad_x[...] = grad[...] + more


def table_back_kernel(ids, token_grads, grad_logits, exits, grad):
    first = pl.program_id(0) * grad.shape[0]
    spot = first + lax.broadcasted_iota(jnp.int32, (grad.shape[0], ids.shape[1]), 0)
    looked = jnp.where(spot == ids[0:1, :], 1.0, 0.0).astype(HALF)
    total = dot32(looked, token_grads[...], NN) + dot32(grad_logits[...], exits[...], TN)
    grad[...] = low(total)


def table_back(ids, token_grads, grad_logits, exits):
    rows, vocabulary = grad_logits.shape
    count, width = token_grads.shape
    ids = jnp.broadcast_to(ids[None], (8, count))
    return pl.pallas_call(
        table_back_kernel,
        grid=(vocabulary // COL,),
        out_shape=jax.ShapeDtypeStruct((vocabulary, width), HALF),
        in_specs=[
            pl.BlockSpec((8, count), lambda i: (0, 0)),
            pl.BlockSpec((count, width), lambda i: (0, 0)),
            pl.BlockSpec((rows, COL), lambda i: (0, i)),
            pl.BlockSpec((rows, width), lambda i: (0, 0)),
        ],
        out_specs=pl.BlockSpec((COL, width), lambda i: (i, 0)),
        cost_estimate=LIGHT,
        compiler_params=pltpu.CompilerParams(vmem_limit_bytes=24 << 20),
        name="table_back",
    )(ids, token_grads, grad_logits, exits)


def on_chip(kernel, name, outs, *args):
    return pl.pallas_call(
        kernel,
        out_shape=[jax.ShapeDtypeStruct(shape, kind) for shape, kind in outs],
        in_specs=[ONCHIP] * len(args),
        out_specs=[ONCHIP] * len(outs),
        cost_estimate=LIGHT,
        name=name,
    )(*args)


def shaped(lead, like, kind):
    return (lead + like.shape, kind)


def attend_forward(masks, causal, q, kv):
    other = flip(kv, "c")
    o, lse = attend(masks, causal, q, kv, other)
    return o, (q, kv, other, o, lse)


def attend_backward(saved, masks, causal, grad):
    grad_q, own, other = attend_back(masks, causal, *saved, grad)
    return grad_q, own, flip(other, "c")


def project(x, gain, w):
    return on_chip(
        project_kernel,
        "project",
        [shaped((), x, HALF), shaped((), x, HALF), shaped((2,), x, HALF)],
        x, gain[None], w,
    )


def memory_pair(memory, w):
    return on_chip(pair_kernel, "memory_pair", [shaped((2,), memory, HALF)], memory, w)[0]


def between(o, w_out, x, gain, w):
    return on_chip(
        between_kernel,
        "between",
        [shaped((), x, FULL), shaped((), x, HALF), shaped((), x, HALF)],
        o, w_out, x, gain[None], w,
    )


def feed(o, w_out, x, gain, w_up, w_down):
    return on_chip(
        feed_kernel,
        "feed",
        [
            shaped((), x, FULL),
            shaped((), x, HALF),
            shaped((w_up.shape[0],), x, HALF),
            shaped((), x, FULL),
        ],
        o, w_out, x, gain[None], w_up, w_down,
    )


def feed_back(grad, kept, gain, w_up, w_down, o, w_out):
    y, normed, hidden = kept
    return on_chip(
        feed_back_kernel,
        "feed_back",
        [
            (w_up.shape, HALF),
            (w_down.shape, HALF),
            shaped((), y, FULL),
            ((1, y.shape[1]), FULL),
            shaped((), y, HALF),
            (w_out.shape, HALF),
        ],
        grad, y, normed, hidden, gain[None], w_up, w_down, o, w_out,
    )


def between_back(grad_q, normed, y, gain, w, grad, o, w_out):
    return on_chip(
        between_back_kernel,
        "between_back",
        [
            (w_out.shape, HALF),
            shaped((), y, FULL),
            ((1, y.shape[1]), FULL),
            shaped((), y, HALF),
            (w_out.shape, HALF),
        ],
        grad_q, normed, y, gain[None], w, grad, o, w_out,
    )


def memory_back(own, other, memory, w):
    return on_chip(
        memory_back_kernel,
        "memory_back",
        [((2,) + w.shape[1:], HALF), shaped((), memory, FULL)],
        own, other, memory, w,
    )


def project_back(grad_q, own, other, normed, x, gain, w, grad):
    return on_chip(
        project_back_kernel,
        "project_back",
        [(w.shape, HALF), shaped((), x, FULL), ((1, x.shape[1]), FULL)],
        grad_q, own, other, normed, x, gain[None], w, grad,
    )


def shards(
    tokens,
    source,
    segments,
    loss_rows,
    targets,
    exit_depth,
    qkv_weight,
    out_weight,
    up_weight,
    down_weight,
    norm_gains,
    embed_table,
    qkv_first,
    out_first,
    up_first,
    down_first,
    gains_first,
    table_first,
    qkv_second,
    out_second,
    up_second,
    down_second,
    gains_second,
    table_second,
):
    sy, sx = lax.axis_index("sy"), lax.axis_index("sx")
    z, c = lax.axis_index("z"), lax.axis_index("c")
    s = sy * 2 + sx
    me = jnp.stack([c, z, s]).astype(jnp.int32)
    owners = lax.axis_size("z") * 2
    tok_dev = tokens.shape[2]
    loss_dev = targets.shape[2]
    voc_dev, width = embed_table.shape
    gain_count, gain_dev = norm_gains.shape
    vocabulary = voc_dev * owners
    root_width = math.sqrt(width)
    half_row = 2 * tok_dev
    unit = qkv_weight.shape[1] // 4
    fast = lax.axis_size("z") == 4 and unit % 16 == 0

    shard_of = {
        "table": embed_table[None],
        "qkv": qkv_weight,
        "out": out_weight,
        "up": up_weight,
        "down": down_weight,
    }
    shard_shapes = {name: array.shape[1:] for name, array in shard_of.items()}
    weights = {}

    def layout(entries):
        kinds = [kind for _, _, kind in entries]
        return kinds, block_counts(entries, shard_shapes, unit)

    def packed(entries):
        return jnp.concatenate(
            [owned_blocks(low(shard_of[name][i]), kind, unit) for name, i, kind in entries]
        )

    def gather(entries):
        mover = Mover()
        mover.stages = gather_stages(mover, me, packed(entries), *layout(entries), unit, owners)
        return mover

    def settle(entries, outs):
        for (name, i, kind), out in zip(entries, outs):
            weights[name, i] = out.reshape(-1, COL, COL) if kind == "blk" else out

    def gather_plainly(entries):
        everything = lax.all_gather(packed(entries), LINE)
        outs = []
        first = 0
        for kind, count in zip(*layout(entries)):
            piece = everything[:, first : first + count]
            first += count
            if kind == "row":
                outs.append(piece.transpose(1, 0, 2, 3).reshape(count, -1, COL))
            else:
                outs.append(piece.reshape(owners, count, 4, unit, COL).transpose(0, 2, 1, 3, 4))
        settle(entries, outs)

    def pieces(entries):
        arrays, kinds, counts = [], [], []
        for (name, i, kind), count in zip(entries, layout(entries)[1]):
            held = grads[name, i]
            for array in held if isinstance(held, tuple) else (held,):
                blocks = array.shape[0] if isinstance(held, tuple) else count
                arrays.append(array.reshape(natural_shape(kind, blocks, unit, owners)))
                kinds.append(kind)
                counts.append(blocks)
        return arrays, kinds, counts

    def reduce(entries, stages=reduce_stages):
        arrays, kinds, counts = pieces(entries)
        mover = Mover()
        mover.stages = stages(mover, me, arrays, kinds, counts, unit)
        return mover

    def take(entries, parts):
        first = 0
        for (name, i, kind), count in zip(entries, layout(entries)[1]):
            reduced[name, i] = owned_natural(parts[:, first : first + count], kind)
            first += count

    def reduce_plainly(entries):
        parts = []
        for array, kind, count in zip(*pieces(entries)):
            if kind == "row":
                array = array.reshape(count, owners, 4, unit, COL).transpose(1, 2, 0, 3, 4)
            parts.append(wide(array))
        total = jnp.concatenate(parts, axis=2)
        total = lax.psum_scatter(total, LINE, scatter_dimension=0, tiled=True)
        total = lax.psum(total, PLANE)[0]
        take(entries, total)
        return jnp.sum(total * total) / 4.0

    if fast:
        first = gather(GATHERED[0])
        ints = [tokens, source, segments, loss_rows, targets, exit_depth]
        ints, shard_of = step((ints, shard_of), first)
        tokens, source, segments, loss_rows, targets, exit_depth = ints
        second = gather(GATHERED[1])

        def gather_long(entries):
            return jnp.concatenate(
                [quarter_blocks(shard_of[name][i], kind, unit, s) for name, i, kind in entries]
            )

        third, fourth = gather_long(GATHERED[2]), gather_long(GATHERED[3])
    if not fast:
        for entries in GATHERED:
            gather_plainly(entries)

    numbers = jnp.concatenate(
        [array[:, 0] for array in (tokens, source, segments, loss_rows, targets, exit_depth)],
        axis=1,
    )
    plane = gathered(gathered(numbers, "c"), PLANE)
    depths_seen = plane[..., 3 * tok_dev + 2 * loss_dev :]
    reached = jnp.stack(
        [
            jnp.sum((depths_seen >= layer_id).astype(jnp.float32), axis=(0, 1, 3))
            for layer_id in range(LAYERS)
        ],
        axis=1,
    )
    gains_now = norm_gains
    if fast:
        reached, gains_now = step((reached, gains_now), first)
        (reached, gains_now), third = hold((reached, gains_now), third)
        third = lax.all_gather(third, PLANE + LINE).reshape(4, owners, *third.shape)
        reached, gains_now = step((reached, gains_now), second)
    small = jnp.concatenate([gains_now.reshape(-1), reached.reshape(-1)])
    small = gathered(gathered(small, "c"), "z").reshape(owners, -1)
    reach = jnp.maximum(
        jnp.sum(small[::2, gain_count * gain_dev :], axis=0).reshape(MICRO, LAYERS), 1.0
    )
    reach = lax.dynamic_index_in_dim(reach, sy, 0, False)
    gains_seen = small[:, : gain_count * gain_dev].reshape(owners, gain_count, gain_dev)
    order = jnp.arange(owners)
    rel = ((order // 2) ^ z) * 2 + ((order % 2) ^ c)
    gains_full = gains_seen[rel].transpose(1, 0, 2).reshape(gain_count, width)
    gains_full = wide(low(gains_full))

    row = lax.dynamic_index_in_dim(plane, sx ^ c, 1, False)
    row = in_order(lax.dynamic_index_in_dim(row, sy, 1, False), s)
    mine = lax.dynamic_slice_in_dim(row, 2 * c, 2, 0)
    theirs = lax.dynamic_slice_in_dim(row, 2 * (1 - c), 2, 0)
    target_ids = mine[:, :tok_dev].reshape(-1)
    source_ids = mine[:, tok_dev : 2 * tok_dev].reshape(-1)
    sentence = mine[:, 2 * tok_dev : 3 * tok_dev].reshape(-1)
    other_sentence = theirs[:, 2 * tok_dev : 3 * tok_dev].reshape(-1)
    rest = 3 * tok_dev
    places = (
        mine[:, rest : rest + loss_dev] + (jnp.arange(2, dtype=jnp.int32) * tok_dev)[:, None]
    ).reshape(-1)
    wanted = mine[:, rest + loss_dev : rest + 2 * loss_dev].reshape(-1)
    depth = mine[:, rest + 2 * loss_dev : rest + 3 * loss_dev].reshape(-1)
    masks = attend_masks(sentence, other_sentence, c * half_row, (1 - c) * half_row)

    ids = jnp.concatenate([source_ids, target_ids])
    if fast:
        ids, small = step((ids, small), first)
        ids = step(ids, second, first)
        settle(GATHERED[0], first.result)
    table = weights["table", 0].reshape(vocabulary, width)
    looked_up = table[ids].astype(jnp.float32) * root_width
    xe = looked_up[:half_row]
    x = looked_up[half_row:]
    kept_enc = (xe, *project(xe, gains_full[0], weights["qkv", 0]))
    if fast:
        xe, kept_enc, x = step((xe, kept_enc, x), second)
    o, saved_enc = attend_forward(masks, False, *kept_enc[2:])
    if fast:
        o, fourth = step((o, fourth), second)
        fourth = lax.all_gather(fourth, PLANE + LINE).reshape(4, owners, *fourth.shape)
        settle(GATHERED[1], second.result)
    *kept_enc_feed, xe = feed(
        o, weights["out", 0], xe, gains_full[1], weights["up", 0], weights["down", 0]
    )
    final_gain = gains_full[2 * ENC]
    memory = low(normalize(xe, final_gain))
    kept = []
    states = []
    for layer_id in range(LAYERS):
        base = 2 * ENC + 1 + 4 * layer_id
        slot = ENC + 2 * layer_id
        if fast and layer_id == 0:
            (x, memory), third = hold((x, memory), third)
            settle(GATHERED[2], unpack(third, *layout(GATHERED[2]), unit, owners))
        kept_self = (x, *project(x, gains_full[base], weights["qkv", slot]))
        o, saved_self = attend_forward(masks, True, *kept_self[2:])
        if fast and layer_id == 1:
            o, fourth = hold(o, fourth)
            settle(GATHERED[3], unpack(fourth, *layout(GATHERED[3]), unit, owners))
        cross = weights["qkv", slot + 1]
        pair = memory_pair(memory, cross)
        *kept_cross, q = between(o, weights["out", slot], x, gains_full[base + 1], cross)
        o, saved_cross = attend_forward(masks, False, q, pair)
        feed_at = ENC + layer_id
        *kept_feed, x = feed(
            o,
            weights["out", slot + 1],
            kept_cross[0],
            gains_full[base + 2],
            weights["up", feed_at],
            weights["down", feed_at],
        )
        kept.append((kept_self, saved_self, kept_cross, saved_cross, kept_feed))
        states.append(x)

    pick = (places[:, None] == jnp.arange(half_row)[None, :]).astype(jnp.bfloat16)
    exit_gains = [gains_full[2 * ENC + 4 + 4 * layer_id] for layer_id in range(LAYERS)]
    exits = jnp.concatenate(
        [low(product(pick, low(normalize(states[i], exit_gains[i])))) for i in range(LAYERS)]
    )
    logits = against_rows(exits, table) * LOGIT_SCALE
    wanted_all = jnp.concatenate([wanted] * LAYERS)
    hit = jnp.arange(vocabulary)[None, :] == wanted_all[:, None]
    picked = jnp.sum(jnp.where(hit, logits, 0.0), axis=-1)
    top = jnp.max(logits, axis=-1)
    lse = top + jnp.log(jnp.sum(jnp.exp(logits - top[:, None]), axis=-1))
    shares = jnp.concatenate(
        [(depth >= i).astype(jnp.float32) / reach[i] / MICRO for i in range(LAYERS)]
    )
    loss_part = jnp.sum((lse - picked) * shares)
    grad_logits = low(
        (jnp.exp(logits - lse[:, None]) - hit.astype(jnp.float32))
        * shares[:, None]
        * LOGIT_SCALE
    )
    grad_exits = product(grad_logits, table)

    grads = {}
    gain_parts = [None] * gain_count
    grad_x = None
    grad_memory = None
    for layer_id in reversed(range(LAYERS)):
        slot = ENC + 2 * layer_id
        base = 2 * ENC + 1 + 4 * layer_id
        count = places.shape[0]
        grad_rows = lax.dot_general(
            wide(pick),
            grad_exits[layer_id * count : (layer_id + 1) * count],
            (((0,), (0,)), ((), ())),
            precision=lax.Precision.HIGHEST,
            preferred_element_type=jnp.float32,
        )
        grad_here, gain_parts[base + 3] = norm_back(
            states[layer_id], exit_gains[layer_id], grad_rows
        )
        grad_x = grad_here if grad_x is None else grad_x + grad_here
        kept_self, saved_self, kept_cross, saved_cross, kept_feed = kept[layer_id]
        up, down = ("up", ENC + layer_id), ("down", ENC + layer_id)
        qkv, out = ("qkv", slot + 1), ("out", slot + 1)
        grads[up], grads[down], grad_x, gain_parts[base + 2], grad_o, grads[out] = feed_back(
            grad_x,
            kept_feed,
            gains_full[base + 2],
            weights[up],
            weights[down],
            saved_cross[3],
            weights[out],
        )
        if fast and layer_id == 1:
            feed_mover = reduce(REDUCED[0], long_reduce_stages)
            grad_x, grad_o = step((grad_x, grad_o), feed_mover, feed_mover)
        if fast and layer_id == 0:
            late = reduce(REDUCED[1], long_reduce_stages)
            grad_x, grad_o = step((grad_x, grad_o), feed_mover, late, late)
        grad_q, own, other = attend_backward(saved_cross, masks, False, grad_o)
        grad_pair, more = memory_back(own, other, memory, weights[qkv])
        grad_memory = more if grad_memory is None else grad_memory + more
        out = ("out", slot)
        grad_query, grad_x, gain_parts[base + 1], grad_o, grads[out] = between_back(
            grad_q,
            kept_cross[1],
            kept_cross[0],
            gains_full[base + 1],
            weights[qkv],
            grad_x,
            saved_self[3],
            weights[out],
        )
        grads[qkv] = (grad_query, grad_pair)
        grad_q, own, other = attend_backward(saved_self, masks, True, grad_o)
        qkv = ("qkv", slot)
        grads[qkv], grad_x, gain_parts[base] = project_back(
            grad_q,
            own,
            other,
            kept_self[1],
            kept_self[0],
            gains_full[base],
            weights[qkv],
            grad_x,
        )
    if fast:
        grad_x, grad_memory = step((grad_x, grad_memory), feed_mover)
    grad_enc, gain_parts[2 * ENC] = norm_back(xe, final_gain, grad_memory)
    up, down, qkv, out = ("up", 0), ("down", 0), ("qkv", 0), ("out", 0)
    grads[up], grads[down], grad_enc, gain_parts[1], grad_o, grads[out] = feed_back(
        grad_enc,
        kept_enc_feed,
        gains_full[1],
        weights[up],
        weights[down],
        saved_enc[3],
        weights[out],
    )
    if fast:
        middle = reduce(REDUCED[2], long_reduce_stages)
        grad_enc, grad_o = step((grad_enc, grad_o), middle, late, middle)
    grad_q, own, other = attend_backward(saved_enc, masks, False, grad_o)
    grads[qkv], grad_enc, gain_parts[0] = project_back(
        grad_q, own, other, kept_enc[1], kept_enc[0], gains_full[0], weights[qkv], grad_enc
    )
    token_ids = jnp.concatenate([source_ids, target_ids])
    token_grads = low(jnp.concatenate([grad_enc, grad_x]) * root_width)
    grads["table", 0] = table_back(token_ids, token_grads, grad_logits, exits)
    gain_grad = jnp.concatenate([part.reshape(1, -1) for part in gain_parts])
    small = jnp.concatenate([gain_grad, jnp.full((1, width), loss_part)])

    reduced = {}
    if fast:
        last = reduce(REDUCED[3])
        tiny = Mover()
        tiny.stages = small_stages(tiny, small, z)
        loss_part = step(loss_part, last, tiny)
        loss_part = step(loss_part, last, tiny, middle)
        loss_part = step(loss_part, last, tiny)
        loss_part = step(loss_part, last, tiny)
        movers = (feed_mover, late, middle, last)
        loss_part = step(loss_part, last, tiny)
        gain_grad, loss_total = tiny.result[:-1], tiny.result[-1, 0]
        squares = all_sum(sum(mover.squares for mover in movers))
        squares = step(squares, late, middle, last)
    else:
        small = all_sum(small)
        gain_grad, loss_total = small[:-1], small[-1, 0]
        squares = all_sum(sum(reduce_plainly(entries) for entries in REDUCED))
    squares = squares + jnp.sum(gain_grad * gain_grad)
    grad_norm = jnp.sqrt(squares)
    clip_factor = CLIP_NORM / jnp.maximum(grad_norm, CLIP_NORM)

    names = ("qkv", "out", "up", "down", "table")
    if fast:
        plan = []
        for bucket, entries in enumerate(REDUCED):
            first = 0
            for (name, i, kind), count in zip(entries, layout(entries)[1]):
                plan.append((bucket, first, count, kind, names.index(name), i))
                first += count
        parts = [part for mover in movers for part in mover.result]
        shapes = [shard_of[name].shape for name in names]
        placed = pl.pallas_call(
            functools.partial(settle_kernel, len(parts), tuple(plan), unit),
            out_shape=[jax.ShapeDtypeStruct(shape, jnp.bfloat16) for shape in shapes],
            in_specs=[SCALAR] + [ANY] * len(parts),
            out_specs=[ONCHIP] * len(shapes),
            scratch_shapes=[pltpu.SemaphoreType.DMA((len(shapes),))],
            cost_estimate=LIGHT,
            name="place_gradients",
        )(me, *parts)
        ready = [wide(array) for array in placed]
    else:
        ready = [
            wide(jnp.stack([reduced[name, i] for i in range(shard_of[name].shape[0])]))
            for name in names
        ]
    gradients = (
        *ready[:4],
        lax.dynamic_slice_in_dim(gain_grad, (2 * z + c) * gain_dev, gain_dev, 1),
        ready[4][0],
    )
    masters = (qkv_weight, out_weight, up_weight, down_weight, norm_gains, embed_table)
    firsts = (qkv_first, out_first, up_first, down_first, gains_first, table_first)
    seconds = (qkv_second, out_second, up_second, down_second, gains_second, table_second)
    results = [
        adam_update(masters[i], firsts[i], seconds[i], gradients[i] * clip_factor) for i in range(6)
    ]
    gains_grad = gradients[4] * clip_factor
    return (
        loss_total,
        grad_norm,
        results[0][0],
        results[1][0],
        results[2][0],
        results[3][0],
        gains_grad,
        results[5][0],
        results[0][1],
        results[1][1],
        results[2][1],
        results[3][1],
        results[4][1],
        results[5][1],
        results[0][2],
        results[1][2],
        results[2][2],
        results[3][2],
        results[4][2],
        results[5][2],
    )


def solution(mesh):
    seq, vocab = mesh.devices.shape
    fine = Mesh(mesh.devices.reshape(2, seq // 2, vocab // 2, 2), ("sy", "sx", "z", "c"))
    ints = P(None, LINE, PLANE)
    block = P(None, LINE, None)
    gains = P(None, LINE)
    rows = P(LINE, None)
    arrays = (block, block, block, block, gains, rows)
    return jax.shard_map(
        shards,
        mesh=fine,
        in_specs=(ints,) * 6 + arrays * 3,
        out_specs=(P(), P(), block, block, block, block, gains, rows) + arrays * 2,
        check_vma=False,
    )
```

```python
import functools
import math

import jax
import jax.numpy as jnp
from jax import lax
from jax.experimental import pallas as pl
from jax.experimental.pallas import tpu as pltpu
from jax.sharding import Mesh
from jax.sharding import PartitionSpec as P

HEADS = 8
HEAD = 64
ENC = 1
LAYERS = 2
MICRO = 2
COL = 512
HALF, FULL = jnp.bfloat16, jnp.float32

NORM_EPS = 1e-06
CLIP_NORM = 0.01
LEARN_RATE = 0.05
BETA_ONE = 0.9
BETA_TWO = 0.999
ADAM_EPS = 1e-08
WEIGHT_DECAY = 0.01
ADAM_STEP = 10
LOGIT_SCALE = 4.0
NEGATIVE = -1e30

PLANE = ("sy", "sx")
LINE = ("z", "c")

TABLE = ("table", 0, "blk")


def attention_parts(i):
    return (("qkv", i, "row"), ("out", i, "row"))


def feed_parts(i):
    return (("up", i, "row"), ("down", i, "blk"))


GATHERED = (
    (TABLE,) + attention_parts(0),
    feed_parts(0),
    attention_parts(1) + attention_parts(2) + feed_parts(1) + attention_parts(3),
    attention_parts(4) + feed_parts(2),
)
REDUCED = (
    feed_parts(2),
    attention_parts(3) + attention_parts(4) + feed_parts(1),
    attention_parts(1) + attention_parts(2) + feed_parts(0),
    (TABLE,) + attention_parts(0),
)


def flip(x, axis, bit=1):
    if isinstance(axis, tuple):
        n = math.prod(lax.axis_size(a) for a in axis)
    else:
        n = lax.axis_size(axis)
    return lax.ppermute(x, axis, [(i, i ^ bit) for i in range(n)])


def bits(axis):
    n = lax.axis_size(axis)
    return [1 << k for k in range(n.bit_length() - 1)]


def gathered(x, axis):
    if isinstance(axis, tuple) or lax.axis_size(axis) <= 4:
        n = 4 if isinstance(axis, tuple) else lax.axis_size(axis)
        return jnp.stack([x] + [flip(x, axis, r) for r in range(1, n)])
    x = x[None]
    for bit in bits(axis):
        x = jnp.concatenate([x, flip(x, axis, bit)], axis=0)
    return x


def in_order(blocks, index):
    n = blocks.shape[0]
    return jnp.concatenate(
        [lax.dynamic_index_in_dim(blocks, i ^ index, 0, keepdims=True) for i in range(n)]
    )


def all_sum(x):
    for axis in ("c", "sx", "sy", "z"):
        for bit in bits(axis):
            x = x + flip(x, axis, bit)
    return x


def hold(carry, things):
    return lax.optimization_barrier((carry, things))


def step(carry, *movers):
    for mover in movers:
        carry, (mover.held, mover.arrived) = hold(carry, (mover.held, mover.arrived))
        leaving = next(mover.stages)
        carry, (arrays, mover.held) = hold(carry, ([array for array, _ in leaving], mover.held))
        mover.arrived = [
            flip(array, *route)
            if route
            else lax.psum_scatter(array, PLANE + ("z",), scatter_dimension=0, tiled=True)
            for array, (_, route) in zip(arrays, leaving)
        ]
    return carry


class Mover:
    def __init__(self):
        self.held = []
        self.arrived = []


def normalize(v, g):
    return v * lax.rsqrt(jnp.mean(v * v, axis=-1, keepdims=True) + NORM_EPS) * g


def norm_back(v, g, cotangent):
    _, pullback = jax.vjp(normalize, v, g)
    return pullback(cotangent)


def product(a, b):
    return jnp.dot(a, b, preferred_element_type=jnp.float32)


def outer_sum(a, b):
    return lax.dot_general(a, b, (((0,), (0,)), ((), ())), preferred_element_type=jnp.float32)


def against_rows(a, b):
    return lax.dot_general(a, b, (((1,), (1,)), ((), ())), preferred_element_type=jnp.float32)


def split_heads(v):
    return v.reshape(v.shape[0], HEADS, HEAD)


def low(v):
    return v.astype(jnp.bfloat16)


def wide(v):
    return v.astype(jnp.float32)


def adam_update(master, first, second, grad):
    first = BETA_ONE * first + (1.0 - BETA_ONE) * grad
    second = BETA_TWO * second + (1.0 - BETA_TWO) * grad * grad
    fixed_first = first / (1.0 - BETA_ONE**ADAM_STEP)
    fixed_second = second / (1.0 - BETA_TWO**ADAM_STEP)
    master = master - LEARN_RATE * (
        fixed_first / (jnp.sqrt(fixed_second) + ADAM_EPS) + WEIGHT_DECAY * master
    )
    return (master, first, second)


def owned_blocks(array, kind, unit):
    if kind == "row":
        rows, columns = array.shape
        return array.reshape(rows, columns // COL, COL).transpose(1, 0, 2)
    rows = array.shape[0]
    per = rows // (4 * unit)
    return array.reshape(4, per, unit, COL).transpose(1, 0, 2, 3).reshape(per, 4 * unit, COL)


def quarter_blocks(array, kind, unit, s):
    size = array.shape[0] // 4
    array = lax.dynamic_slice_in_dim(array, s * size, size, axis=0)
    if kind == "row":
        return low(array).reshape(unit, -1, COL).transpose(1, 0, 2)
    return low(array).reshape(-1, unit, COL)


def block_counts(entries, shard_shapes, unit):
    counts = []
    for name, _, kind in entries:
        rows, columns = shard_shapes[name]
        counts.append(columns // COL if kind == "row" else rows // (4 * unit))
    return counts


def natural_shape(kind, count, unit, owners):
    if kind == "row":
        return (count, owners * 4 * unit, COL)
    return (owners, 4, count, unit, COL)


def scatter_kernel(plan, unit, me_ref, *refs):
    pieces, outs, sem = refs[:10], refs[10:-1], refs[-1]
    c, z, s = me_ref[0], me_ref[1], me_ref[2]

    def put(out, kind, owner, part, rows, source):
        if kind == "row":
            start = pl.multiple_of(owner * (4 * unit) + part * unit, unit)
            target = outs[out].at[:, pl.ds(start, rows), :]
        else:
            target = outs[out].at[owner, part]
        pltpu.make_async_copy(source, target, sem.at[out]).start()

    for c_rel in range(2):
        shard, *quarters = pieces[5 * c_rel : 5 * c_rel + 5]
        for z_rel in range(4):
            owner = (z ^ z_rel) * 2 + (c ^ c_rel)
            for out, (kind, first, count) in enumerate(plan):
                last = first + count
                if z_rel == 0:
                    if kind == "row":
                        put(out, kind, owner, 0, 4 * unit, shard.at[first:last])
                    else:
                        for part in range(4):
                            rows = pl.ds(part * unit, unit)
                            put(out, kind, owner, part, unit, shard.at[first:last, rows, :])
                else:
                    for s_rel, quarter in enumerate(quarters):
                        put(out, kind, owner, s ^ s_rel, unit, quarter.at[z_rel - 1, first:last])
    for out in range(len(plan)):
        pltpu.make_async_copy(outs[out], outs[out], sem.at[out]).wait()


def collect_kernel(plan, unit, ordered, me_ref, *refs):
    grads, keep, send, sem = refs[: len(plan)], refs[len(plan)], refs[len(plan) + 1], refs[-1]
    c, z, s = me_ref[0], me_ref[1], me_ref[2]
    for c_rel, out in ((0, keep), (1, send)):
        for z_rel in range(4):
            owner = (z ^ z_rel) * 2 + (c ^ c_rel)
            for s_rel in range(4):
                part = s ^ s_rel
                for grad, (kind, first, count) in zip(grads, plan):
                    if kind == "row":
                        start = pl.multiple_of(owner * (4 * unit) + part * unit, unit)
                        source = grad.at[:, pl.ds(start, unit), :]
                    else:
                        source = grad.at[owner, part]
                    place = (part, z ^ z_rel) if ordered else (s_rel, z_rel)
                    target = out.at[*place, first : first + count]
                    pltpu.make_async_copy(source, target, sem.at[c_rel]).start()
    for c_rel, out in ((0, keep), (1, send)):
        pltpu.make_async_copy(out, out, sem.at[c_rel]).wait()


LIGHT = pl.CostEstimate(flops=1, bytes_accessed=1, transcendentals=0)
SMALL = pltpu.CompilerParams(vmem_limit_bytes=32 << 20)
ANY = pl.BlockSpec(memory_space=pl.ANY)
ONCHIP = pl.BlockSpec(memory_space=pltpu.VMEM)
SCALAR = pl.BlockSpec(memory_space=pltpu.SMEM)


def gather_stages(mover, me, shard, kinds, counts, unit, owners):
    starts = [sum(counts[:i]) for i in range(len(counts))]
    mover.held = [shard]
    part = lax.dynamic_slice_in_dim(shard, me[2] * unit, unit, axis=1)
    yield [(part, ("z", bit)) for bit in (1, 2, 3)]
    mine = jnp.stack(mover.arrived)
    mover.held.append(mine)
    yield [(mine, (PLANE, bit)) for bit in (1, 2, 3)]
    mover.held += mover.arrived
    yield [(piece, ("c",)) for piece in mover.held]
    plan = tuple(zip(kinds, starts, counts))
    mover.result = pl.pallas_call(
        functools.partial(scatter_kernel, plan, unit),
        out_shape=[
            jax.ShapeDtypeStruct(natural_shape(kind, count, unit, owners), jnp.bfloat16)
            for kind, count in zip(kinds, counts)
        ],
        in_specs=[SCALAR] + [ANY] * 10,
        out_specs=[ONCHIP] * len(plan),
        scratch_shapes=[pltpu.SemaphoreType.DMA((len(plan),))],
        cost_estimate=LIGHT,
        compiler_params=SMALL,
        name="place_weights",
    )(me, *mover.held, *mover.arrived)
    mover.held = []
    yield []


def unpack_kernel(plan, pieces, *refs):
    outs, sem = refs[:-1], refs[-1]
    for out, (kind, first, count) in enumerate(plan):
        for part in range(4):
            if kind == "blk":
                source = pieces.at[part, :, first : first + count]
                pltpu.make_async_copy(source, outs[out].at[:, part], sem.at[out]).start()
                continue
            for k in range(count):
                source = pieces.at[part, :, first + k]
                pltpu.make_async_copy(source, outs[out].at[k, :, part], sem.at[out]).start()
    for out in range(len(plan)):
        pltpu.make_async_copy(outs[out], outs[out], sem.at[out]).wait()


def unpack(pieces, kinds, counts, unit, owners):
    starts = [sum(counts[:i]) for i in range(len(counts))]
    shapes = [
        (count, owners, 4, unit, COL) if kind == "row" else (owners, 4, count, unit, COL)
        for kind, count in zip(kinds, counts)
    ]
    placed = pl.pallas_call(
        functools.partial(unpack_kernel, tuple(zip(kinds, starts, counts))),
        out_shape=[jax.ShapeDtypeStruct(shape, jnp.bfloat16) for shape in shapes],
        in_specs=[ANY],
        out_specs=[ONCHIP] * len(shapes),
        scratch_shapes=[pltpu.SemaphoreType.DMA((len(shapes),))],
        cost_estimate=LIGHT,
        compiler_params=SMALL,
        name="place_gathered",
    )(pieces)
    return [
        out.reshape(count, -1, COL) if kind == "row" else out
        for out, kind, count in zip(placed, kinds, counts)
    ]


def added(arrays):
    total = wide(arrays[0])
    for array in arrays[1:]:
        total = total + wide(array)
    return total


def plane_sum_kernel(keep, core, from_x, from_y, left, right, own, *sends):
    half = left.shape[1]
    for bit in range(4):
        for part, (one, two) in ((slice(0, half), (from_x, left)), (slice(half, None), (from_y, right))):
            total = added([keep[bit, part], core[bit, part], one[bit], two[bit]])
            if bit == 0:
                own[part] = total
            else:
                sends[bit - 1][part] = low(total)


def line_sum_kernel(own, one, two, three, whole, squares):
    total = added([own[...], one[...], two[...], three[...]])
    whole[...] = low(total)
    squares[0, 0] = jnp.sum(total * total)


def collect(me, grads, kinds, counts, unit, ordered):
    starts = [sum(counts[:i]) for i in range(len(counts))]
    plan = tuple(zip(kinds, starts, counts))
    shape = jax.ShapeDtypeStruct((4, 4, sum(counts), unit, COL), jnp.bfloat16)
    return pl.pallas_call(
        functools.partial(collect_kernel, plan, unit, ordered),
        out_shape=[shape, shape],
        in_specs=[SCALAR] + [ANY] * len(plan),
        out_specs=[ONCHIP, ONCHIP],
        scratch_shapes=[pltpu.SemaphoreType.DMA((2,))],
        cost_estimate=LIGHT,
        compiler_params=SMALL,
        name="collect_gradients",
    )(me, *grads)


def long_reduce_stages(mover, me, grads, kinds, counts, unit):
    keep, send = collect(me, grads, kinds, counts, unit, True)
    mover.held = [keep]
    yield [(send, ("c",))]
    chip = low(added(mover.held + mover.arrived))
    mover.held = []
    yield [(chip.reshape(16, *chip.shape[2:]), None)]
    own = mover.arrived[0][0]
    mover.squares = jnp.sum(wide(own) * wide(own))
    mover.held = [own]
    yield [(own, (PLANE, bit)) for bit in (1, 2, 3)]
    mover.result = mover.held + mover.arrived
    mover.held = []
    yield []


def reduce_stages(mover, me, grads, kinds, counts, unit):
    total = sum(counts)
    keep, send = collect(me, grads, kinds, counts, unit, False)
    mover.held = [keep]
    half = total // 2
    yield [(send, ("c",))]
    mover.held = [a.reshape(2, 2, *a.shape[1:]) for a in mover.held + mover.arrived]
    yield [
        (low(added([a[:, 1, :, :half] for a in mover.held])), ("sx",)),
        (low(added([a[1, :, :, half:] for a in mover.held])), ("sy",)),
    ]
    mover.held += mover.arrived

    def sides():
        both, (come_x, come_y) = mover.held[:2], mover.held[2:4]
        return (
            [a[:, 0, :, :half] for a in both] + [come_x],
            [a[0, :, :, half:] for a in both] + [come_y],
        )

    left, right = sides()
    yield [(low(added([a[1] for a in left])), ("sy",)), (low(added([a[1] for a in right])), ("sx",))]
    mover.held += mover.arrived

    block = (total, unit, COL)
    first_part = pl.BlockSpec((None, None, 4, *block), lambda i: (0, 0, 0, 0, 0, 0))
    half_part = [pl.BlockSpec((None, 4, n, unit, COL), lambda i: (0, 0, 0, 0, 0)) for n in (half, total - half)]
    own, *sends = pl.pallas_call(
        plane_sum_kernel,
        grid=(1,),
        out_shape=[jax.ShapeDtypeStruct(block, FULL)] + [jax.ShapeDtypeStruct(block, HALF)] * 3,
        in_specs=[first_part, first_part, *half_part, ONCHIP, ONCHIP],
        out_specs=[ONCHIP] * 4,
        cost_estimate=LIGHT,
        compiler_params=SMALL,
        name="plane_sum",
    )(*mover.held)
    mover.held = [own]
    yield [(send, ("z", bit)) for bit, send in zip((1, 2, 3), sends)]
    own, squares = pl.pallas_call(
        line_sum_kernel,
        out_shape=[
            jax.ShapeDtypeStruct(block, HALF),
            jax.ShapeDtypeStruct((1, 1), FULL),
        ],
        in_specs=[ONCHIP] * 4,
        out_specs=[ONCHIP, SCALAR],
        cost_estimate=LIGHT,
        compiler_params=SMALL,
        name="line_sum",
    )(*mover.held, *mover.arrived)
    mover.squares = squares[0, 0]
    mover.held = [own]
    yield [(own, (PLANE, bit)) for bit in (1, 2, 3)]
    mover.result = mover.held + mover.arrived
    mover.held = []
    yield []


def small_stages(mover, x, z):
    for axis in ("c", "sx", "sy"):
        mover.held = [x]
        yield [(x, (axis,))]
        x = mover.held[0] + mover.arrived[0]
    mover.held = [x]
    yield [(x, ("z", bit)) for bit in (1, 2, 3)]
    mover.result = jnp.sum(in_order(jnp.stack(mover.held + mover.arrived), z), axis=0)
    yield []


def settle_kernel(sizes, plan, unit, me_ref, *refs):
    buckets, outs, sem = refs[:sizes], refs[sizes:-1], refs[-1]
    s = me_ref[2]
    for bucket, first, count, kind, out, i in plan:
        for s_rel in range(4):
            source = buckets[4 * bucket + s_rel]
            part = s ^ s_rel
            if kind == "blk":
                for k in range(count):
                    start = pl.multiple_of((part * count + k) * unit, unit)
                    target = outs[out].at[i, pl.ds(start, unit), :]
                    pltpu.make_async_copy(source.at[first + k], target, sem.at[out]).start()
                continue
            rows = pl.ds(pl.multiple_of(part * unit, unit), unit)
            for k in range(count):
                target = outs[out].at[i, rows, k * COL : k * COL + COL]
                pltpu.make_async_copy(source.at[first + k], target, sem.at[out]).start()
    for out, ref in enumerate(outs):
        pltpu.make_async_copy(ref, ref, sem.at[out]).wait()


def owned_natural(parts, kind):
    if kind == "row":
        four, count, unit, _ = parts.shape
        return parts.transpose(0, 2, 1, 3).reshape(four * unit, count * COL)
    return parts.reshape(-1, COL)


BQ = 128
CK = 256
CF = 256
NT = (((1,), (1,)), ((), ()))
TN = (((0,), (0,)), ((), ()))
NN = (((1,), (0,)), ((), ()))


def dot32(a, b, dims):
    return lax.dot_general(a, b, dims, preferred_element_type=jnp.float32)


def load_halves(own, other, whole, sem):
    half = whole.shape[0] // 2
    copies = [
        pltpu.make_async_copy(own, whole.at[pl.ds(0, half)], sem.at[0]),
        pltpu.make_async_copy(other, whole.at[pl.ds(half, half)], sem.at[1]),
    ]
    for copy in copies:
        copy.start()
    return copies


def pair_rows(block, scale=None):
    lane = lax.broadcasted_iota(jnp.int32, block.shape, 1)
    zero = jnp.zeros_like(block)
    if scale is not None:
        block = block * jnp.asarray(scale, block.dtype)
    return jnp.concatenate(
        [jnp.where(lane < HEAD, block, zero), jnp.where(lane < HEAD, zero, block)], axis=0
    )


def pair_lanes(stacked):
    rows = stacked.shape[0] // 2
    lane = lax.broadcasted_iota(jnp.int32, (rows, 2 * HEAD), 1)
    return jnp.where(lane < HEAD, stacked[:rows], stacked[rows:])


def open_to(act, bounds, rows, j, chunks):
    half = chunks // 2
    base = jnp.where(j < half, act[0] + j * CK, act[1] + (j - half) * CK)
    spot = base + lax.broadcasted_iota(jnp.int32, (CK, BQ), 0)
    open_ = (spot >= bounds[0:1, rows]) & (spot <= bounds[1:2, rows])
    return jnp.concatenate([open_, open_], axis=1)


def attend_kernel(
    act, bounds, q, kv_own, kv_oth, o, lse,
    k_all, v_all, scores, queries, top, total, acc, sem_k, sem_v,
):
    pairs = q.shape[1] // (2 * HEAD)
    blocks = q.shape[0] // BQ
    chunks = k_all.shape[0] // CF
    half = chunks // 2
    waits = load_halves(kv_own.at[0], kv_oth.at[0], k_all, sem_k)
    waits += load_halves(kv_own.at[1], kv_oth.at[1], v_all, sem_v)
    for copy in waits:
        copy.wait()
    square = lax.broadcasted_iota(jnp.int32, (BQ, BQ), 0)
    along = lax.broadcasted_iota(jnp.int32, (BQ, BQ), 1)

    def one_block(b, _):
        rows = pl.ds(pl.multiple_of(b * BQ, BQ), BQ)
        for h in range(pairs):
            queries[h] = pair_rows(q[rows, h * 128 : h * 128 + 128], HEAD ** (-0.5))
        top[...] = jnp.full_like(top, NEGATIVE)
        total[...] = jnp.zeros_like(total)
        acc[...] = jnp.zeros_like(acc)
        least = jnp.broadcast_to(bounds[0:1, rows], (BQ, BQ)).T
        most = jnp.broadcast_to(bounds[1:2, rows], (BQ, BQ)).T

        def first(j, _):
            @pl.when(act[2 + b * chunks + j] > 0)
            def _():
                keys = pl.ds(pl.multiple_of(j * CF, CF), CF)
                base = jnp.where(j < half, act[0] + j * CF, act[1] + (j - half) * CF)
                open_ = []
                for part in range(CF // 128):
                    spot = base + part * 128 + along
                    one = (spot >= least) & (spot <= most)
                    open_.append(jnp.concatenate([one, one], axis=0))
                for h in range(pairs):
                    s = dot32(queries[h], k_all[keys, h * 128 : h * 128 + 128], NT)
                    best = top[h]
                    for part, one in enumerate(open_):
                        t = jnp.where(one, s[:, part * 128 : part * 128 + 128], NEGATIVE)
                        scores[h, j, :, part * 128 : part * 128 + 128] = t
                        best = jnp.maximum(best, t)
                    top[h] = best

            return 0

        lax.fori_loop(0, chunks, first, 0)
        for h in range(pairs):
            top[h] = jnp.broadcast_to(jnp.max(top[h], axis=1, keepdims=True), top.shape[1:])

        def second(j, _):
            @pl.when(act[2 + b * chunks + j] > 0)
            def _():
                keys = pl.ds(pl.multiple_of(j * CF, CF), CF)
                for h in range(pairs):
                    parts = []
                    more = total[h]
                    for part in range(CF // 128):
                        e = jnp.exp(scores[h, j, :, part * 128 : part * 128 + 128] - top[h])
                        more = more + e
                        parts.append(e.astype(jnp.bfloat16))
                    total[h] = more
                    e = parts[0] if len(parts) == 1 else jnp.concatenate(parts, axis=1)
                    acc[h] = acc[h] + dot32(e, v_all[keys, h * 128 : h * 128 + 128], NN)

            return 0

        lax.fori_loop(0, chunks, second, 0)
        for h in range(pairs):
            denom = jnp.broadcast_to(
                jnp.sum(total[h], axis=1, keepdims=True), total.shape[1:]
            )
            o[rows, h * 128 : h * 128 + 128] = pair_lanes(acc[h] / denom).astype(o.dtype)
            for part in range(2):
                span = slice(part * BQ, part * BQ + BQ)

                def line(level, span=span):
                    own = jnp.where(square == along, level[span], 0.0)
                    return jnp.sum(own, axis=0, keepdims=True)

                lse[b, h, :, span] = line(top[h]) + jnp.log(line(denom))
        return 0

    lax.fori_loop(0, blocks, one_block, 0)


def attend_back_kernel(
    act, bounds, q, kv_own, kv_oth, o, lse, grad,
    grad_q, grad_own, grad_oth,
    k_all, v_all, k_turned, queries, grads, delta, grad_queries, sem_k, sem_v,
):
    pairs = q.shape[1] // (2 * HEAD)
    blocks = q.shape[0] // BQ
    chunks = k_all.shape[0] // CK
    waits = load_halves(kv_own.at[0], kv_oth.at[0], k_all, sem_k)
    waits += load_halves(kv_own.at[1], kv_oth.at[1], v_all, sem_v)
    grad_own[...] = jnp.zeros_like(grad_own)
    grad_oth[...] = jnp.zeros_like(grad_oth)
    for copy in waits:
        copy.wait()

    def turn(j, _):
        for h in range(pairs):
            for part in range(CK // 128):
                keys = pl.ds(pl.multiple_of(j * CK + part * 128, 128), 128)
                k_turned[j, h, :, part * 128 : part * 128 + 128] = k_all[
                    keys, h * 128 : h * 128 + 128
                ].T
        return 0

    lax.fori_loop(0, chunks, turn, 0)

    def one_block(b, _):
        rows = pl.ds(pl.multiple_of(b * BQ, BQ), BQ)
        for h in range(pairs):
            lanes = slice(h * 128, h * 128 + 128)
            queries[h] = pair_rows(q[rows, lanes], HEAD ** (-0.5))
            grads[h] = pair_rows(grad[rows, lanes])
            both = (o[rows, lanes].astype(jnp.float32) * grad[rows, lanes].astype(jnp.float32)).T
            delta[h] = jnp.concatenate(
                [
                    jnp.sum(both[:HEAD], axis=0, keepdims=True),
                    jnp.sum(both[HEAD:], axis=0, keepdims=True),
                ],
                axis=1,
            )
        grad_queries[...] = jnp.zeros_like(grad_queries)

        def one_chunk(j, target, local):
            keys = pl.ds(pl.multiple_of(j * CK, CK), CK)
            own_keys = pl.ds(pl.multiple_of(local * CK, CK), CK)
            open_ = open_to(act, bounds, rows, j, chunks)
            for h in range(pairs):
                lanes = slice(h * 128, h * 128 + 128)
                s = jnp.where(open_, dot32(k_all[keys, lanes], queries[h], NT), NEGATIVE)
                p = jnp.exp(s - lse[b, h])
                ds = p * (dot32(v_all[keys, lanes], grads[h], NT) - delta[h])
                p = p.astype(jnp.bfloat16)
                ds = ds.astype(jnp.bfloat16)
                target[0, own_keys, lanes] += dot32(ds, queries[h], NN)
                target[1, own_keys, lanes] += dot32(p, grads[h], NN)
                grad_queries[h] += dot32(k_turned[j, h], ds, NN)

        def own_chunk(j, _):
            @pl.when(act[2 + b * chunks + j] > 0)
            def _():
                one_chunk(j, grad_own, j)

            return 0

        def oth_chunk(j, _):
            @pl.when(act[2 + b * chunks + j] > 0)
            def _():
                one_chunk(j, grad_oth, j - chunks // 2)

            return 0

        lax.fori_loop(0, chunks // 2, own_chunk, 0)
        lax.fori_loop(chunks // 2, chunks, oth_chunk, 0)
        for h in range(pairs):
            grad_q[rows, h * 128 : h * 128 + 128] = (
                pair_lanes(grad_queries[h].T) * HEAD ** (-0.5)
            ).astype(grad_q.dtype)
        return 0

    lax.fori_loop(0, blocks, one_block, 0)


def attend_masks(sentence, other, start, other_start):
    n = sentence.shape[0]
    seg = jnp.concatenate([sentence, other])
    spots = start + jnp.arange(n, dtype=jnp.int32)
    pos = jnp.concatenate([spots, other_start + jnp.arange(n, dtype=jnp.int32)])
    begin = jnp.sum((seg[None, :] < sentence[:, None]).astype(jnp.int32), axis=1)
    end = jnp.sum((seg[None, :] <= sentence[:, None]).astype(jnp.int32), axis=1) - 1
    made = {}
    for causal, last, size in ((c, l, k) for c, l in ((False, end), (True, spots)) for k in (CF, CK)):
        keys = pos.reshape(-1, size)
        live = (begin.reshape(-1, BQ).min(1)[:, None] <= keys.max(1)[None, :]) & (
            last.reshape(-1, BQ).max(1)[:, None] >= keys.min(1)[None, :]
        )
        starts = jnp.stack([start, other_start]).astype(jnp.int32)
        act = jnp.concatenate([starts, live.astype(jnp.int32).reshape(-1)])
        made[causal, size] = (act, jnp.pad(jnp.stack([begin, last]), ((0, 6), (0, 0))))
    return made


def attend(masks, causal, q, kv, kv_oth):
    n, width = q.shape
    pairs = width // (2 * HEAD)
    return pl.pallas_call(
        attend_kernel,
        out_shape=[
            jax.ShapeDtypeStruct((n, width), jnp.bfloat16),
            jax.ShapeDtypeStruct((n // BQ, pairs, 1, 2 * BQ), jnp.float32),
        ],
        in_specs=[SCALAR] + [ONCHIP] * 2 + [ANY] * 2,
        out_specs=[ONCHIP, ONCHIP],
        scratch_shapes=[
            pltpu.VMEM((2 * n, width), jnp.bfloat16),
            pltpu.VMEM((2 * n, width), jnp.bfloat16),
            pltpu.VMEM((pairs, 2 * n // CF, 2 * BQ, CF), jnp.float32),
            pltpu.VMEM((pairs, 2 * BQ, 128), jnp.bfloat16),
            pltpu.VMEM((pairs, 2 * BQ, 128), jnp.float32),
            pltpu.VMEM((pairs, 2 * BQ, 128), jnp.float32),
            pltpu.VMEM((pairs, 2 * BQ, 128), jnp.float32),
            pltpu.SemaphoreType.DMA((2,)),
            pltpu.SemaphoreType.DMA((2,)),
        ],
        cost_estimate=LIGHT,
        compiler_params=SMALL,
        name="attend",
    )(*masks[causal, CF], q, kv, kv_oth)


def attend_back(masks, causal, q, kv, kv_oth, o, lse, grad):
    n, width = q.shape
    pairs = width // (2 * HEAD)
    chunks = 2 * n // CK
    return pl.pallas_call(
        attend_back_kernel,
        out_shape=[
            jax.ShapeDtypeStruct((n, width), jnp.bfloat16),
            jax.ShapeDtypeStruct((2, n, width), jnp.float32),
            jax.ShapeDtypeStruct((2, n, width), jnp.float32),
        ],
        in_specs=[SCALAR] + [ONCHIP] * 2 + [ANY] * 2 + [ONCHIP] * 3,
        out_specs=[ONCHIP] * 3,
        scratch_shapes=[
            pltpu.VMEM((2 * n, width), jnp.bfloat16),
            pltpu.VMEM((2 * n, width), jnp.bfloat16),
            pltpu.VMEM((chunks, pairs, 128, CK), jnp.bfloat16),
            pltpu.VMEM((pairs, 2 * BQ, 128), jnp.bfloat16),
            pltpu.VMEM((pairs, 2 * BQ, 128), jnp.bfloat16),
            pltpu.VMEM((pairs, 1, 2 * BQ), jnp.float32),
            pltpu.VMEM((pairs, 128, 2 * BQ), jnp.float32),
            pltpu.SemaphoreType.DMA((2,)),
            pltpu.SemaphoreType.DMA((2,)),
        ],
        cost_estimate=LIGHT,
        compiler_params=SMALL,
        name="attend_back",
    )(*masks[causal, CK], q, kv, kv_oth, o, lse, grad)


def rms(v, gain):
    scale = lax.rsqrt(jnp.mean(v * v, axis=-1, keepdims=True) + NORM_EPS)
    return v * scale * gain


def rms_back(v, gain, grad):
    scale = lax.rsqrt(jnp.mean(v * v, axis=-1, keepdims=True) + NORM_EPS)
    scaled = grad * gain
    lean = jnp.mean(scaled * v, axis=-1, keepdims=True) * (scale * scale * scale)
    return scaled * scale - v * lean, jnp.sum(grad * v * scale, axis=0, keepdims=True)


def project_kernel(x, gain, w, normed, q, kv):
    a = low(rms(x[...], gain[...]))
    normed[...] = a
    q[...] = low(dot32(a, w[0], NN))
    kv[0] = low(dot32(a, w[1], NN))
    kv[1] = low(dot32(a, w[2], NN))


def pair_kernel(memory, w, kv):
    m = memory[...]
    kv[0] = low(dot32(m, w[1], NN))
    kv[1] = low(dot32(m, w[2], NN))


def between_kernel(o, w_out, x, gain, w, y, normed, q):
    state = x[...] + dot32(o[...], w_out[0], NN)
    y[...] = state
    c = low(rms(state, gain[...]))
    normed[...] = c
    q[...] = low(dot32(c, w[0], NN))


def feed_kernel(o, w_out, x, gain, w_up, w_down, y, normed, hidden, z):
    state = x[...] + dot32(o[...], w_out[0], NN)
    y[...] = state
    f = low(rms(state, gain[...]))
    normed[...] = f
    for i in range(w_up.shape[0]):
        r = low(jnp.maximum(dot32(f, w_up[i], NN), 0.0))
        hidden[i] = r
        state = state + dot32(r, w_down[i], NN)
    z[...] = state


def out_back(g, o, w_out, grad_o, grad_out):
    grad_o[...] = low(dot32(g, w_out[0], NT))
    grad_out[0] = low(dot32(o[...], g, TN))


def feed_back_kernel(
    grad, y, normed, hidden, gain, w_up, w_down, o, w_out,
    grad_up, grad_down, grad_y, grad_gain, grad_o, grad_out,
):
    g = low(grad[...])
    f = normed[...]
    back = jnp.zeros(grad.shape, jnp.float32)
    for i in range(w_up.shape[0]):
        r = hidden[i]
        grad_down[i] = low(dot32(r, g, TN))
        h = low(jnp.where(r > 0, dot32(g, w_down[i], NT), 0.0))
        grad_up[i] = low(dot32(f, h, TN))
        back = back + dot32(h, w_up[i], NT)
    more, grad_gain[...] = rms_back(y[...], gain[...], back)
    total = grad[...] + more
    grad_y[...] = total
    out_back(low(total), o, w_out, grad_o, grad_out)


def between_back_kernel(
    grad_q, normed, y, gain, w, grad, o, w_out,
    grad_w, grad_x, grad_gain, grad_o, grad_out,
):
    g = grad_q[...]
    grad_w[0] = low(dot32(normed[...], g, TN))
    more, grad_gain[...] = rms_back(y[...], gain[...], dot32(g, w[0], NT))
    total = grad[...] + more
    grad_x[...] = total
    out_back(low(total), o, w_out, grad_o, grad_out)


def memory_back_kernel(own, other, memory, w, grad_w, grad_memory):
    m = memory[...]
    total = None
    for i in range(2):
        g = low(own[i] + other[i])
        grad_w[i] = low(dot32(m, g, TN))
        part = dot32(g, w[i + 1], NT)
        total = part if total is None else total + part
    grad_memory[...] = total


def project_back_kernel(
    grad_q, own, other, normed, x, gain, w, grad,
    grad_w, grad_x, grad_gain,
):
    a = normed[...]
    back = None
    for i in range(3):
        g = grad_q[...] if i == 0 else low(own[i - 1] + other[i - 1])
        grad_w[i] = low(dot32(a, g, TN))
        part = dot32(g, w[i], NT)
        back = part if back is None else back + part
    more, grad_gain[...] = rms_back(x[...], gain[...], back)
    grad_x[...] = grad[...] + more


def table_back_kernel(ids, token_grads, grad_logits, exits, grad):
    first = pl.program_id(0) * grad.shape[0]
    spot = first + lax.broadcasted_iota(jnp.int32, (grad.shape[0], ids.shape[1]), 0)
    looked = jnp.where(spot == ids[0:1, :], 1.0, 0.0).astype(HALF)
    total = dot32(looked, token_grads[...], NN) + dot32(grad_logits[...], exits[...], TN)
    grad[...] = low(total)


def table_back(ids, token_grads, grad_logits, exits):
    rows, vocabulary = grad_logits.shape
    count, width = token_grads.shape
    ids = jnp.broadcast_to(ids[None], (8, count))
    return pl.pallas_call(
        table_back_kernel,
        grid=(vocabulary // COL,),
        out_shape=jax.ShapeDtypeStruct((vocabulary, width), HALF),
        in_specs=[
            pl.BlockSpec((8, count), lambda i: (0, 0)),
            pl.BlockSpec((count, width), lambda i: (0, 0)),
            pl.BlockSpec((rows, COL), lambda i: (0, i)),
            pl.BlockSpec((rows, width), lambda i: (0, 0)),
        ],
        out_specs=pl.BlockSpec((COL, width), lambda i: (i, 0)),
        cost_estimate=LIGHT,
        compiler_params=pltpu.CompilerParams(vmem_limit_bytes=24 << 20),
        name="table_back",
    )(ids, token_grads, grad_logits, exits)


def on_chip(kernel, name, outs, *args):
    return pl.pallas_call(
        kernel,
        out_shape=[jax.ShapeDtypeStruct(shape, kind) for shape, kind in outs],
        in_specs=[ONCHIP] * len(args),
        out_specs=[ONCHIP] * len(outs),
        cost_estimate=LIGHT,
        compiler_params=SMALL,
        name=name,
    )(*args)


def shaped(lead, like, kind):
    return (lead + like.shape, kind)


def attend_forward(masks, causal, q, kv):
    other = flip(kv, "c")
    o, lse = attend(masks, causal, q, kv, other)
    return o, (q, kv, other, o, lse)


def attend_backward(saved, masks, causal, grad):
    grad_q, own, other = attend_back(masks, causal, *saved, grad)
    return grad_q, own, flip(other, "c")


def project(x, gain, w):
    return on_chip(
        project_kernel,
        "project",
        [shaped((), x, HALF), shaped((), x, HALF), shaped((2,), x, HALF)],
        x, gain[None], w,
    )


def memory_pair(memory, w):
    return on_chip(pair_kernel, "memory_pair", [shaped((2,), memory, HALF)], memory, w)[0]


def between(o, w_out, x, gain, w):
    return on_chip(
        between_kernel,
        "between",
        [shaped((), x, FULL), shaped((), x, HALF), shaped((), x, HALF)],
        o, w_out, x, gain[None], w,
    )


def feed(o, w_out, x, gain, w_up, w_down):
    return on_chip(
        feed_kernel,
        "feed",
        [
            shaped((), x, FULL),
            shaped((), x, HALF),
            shaped((w_up.shape[0],), x, HALF),
            shaped((), x, FULL),
        ],
        o, w_out, x, gain[None], w_up, w_down,
    )


def feed_back(grad, kept, gain, w_up, w_down, o, w_out):
    y, normed, hidden = kept
    return on_chip(
        feed_back_kernel,
        "feed_back",
        [
            (w_up.shape, HALF),
            (w_down.shape, HALF),
            shaped((), y, FULL),
            ((1, y.shape[1]), FULL),
            shaped((), y, HALF),
            (w_out.shape, HALF),
        ],
        grad, y, normed, hidden, gain[None], w_up, w_down, o, w_out,
    )


def between_back(grad_q, normed, y, gain, w, grad, o, w_out):
    return on_chip(
        between_back_kernel,
        "between_back",
        [
            (w_out.shape, HALF),
            shaped((), y, FULL),
            ((1, y.shape[1]), FULL),
            shaped((), y, HALF),
            (w_out.shape, HALF),
        ],
        grad_q, normed, y, gain[None], w, grad, o, w_out,
    )


def memory_back(own, other, memory, w):
    return on_chip(
        memory_back_kernel,
        "memory_back",
        [((2,) + w.shape[1:], HALF), shaped((), memory, FULL)],
        own, other, memory, w,
    )


def project_back(grad_q, own, other, normed, x, gain, w, grad):
    return on_chip(
        project_back_kernel,
        "project_back",
        [(w.shape, HALF), shaped((), x, FULL), ((1, x.shape[1]), FULL)],
        grad_q, own, other, normed, x, gain[None], w, grad,
    )


def shards(
    tokens,
    source,
    segments,
    loss_rows,
    targets,
    exit_depth,
    qkv_weight,
    out_weight,
    up_weight,
    down_weight,
    norm_gains,
    embed_table,
    qkv_first,
    out_first,
    up_first,
    down_first,
    gains_first,
    table_first,
    qkv_second,
    out_second,
    up_second,
    down_second,
    gains_second,
    table_second,
):
    sy, sx = lax.axis_index("sy"), lax.axis_index("sx")
    z, c = lax.axis_index("z"), lax.axis_index("c")
    s = sy * 2 + sx
    me = jnp.stack([c, z, s]).astype(jnp.int32)
    owners = lax.axis_size("z") * 2
    tok_dev = tokens.shape[2]
    loss_dev = targets.shape[2]
    voc_dev, width = embed_table.shape
    gain_count, gain_dev = norm_gains.shape
    vocabulary = voc_dev * owners
    root_width = math.sqrt(width)
    half_row = 2 * tok_dev
    unit = qkv_weight.shape[1] // 4
    fast = lax.axis_size("z") == 4 and unit % 16 == 0

    shard_of = {
        "table": embed_table[None],
        "qkv": qkv_weight,
        "out": out_weight,
        "up": up_weight,
        "down": down_weight,
    }
    shard_shapes = {name: array.shape[1:] for name, array in shard_of.items()}
    weights = {}

    def layout(entries):
        kinds = [kind for _, _, kind in entries]
        return kinds, block_counts(entries, shard_shapes, unit)

    def packed(entries):
        return jnp.concatenate(
            [owned_blocks(low(shard_of[name][i]), kind, unit) for name, i, kind in entries]
        )

    def gather(entries):
        mover = Mover()
        mover.stages = gather_stages(mover, me, packed(entries), *layout(entries), unit, owners)
        return mover

    def settle(entries, outs):
        for (name, i, kind), out in zip(entries, outs):
            weights[name, i] = out.reshape(-1, COL, COL) if kind == "blk" else out

    def gather_plainly(entries):
        everything = lax.all_gather(packed(entries), LINE)
        outs = []
        first = 0
        for kind, count in zip(*layout(entries)):
            piece = everything[:, first : first + count]
            first += count
            if kind == "row":
                outs.append(piece.transpose(1, 0, 2, 3).reshape(count, -1, COL))
            else:
                outs.append(piece.reshape(owners, count, 4, unit, COL).transpose(0, 2, 1, 3, 4))
        settle(entries, outs)

    def pieces(entries):
        arrays, kinds, counts = [], [], []
        for (name, i, kind), count in zip(entries, layout(entries)[1]):
            held = grads[name, i]
            for array in held if isinstance(held, tuple) else (held,):
                blocks = array.shape[0] if isinstance(held, tuple) else count
                arrays.append(array.reshape(natural_shape(kind, blocks, unit, owners)))
                kinds.append(kind)
                counts.append(blocks)
        return arrays, kinds, counts

    def reduce(entries, stages=reduce_stages):
        arrays, kinds, counts = pieces(entries)
        mover = Mover()
        mover.stages = stages(mover, me, arrays, kinds, counts, unit)
        return mover

    def take(entries, parts):
        first = 0
        for (name, i, kind), count in zip(entries, layout(entries)[1]):
            reduced[name, i] = owned_natural(parts[:, first : first + count], kind)
            first += count

    def reduce_plainly(entries):
        parts = []
        for array, kind, count in zip(*pieces(entries)):
            if kind == "row":
                array = array.reshape(count, owners, 4, unit, COL).transpose(1, 2, 0, 3, 4)
            parts.append(wide(array))
        total = jnp.concatenate(parts, axis=2)
        total = lax.psum_scatter(total, LINE, scatter_dimension=0, tiled=True)
        total = lax.psum(total, PLANE)[0]
        take(entries, total)
        return jnp.sum(total * total) / 4.0

    if fast:
        first = gather(GATHERED[0])
        ints = [tokens, source, segments, loss_rows, targets, exit_depth]
        ints, shard_of = step((ints, shard_of), first)
        tokens, source, segments, loss_rows, targets, exit_depth = ints
        second = gather(GATHERED[1])

        def gather_long(entries):
            return jnp.concatenate(
                [quarter_blocks(shard_of[name][i], kind, unit, s) for name, i, kind in entries]
            )

        third, fourth = gather_long(GATHERED[2]), gather_long(GATHERED[3])
    if not fast:
        for entries in GATHERED:
            gather_plainly(entries)

    numbers = jnp.concatenate(
        [array[:, 0] for array in (tokens, source, segments, loss_rows, targets, exit_depth)],
        axis=1,
    )
    plane = gathered(gathered(numbers, "c"), PLANE)
    depths_seen = plane[..., 3 * tok_dev + 2 * loss_dev :]
    reached = jnp.stack(
        [
            jnp.sum((depths_seen >= layer_id).astype(jnp.float32), axis=(0, 1, 3))
            for layer_id in range(LAYERS)
        ],
        axis=1,
    )
    gains_now = norm_gains
    if fast:
        reached, gains_now = step((reached, gains_now), first)
        (reached, gains_now), third = hold((reached, gains_now), third)
        third = lax.all_gather(third, PLANE + LINE).reshape(4, owners, *third.shape)
        reached, gains_now = step((reached, gains_now), second)
    small = jnp.concatenate([gains_now.reshape(-1), reached.reshape(-1)])
    small = gathered(gathered(small, "c"), "z").reshape(owners, -1)
    reach = jnp.maximum(
        jnp.sum(small[::2, gain_count * gain_dev :], axis=0).reshape(MICRO, LAYERS), 1.0
    )
    reach = lax.dynamic_index_in_dim(reach, sy, 0, False)
    gains_seen = small[:, : gain_count * gain_dev].reshape(owners, gain_count, gain_dev)
    order = jnp.arange(owners)
    rel = ((order // 2) ^ z) * 2 + ((order % 2) ^ c)
    gains_full = gains_seen[rel].transpose(1, 0, 2).reshape(gain_count, width)
    gains_full = wide(low(gains_full))

    row = lax.dynamic_index_in_dim(plane, sx ^ c, 1, False)
    row = in_order(lax.dynamic_index_in_dim(row, sy, 1, False), s)
    mine = lax.dynamic_slice_in_dim(row, 2 * c, 2, 0)
    theirs = lax.dynamic_slice_in_dim(row, 2 * (1 - c), 2, 0)
    target_ids = mine[:, :tok_dev].reshape(-1)
    source_ids = mine[:, tok_dev : 2 * tok_dev].reshape(-1)
    sentence = mine[:, 2 * tok_dev : 3 * tok_dev].reshape(-1)
    other_sentence = theirs[:, 2 * tok_dev : 3 * tok_dev].reshape(-1)
    rest = 3 * tok_dev
    places = (
        mine[:, rest : rest + loss_dev] + (jnp.arange(2, dtype=jnp.int32) * tok_dev)[:, None]
    ).reshape(-1)
    wanted = mine[:, rest + loss_dev : rest + 2 * loss_dev].reshape(-1)
    depth = mine[:, rest + 2 * loss_dev : rest + 3 * loss_dev].reshape(-1)
    masks = attend_masks(sentence, other_sentence, c * half_row, (1 - c) * half_row)

    ids = jnp.concatenate([source_ids, target_ids])
    if fast:
        ids, small = step((ids, small), first)
        ids = step(ids, second, first)
        settle(GATHERED[0], first.result)
    table = weights["table", 0].reshape(vocabulary, width)
    looked_up = table[ids].astype(jnp.float32) * root_width
    xe = looked_up[:half_row]
    x = looked_up[half_row:]
    kept_enc = (xe, *project(xe, gains_full[0], weights["qkv", 0]))
    if fast:
        xe, kept_enc, x = step((xe, kept_enc, x), second)
    o, saved_enc = attend_forward(masks, False, *kept_enc[2:])
    if fast:
        o, fourth = step((o, fourth), second)
        fourth = lax.all_gather(fourth, PLANE + LINE).reshape(4, owners, *fourth.shape)
        settle(GATHERED[1], second.result)
    *kept_enc_feed, xe = feed(
        o, weights["out", 0], xe, gains_full[1], weights["up", 0], weights["down", 0]
    )
    final_gain = gains_full[2 * ENC]
    memory = low(normalize(xe, final_gain))
    kept = []
    states = []
    for layer_id in range(LAYERS):
        base = 2 * ENC + 1 + 4 * layer_id
        slot = ENC + 2 * layer_id
        if fast and layer_id == 0:
            (x, memory), third = hold((x, memory), third)
            settle(GATHERED[2], unpack(third, *layout(GATHERED[2]), unit, owners))
        kept_self = (x, *project(x, gains_full[base], weights["qkv", slot]))
        o, saved_self = attend_forward(masks, True, *kept_self[2:])
        if fast and layer_id == 1:
            o, fourth = hold(o, fourth)
            settle(GATHERED[3], unpack(fourth, *layout(GATHERED[3]), unit, owners))
        cross = weights["qkv", slot + 1]
        pair = memory_pair(memory, cross)
        *kept_cross, q = between(o, weights["out", slot], x, gains_full[base + 1], cross)
        o, saved_cross = attend_forward(masks, False, q, pair)
        feed_at = ENC + layer_id
        *kept_feed, x = feed(
            o,
            weights["out", slot + 1],
            kept_cross[0],
            gains_full[base + 2],
            weights["up", feed_at],
            weights["down", feed_at],
        )
        kept.append((kept_self, saved_self, kept_cross, saved_cross, kept_feed))
        states.append(x)

    pick = (places[:, None] == jnp.arange(half_row)[None, :]).astype(jnp.bfloat16)
    exit_gains = [gains_full[2 * ENC + 4 + 4 * layer_id] for layer_id in range(LAYERS)]
    exits = jnp.concatenate(
        [low(product(pick, low(normalize(states[i], exit_gains[i])))) for i in range(LAYERS)]
    )
    logits = against_rows(exits, table) * LOGIT_SCALE
    wanted_all = jnp.concatenate([wanted] * LAYERS)
    hit = jnp.arange(vocabulary)[None, :] == wanted_all[:, None]
    picked = jnp.sum(jnp.where(hit, logits, 0.0), axis=-1)
    top = jnp.max(logits, axis=-1)
    lse = top + jnp.log(jnp.sum(jnp.exp(logits - top[:, None]), axis=-1))
    shares = jnp.concatenate(
        [(depth >= i).astype(jnp.float32) / reach[i] / MICRO for i in range(LAYERS)]
    )
    loss_part = jnp.sum((lse - picked) * shares)
    grad_logits = low(
        (jnp.exp(logits - lse[:, None]) - hit.astype(jnp.float32))
        * shares[:, None]
        * LOGIT_SCALE
    )
    grad_exits = product(grad_logits, table)

    grads = {}
    gain_parts = [None] * gain_count
    grad_x = None
    grad_memory = None
    for layer_id in reversed(range(LAYERS)):
        slot = ENC + 2 * layer_id
        base = 2 * ENC + 1 + 4 * layer_id
        count = places.shape[0]
        grad_rows = lax.dot_general(
            wide(pick),
            grad_exits[layer_id * count : (layer_id + 1) * count],
            (((0,), (0,)), ((), ())),
            precision=lax.Precision.HIGHEST,
            preferred_element_type=jnp.float32,
        )
        grad_here, gain_parts[base + 3] = norm_back(
            states[layer_id], exit_gains[layer_id], grad_rows
        )
        grad_x = grad_here if grad_x is None else grad_x + grad_here
        kept_self, saved_self, kept_cross, saved_cross, kept_feed = kept[layer_id]
        up, down = ("up", ENC + layer_id), ("down", ENC + layer_id)
        qkv, out = ("qkv", slot + 1), ("out", slot + 1)
        grads[up], grads[down], grad_x, gain_parts[base + 2], grad_o, grads[out] = feed_back(
            grad_x,
            kept_feed,
            gains_full[base + 2],
            weights[up],
            weights[down],
            saved_cross[3],
            weights[out],
        )
        if fast and layer_id == 1:
            feed_mover = reduce(REDUCED[0], long_reduce_stages)
            grad_x, grad_o = step((grad_x, grad_o), feed_mover, feed_mover)
        if fast and layer_id == 0:
            late = reduce(REDUCED[1], long_reduce_stages)
            grad_x, grad_o = step((grad_x, grad_o), feed_mover, late, late)
        grad_q, own, other = attend_backward(saved_cross, masks, False, grad_o)
        grad_pair, more = memory_back(own, other, memory, weights[qkv])
        grad_memory = more if grad_memory is None else grad_memory + more
        out = ("out", slot)
        grad_query, grad_x, gain_parts[base + 1], grad_o, grads[out] = between_back(
            grad_q,
            kept_cross[1],
            kept_cross[0],
            gains_full[base + 1],
            weights[qkv],
            grad_x,
            saved_self[3],
            weights[out],
        )
        grads[qkv] = (grad_query, grad_pair)
        grad_q, own, other = attend_backward(saved_self, masks, True, grad_o)
        qkv = ("qkv", slot)
        grads[qkv], grad_x, gain_parts[base] = project_back(
            grad_q,
            own,
            other,
            kept_self[1],
            kept_self[0],
            gains_full[base],
            weights[qkv],
            grad_x,
        )
    if fast:
        grad_x, grad_memory = step((grad_x, grad_memory), feed_mover)
    grad_enc, gain_parts[2 * ENC] = norm_back(xe, final_gain, grad_memory)
    up, down, qkv, out = ("up", 0), ("down", 0), ("qkv", 0), ("out", 0)
    grads[up], grads[down], grad_enc, gain_parts[1], grad_o, grads[out] = feed_back(
        grad_enc,
        kept_enc_feed,
        gains_full[1],
        weights[up],
        weights[down],
        saved_enc[3],
        weights[out],
    )
    if fast:
        middle = reduce(REDUCED[2], long_reduce_stages)
        grad_enc, grad_o = step((grad_enc, grad_o), middle, late, middle)
    grad_q, own, other = attend_backward(saved_enc, masks, False, grad_o)
    grads[qkv], grad_enc, gain_parts[0] = project_back(
        grad_q, own, other, kept_enc[1], kept_enc[0], gains_full[0], weights[qkv], grad_enc
    )
    token_ids = jnp.concatenate([source_ids, target_ids])
    token_grads = low(jnp.concatenate([grad_enc, grad_x]) * root_width)
    grads["table", 0] = table_back(token_ids, token_grads, grad_logits, exits)
    gain_grad = jnp.concatenate([part.reshape(1, -1) for part in gain_parts])
    small = jnp.concatenate([gain_grad, jnp.full((1, width), loss_part)])

    reduced = {}
    if fast:
        last = reduce(REDUCED[3])
        tiny = Mover()
        tiny.stages = small_stages(tiny, small, z)
        loss_part = step(loss_part, last, tiny)
        loss_part = step(loss_part, last, tiny, middle)
        loss_part = step(loss_part, last, tiny)
        loss_part = step(loss_part, last, tiny)
        movers = (feed_mover, late, middle, last)
        loss_part = step(loss_part, last, tiny)
        gain_grad, loss_total = tiny.result[:-1], tiny.result[-1, 0]
        squares = all_sum(sum(mover.squares for mover in movers))
        squares = step(squares, late, middle, last)
    else:
        small = all_sum(small)
        gain_grad, loss_total = small[:-1], small[-1, 0]
        squares = all_sum(sum(reduce_plainly(entries) for entries in REDUCED))
    squares = squares + jnp.sum(gain_grad * gain_grad)
    grad_norm = jnp.sqrt(squares)
    clip_factor = CLIP_NORM / jnp.maximum(grad_norm, CLIP_NORM)

    names = ("qkv", "out", "up", "down", "table")
    if fast:
        plan = []
        for bucket, entries in enumerate(REDUCED):
            first = 0
            for (name, i, kind), count in zip(entries, layout(entries)[1]):
                plan.append((bucket, first, count, kind, names.index(name), i))
                first += count
        parts = [part for mover in movers for part in mover.result]
        shapes = [shard_of[name].shape for name in names]
        placed = pl.pallas_call(
            functools.partial(settle_kernel, len(parts), tuple(plan), unit),
            out_shape=[jax.ShapeDtypeStruct(shape, jnp.bfloat16) for shape in shapes],
            in_specs=[SCALAR] + [ANY] * len(parts),
            out_specs=[ONCHIP] * len(shapes),
            scratch_shapes=[pltpu.SemaphoreType.DMA((len(shapes),))],
            cost_estimate=LIGHT,
            compiler_params=SMALL,
            name="place_gradients",
        )(me, *parts)
        ready = [wide(array) for array in placed]
    else:
        ready = [
            wide(jnp.stack([reduced[name, i] for i in range(shard_of[name].shape[0])]))
            for name in names
        ]
    gradients = (
        *ready[:4],
        lax.dynamic_slice_in_dim(gain_grad, (2 * z + c) * gain_dev, gain_dev, 1),
        ready[4][0],
    )
    masters = (qkv_weight, out_weight, up_weight, down_weight, norm_gains, embed_table)
    firsts = (qkv_first, out_first, up_first, down_first, gains_first, table_first)
    seconds = (qkv_second, out_second, up_second, down_second, gains_second, table_second)
    results = [
        adam_update(masters[i], firsts[i], seconds[i], gradients[i] * clip_factor) for i in range(6)
    ]
    gains_grad = gradients[4] * clip_factor
    return (
        loss_total,
        grad_norm,
        results[0][0],
        results[1][0],
        results[2][0],
        results[3][0],
        gains_grad,
        results[5][0],
        results[0][1],
        results[1][1],
        results[2][1],
        results[3][1],
        results[4][1],
        results[5][1],
        results[0][2],
        results[1][2],
        results[2][2],
        results[3][2],
        results[4][2],
        results[5][2],
    )


def solution(mesh):
    seq, vocab = mesh.devices.shape
    fine = Mesh(mesh.devices.reshape(2, seq // 2, vocab // 2, 2), ("sy", "sx", "z", "c"))
    ints = P(None, LINE, PLANE)
    block = P(None, LINE, None)
    gains = P(None, LINE)
    rows = P(LINE, None)
    arrays = (block, block, block, block, gains, rows)
    return jax.shard_map(
        shards,
        mesh=fine,
        in_specs=(ints,) * 6 + arrays * 3,
        out_specs=(P(), P(), block, block, block, block, gains, rows) + arrays * 2,
        check_vma=False,
    )
```
